32 devices in a mesh: tensor: 4 (over z), dp: 4 (over y, core), ctx: 2 (over x).
Axes of the slice: x: 2, y: 2, z: 4, core: 2. Of those that a mesh axis runs over, the one named last changes fastest.
Arguments:
- block_input: bfloat16 [4, 2, 1024, 768], P('dp', 'ctx', 'tensor'), may hold values from -6 to 6
- seq_lengths: int32 [4, 16], P('dp'), may hold values from 0 to 2048, as said below
- project_weight: bfloat16 [2, 768, 2304], P(None, ('dp', 'ctx'), 'tensor'), may hold values from -0.21875 to 0.21875
- project_bias: bfloat16 [2, 2304], P(None, ('tensor', 'dp', 'ctx')), may hold values from -3 to 3
- dense_weight: bfloat16 [2, 768, 768], P(None, ('tensor', 'dp', 'ctx')), may hold values from -0.75 to 0.75
- up_weight: bfloat16 [2, 768, 3072], P(None, ('dp', 'ctx'), 'tensor'), may hold values from -0.21875 to 0.21875
- up_bias: bfloat16 [2, 3072], P(None, ('tensor', 'dp', 'ctx')), may hold values from -3 to 3
- down_weight: bfloat16 [2, 3072, 768], P(None, ('tensor', 'dp', 'ctx')), may hold values from -0.109375 to 0.109375
- norm_gains: bfloat16 [2, 768, 2], replicated, may hold values from 0.5 to 1.5
- shift_vectors: bfloat16 [2, 768, 4], replicated, may hold values from -2 to 2
- cotangent: float32 [4, 2, 1024, 768], P('dp', 'ctx', 'tensor'), may hold values from -6 to 6
Outputs:
- block_output: float32 [4, 2, 1024, 768], P('dp', 'ctx', 'tensor')
- input_grad: float32 [4, 2, 1024, 768], P('dp', 'ctx', 'tensor')
- project_weight_grad: float32 [2, 768, 2304], P(None, ('dp', 'ctx'), 'tensor')
- project_bias_grad: float32 [2, 2304], P(None, ('tensor', 'dp', 'ctx'))
- dense_weight_grad: float32 [2, 768, 768], P(None, ('tensor', 'dp', 'ctx'))
- up_weight_grad: float32 [2, 768, 3072], P(None, ('dp', 'ctx'), 'tensor')
- up_bias_grad: float32 [2, 3072], P(None, ('tensor', 'dp', 'ctx'))
- down_weight_grad: float32 [2, 3072, 768], P(None, ('tensor', 'dp', 'ctx'))
- norm_gains_grad: float32 [2, 768, 2], P(None, ('tensor', 'dp', 'ctx'))
- shift_vectors_grad: float32 [2, 768, 4], P(None, ('tensor', 'dp', 'ctx'))
The draws below stay inside these ranges and needn't reach their ends.
Inputs may be any that keep to these rules, and one draw needn't show every extreme that they name: `seq_lengths`: each row's entries sum to 2048; its nonzero entries come first, and each of them but the last is 128 or more; a row's slots hold its sequences one after another in this order.
All inputs are finite; a program needn't handle non-finite values.
Results may differ from the reference program's by a relative error of at most 0.018.
Values may be sent and summed in bfloat16 or wider, within the bound.
No kernel may reach another device: no remote copies, remote signals or barrier semaphores. Data moves between devices by JAX's collectives and lax.ppermute only.
A program may use at most 128 MiB of HBM per device.

```python
import jax
import jax.numpy as jnp
from jax import lax

D = 768
HEADS = 12
HEAD_DIM = 64
FF = 3072
ROTARY = 16
LAYERS = 2
ROW_LEN = 2048
SHORTEST = 128
ROWS_DEV = 1
ROWS = 4
STRETCH = 1024
SEQ_SLOTS = 16
N_CTX = 2


def draw_seq_lengths(key, part):
    key_pick, key_first, key_second, key_extra, key_cut = jax.random.split(key, 5)
    levels = (ROW_LEN // SHORTEST).bit_length() - 1
    groups = ROWS // ROWS_DEV
    shape = (ROWS, SEQ_SLOTS)
    power = jnp.minimum(jax.random.randint(key_first, shape, 0, levels + 1), jax.random.randint(key_second, shape, 0, levels + 1))
    base = SHORTEST * jnp.left_shift(jnp.ones_like(power), power)
    extra = jax.random.randint(key_extra, shape, 0, 1 << 20) % base
    wanted = jnp.minimum(base + extra, ROW_LEN)
    pick = jax.random.randint(key_pick, (groups,), 0, ROWS_DEV)
    row_ids = jnp.arange(ROWS, dtype=jnp.int32)
    chosen = row_ids % ROWS_DEV == jnp.repeat(pick, ROWS_DEV)
    cut = jax.random.randint(key_cut, (ROWS,), 0, STRETCH) * (row_ids >= ROWS_DEV).astype(jnp.int32)
    span = ROW_LEN - cut
    leading = jnp.concatenate([span[:, None], wanted[:, :-1]], axis=1)
    wanted = jnp.where(chosen[:, None], leading, wanted)
    ends = jnp.cumsum(wanted, axis=1)
    starts = ends - wanted
    return jnp.clip(ROW_LEN - starts, 0, wanted).astype(jnp.int32)


def steps_of(key, extent, cuts, low, top_value):
    def one(dim, shards_of):
        draws = jax.random.uniform(jax.random.fold_in(jax.random.fold_in(key, 6), dim), (shards_of,), jnp.float32, low / len(cuts), top_value / len(cuts))
        return jnp.repeat(jnp.exp(draws), extent[dim] // shards_of).reshape((-1,) + (1,) * (len(extent) - dim - 1))

    level = one(*cuts[0])
    for cut in cuts[1:]:
        level = level * one(*cut)
    return level


def normal_values(rng, dims, scale, most, cuts=(), held_as=jnp.bfloat16):
    drawn = jax.random.normal(rng, dims, jnp.float32) * scale
    if len(cuts) > 0:
        drawn = steps_of(rng, dims, cuts, -0.22, 0.18) * drawn
    return jnp.clip(drawn, min=-most, max=most).astype(held_as)


def setup_inputs(seed: int = 0) -> dict:
    key_of = jax.random.split(jax.random.key(seed), 12)
    block_input = normal_values(key_of[0], (ROWS, N_CTX, STRETCH, D), 1.0, 6.0, ((0, 4), (1, 2), (2, 4)))
    seq_lengths = draw_seq_lengths(jax.random.fold_in(key_of[11], 71), 0)
    project_weight = normal_values(key_of[2], (LAYERS, D, 3 * D), D ** -0.5, 0.21875, ((1, 8), (2, 4)))
    project_bias = normal_values(key_of[3], (LAYERS, 3 * D), 0.5, 3.0, ((1, 32),))
    dense_weight = normal_values(key_of[4], (LAYERS, D, D), HEAD_DIM ** -0.5, 0.75, ((1, 32),))
    up_weight = normal_values(key_of[5], (LAYERS, D, FF), D ** -0.5, 0.21875, ((1, 8), (2, 4)))
    up_bias = normal_values(key_of[6], (LAYERS, FF), 0.5, 3.0, ((1, 32),))
    down_weight = normal_values(key_of[7], (LAYERS, FF, D), FF ** -0.5, 0.109375, ((1, 32),))
    norm_gains = jnp.clip(1.0 + 0.1 * jax.random.normal(key_of[8], (LAYERS, D, 2), jnp.float32), 0.5, 1.5).astype(jnp.bfloat16)
    shift_vectors = normal_values(key_of[9], (LAYERS, D, 4), 0.3, 2.0)
    cotangent = normal_values(key_of[10], (ROWS, N_CTX, STRETCH, D), 1.0, 6.0, ((0, 4), (1, 2), (2, 4)), jnp.float32)
    return {"block_input": block_input, "seq_lengths": seq_lengths, "project_weight": project_weight, "project_bias": project_bias, "dense_weight": dense_weight, "up_weight": up_weight, "up_bias": up_bias, "down_weight": down_weight, "norm_gains": norm_gains, "shift_vectors": shift_vectors, "cotangent": cotangent}


@jax.custom_vjp
def low(v):
    return lax.optimization_barrier(v.astype(jnp.bfloat16)).astype(jnp.float32)

@jax.custom_vjp
def low_back(v):
    return v

def low_keep(v):
    return (low(v), None)

def low_pass(kept, grad):
    return (grad,)

def back_keep(v):
    return (v, None)

def back_low(kept, grad):
    return (low(grad),)
low.defvjp(low_keep, low_pass)
low_back.defvjp(back_keep, back_low)
EPSILON = 1e-05
MASKED = -1e+30
PRECISE = lax.Precision.HIGHEST

def matmul(left, right):
    return jnp.dot(left, right, preferred_element_type=jnp.float32, precision=PRECISE)

def slot_tables(seq_lengths):
    ends = jnp.cumsum(seq_lengths, axis=1).astype(jnp.int32)
    slots = jnp.arange(ROW_LEN, dtype=jnp.int32)
    passed = (ends[:, None, :] <= slots[None, :, None]).astype(jnp.int32)
    segment = lax.optimization_barrier(jnp.sum(passed, axis=2)).astype(jnp.int32)
    begin = lax.optimization_barrier(jnp.sum(passed * seq_lengths[:, None, :], axis=2)).astype(jnp.int32)
    return (segment, slots[None, :] - begin)

def rotary_tables(position):
    frequency = 1.0 / 10000.0 ** (jnp.arange(0, ROTARY, 2, dtype=jnp.float32) / ROTARY)
    angle = position.astype(jnp.float32)[..., None] * frequency
    angle = jnp.concatenate([angle, angle], axis=-1)[..., None, :]
    return (jnp.cos(angle), jnp.sin(angle))

def rotate(vectors, cosine, sine):
    head = vectors[..., :ROTARY]
    half = ROTARY // 2
    turned = jnp.concatenate([-head[..., half:], head[..., :half]], axis=-1)
    return jnp.concatenate([head * cosine + turned * sine, vectors[..., ROTARY:]], axis=-1)

def norm_apply(values, gain, shift):
    centre = values - lax.optimization_barrier(jnp.mean(values, axis=-1, keepdims=True))
    spread = lax.optimization_barrier(jnp.mean(centre * centre, axis=-1, keepdims=True))
    return centre * lax.rsqrt(spread + EPSILON) * gain + shift

def attend_one(query, keys, values, segment):
    slots = jnp.arange(ROW_LEN, dtype=jnp.int32)
    allowed = (segment[:, None] == segment[None, :]) & (slots[None, :] <= slots[:, None])
    scores = low_back(matmul(query, keys.T) * HEAD_DIM ** (-0.5))
    probability = jax.nn.softmax(jnp.where(allowed, scores, MASKED), axis=-1)
    return matmul(low(probability), values)

def heads_first(array):
    rows = array.shape[0]
    return jnp.transpose(array, (0, 2, 1, 3)).reshape(rows * HEADS, ROW_LEN, HEAD_DIM)

def layer_forward(residual, segment, cosine, sine, mix_w, mix_b, dense_w, up_w, up_b, down_w, gains, shifts):
    rows = residual.shape[0]
    rounded = low(residual)
    first = low(norm_apply(rounded, gains[:, 0], shifts[:, 0])).reshape(-1, D)
    second = low(norm_apply(rounded, gains[:, 1], shifts[:, 1])).reshape(-1, D)
    projected = low_back(matmul(first, mix_w) + mix_b).reshape(rows, ROW_LEN, HEADS, 3, HEAD_DIM)
    query = low(rotate(projected[:, :, :, 0], cosine, sine))
    keys = low(rotate(projected[:, :, :, 1], cosine, sine))
    values = low(projected[:, :, :, 2])
    segment_heads = jnp.repeat(segment, HEADS, axis=0)
    attend_saved = jax.checkpoint(attend_one)

    def one_item(item):
        return attend_saved(item[0], item[1], item[2], item[3])
    mixed = lax.map(one_item, (heads_first(query), heads_first(keys), heads_first(values), segment_heads))
    mixed = jnp.transpose(mixed.reshape(rows, HEADS, ROW_LEN, HEAD_DIM), (0, 2, 1, 3)).reshape(-1, D)
    mixed = low(low_back(mixed))
    hidden = low_back(matmul(second, up_w) + up_b)
    active = low(jax.nn.gelu(hidden, approximate=False))
    branch = low_back(matmul(mixed, dense_w) + matmul(active, down_w)).reshape(rows, ROW_LEN, D)
    return residual + branch + shifts[:, 2] + shifts[:, 3]

def reference(block_input, seq_lengths, project_weight, project_bias, dense_weight, up_weight, up_bias, down_weight, norm_gains, shift_vectors, cotangent):
    segment, position = slot_tables(seq_lengths)
    cosine, sine = rotary_tables(position)
    weights = tuple((array.astype(jnp.float32) for array in (project_weight, project_bias, dense_weight, up_weight, up_bias, down_weight, norm_gains, shift_vectors)))

    def forward(residual, mix_all, mix_bias, dense_all, up_all, up_bias_all, down_all, gains_all, shifts_all):
        for layer in range(LAYERS):
            residual = layer_forward(residual, segment, cosine, sine, mix_all[layer], mix_bias[layer], dense_all[layer], up_all[layer], up_bias_all[layer], down_all[layer], gains_all[layer], shifts_all[layer])
        return residual
    start = block_input.astype(jnp.float32).reshape(ROWS, ROW_LEN, D)
    output, pullback = jax.vjp(forward, start, *weights)
    grads = pullback(cotangent.astype(jnp.float32).reshape(ROWS, ROW_LEN, D))
    shape = (ROWS, N_CTX, STRETCH, D)
    return (output.reshape(shape), grads[0].reshape(shape), grads[1], grads[2], grads[3], grads[4], grads[5], grads[6], grads[7], grads[8])
```

```python
from functools import partial

import jax
import jax.numpy as jnp
from jax import lax
from jax.experimental import pallas as pl
from jax.experimental.pallas import tpu as pltpu
from jax.sharding import PartitionSpec as P

HEAD_DIM = 64
ROTARY = 16
LAYERS = 2
EPSILON = 1e-05
MASKED = -1e30
LANES = 128
SCALE = HEAD_DIM ** (-0.5)
FAR = 1 << 24
BF = jnp.bfloat16
F32 = jnp.float32
NT = (((1,), (1,)), ((), ()))


def dot(a, b):
    return jnp.dot(a, b, preferred_element_type=F32)


def dot_nt(a, b):
    return lax.dot_general(a, b, NT, preferred_element_type=F32)


def params(mib=56):
    return pltpu.CompilerParams(vmem_limit_bytes=mib << 20)


def z_gather(own):
    n = lax.axis_size("tensor")
    return [own] + [
        lax.ppermute(own, "tensor", [(s, (s - c) % n) for s in range(n)]) for c in range(1, n)
    ]


def z_scatter(parts):
    n = lax.axis_size("tensor")
    total = parts[0].astype(F32)
    for c in range(1, n):
        got = lax.ppermute(parts[c].astype(BF), "tensor", [(s, (s + c) % n) for s in range(n)])
        total = total + got.astype(F32)
    return total


def bits_of(axis):
    return lax.axis_size(axis).bit_length() - 1


def scatter_weights(value, first_y, wire=BF):
    nd, nc = lax.axis_size("dp"), lax.axis_size("ctx")
    kd, kc = bits_of("dp"), bits_of("ctx")
    if nd != 1 << kd or nc != 1 << kc:
        flat = value.astype(wire)
        return lax.psum_scatter(flat, ("dp", "ctx"), scatter_dimension=0, tiled=True)[0].astype(F32)
    labels = [("dp", b) for b in reversed(range(kd))] + [("ctx", b) for b in reversed(range(kc))]
    core = [("dp", 0)] if kd else []
    y_steps = [("dp", b) for b in range(1, kd)]
    x_steps = [("ctx", b) for b in range(kc)]
    order = core + (y_steps + x_steps if first_y else x_steps + y_steps)
    rest = value.shape[1:]
    value = value.reshape((2,) * (kd + kc) + rest)
    for axis, bit in order:
        dim = labels.index((axis, bit))
        mine = (lax.axis_index(axis) >> bit) & 1
        send = lax.dynamic_index_in_dim(value, 1 - mine, dim, keepdims=False).astype(wire)
        keep = lax.dynamic_index_in_dim(value, mine, dim, keepdims=False)
        size = lax.axis_size(axis)
        got = lax.ppermute(send, axis, [(s, s ^ (1 << bit)) for s in range(size)])
        value = keep + got.astype(F32)
        labels.pop(dim)
    return value


def rotated(tile, cosine, sine_a, sine_b):
    return tile * cosine + pltpu.roll(tile, LANES - 8, 1) * sine_a + pltpu.roll(tile, 8, 1) * sine_b


def unrotated(tile, cosine, sine_a, sine_b):
    return tile * cosine - pltpu.roll(tile, LANES - 8, 1) * sine_a - pltpu.roll(tile, 8, 1) * sine_b


def unit_of(x):
    values = x.astype(F32)
    centre = values - jnp.mean(values, axis=-1, keepdims=True)
    inverse = lax.rsqrt(jnp.mean(centre * centre, axis=-1, keepdims=True) + EPSILON)
    return centre * inverse


def entry_kernel(
    heads, x_ref, up_ref, mix_ref, bias_ref, vec_ref, cos_ref, sa_ref, sb_ref,
    first_ref, second_ref, q_ref, kv_ref, active_ref, slope_ref,
):
    width = x_ref.shape[-1]
    unit = unit_of(x_ref[0])
    first = (unit * vec_ref[0:1] + vec_ref[2:3]).astype(BF)
    second = (unit * vec_ref[1:2] + vec_ref[3:4]).astype(BF)
    first_ref[0] = first
    second_ref[0] = second
    mixw = mix_ref[...].reshape(width, -1)
    proj = dot(first, mixw) + bias_ref[1:2, : mixw.shape[1]]
    cosine, sine_a, sine_b = cos_ref[0], sa_ref[0], sb_ref[0]
    for h in range(heads):
        cols = slice(h * LANES, (h + 1) * LANES)
        kv_ref[0, :, cols] = rotated(proj[:, cols], cosine, sine_a, sine_b).astype(BF)
        qcols = slice((heads + h) * LANES, (heads + h + 1) * LANES)
        q_ref[0, :, cols] = (rotated(proj[:, qcols], cosine, sine_a, sine_b) * SCALE).astype(BF)
    upw = up_ref[...].reshape(width, -1)
    hidden = dot(second, upw) + bias_ref[0:1, : upw.shape[1]]
    half = 0.5 * (1.0 + lax.erf(hidden * (0.5**0.5)))
    active_ref[0] = (hidden * half).astype(BF)
    bell = jnp.exp(hidden * hidden * -0.5) * 0.3989422804014327
    slope_ref[0] = (half + hidden * bell).astype(BF)


def entry(xs, gathered, k, bias, vec, tables, heads):
    n, tokens, width = xs.shape
    shards = gathered.shape[0]
    ff = gathered.shape[2]
    wide = heads * LANES
    token = lambda w: pl.BlockSpec((1, tokens, w), lambda c: (c, 0, 0))
    whole = lambda a: pl.BlockSpec(a.shape, lambda c: (0,) * a.ndim)
    weight = lambda j: pl.BlockSpec((shards, k, ff), lambda c: (0, j, 0))
    out = lambda w: jax.ShapeDtypeStruct((n, tokens, w), BF)
    return pl.pallas_call(
        partial(entry_kernel, heads),
        grid=(n,),
        in_specs=[token(width), weight(0), weight(2), whole(bias), whole(vec)]
        + [token(LANES)] * 3,
        out_specs=[token(width), token(width), token(wide), token(wide), token(ff), token(ff)],
        out_shape=[out(width), out(width), out(wide), out(wide), out(ff), out(ff)],
        compiler_params=params(),
        name="entry",
    )(xs, gathered, gathered, bias, vec, *tables)


def load_pairs(kv_refs, kv_s):
    n = kv_refs[0].shape[0]
    for e, ref in enumerate(kv_refs):
        for c in range(n):
            kv_s[e * n + c] = ref[c, 0]


def allowed_pairs(base_ref, begin_ref, kb, c, n, blocks, shape):
    key_slot = base_ref[n + kb] + lax.broadcasted_iota(jnp.int32, shape, 0)
    query_slot = base_ref[c] + lax.broadcasted_iota(jnp.int32, shape, 1)
    return (key_slot >= begin_ref[0, c]) & (key_slot <= query_slot)


def attend_kernel(
    heads, extras, need_ref, base_ref, begin_ref, q_ref, *refs
):
    kv_refs = refs[: 1 + extras]
    mixed_ref, ot_ref, lse_ref, kv_s, vt_s, top_s, total_s, acc_s = refs[1 + extras :]
    n, _, count, _ = q_ref.shape
    blocks = n * (1 + extras)
    row = pl.program_id(0)
    load_pairs(kv_refs, kv_s)

    def turn(kb, _):
        for h in range(heads):
            tile = kv_s[kb, :, h * LANES : (h + 1) * LANES].astype(F32)
            vt_s[kb, h] = tile.T[HEAD_DIM:].astype(BF)
        return 0

    lax.fori_loop(0, blocks, turn, 0)

    def per_query(c, _):
        top_s[...] = jnp.full(top_s.shape, MASKED, F32)
        total_s[...] = jnp.zeros(total_s.shape, F32)
        acc_s[...] = jnp.zeros(acc_s.shape, F32)

        def per_key(kb, _):
            @pl.when(need_ref[row, c * blocks + kb] > 0)
            def _():
                allowed = allowed_pairs(
                    base_ref, begin_ref, kb, c, n, blocks, (count, count)
                )
                for h in range(heads):
                    cols = slice(h * LANES, (h + 1) * LANES)
                    scores = dot_nt(kv_s[kb, :, cols], q_ref[c, 0, :, cols])
                    scores = jnp.where(allowed, scores, MASKED)
                    old = top_s[h]
                    new = jnp.maximum(old, jnp.max(scores, axis=0, keepdims=True))
                    fade = jnp.exp(old - new)
                    weights = jnp.exp(scores - new)
                    top_s[h] = new
                    total_s[h] = total_s[h] * fade + jnp.sum(weights, axis=0, keepdims=True)
                    acc_s[h] = acc_s[h] * fade + dot(vt_s[kb, h], weights.astype(BF))

            return 0

        lax.fori_loop(0, blocks, per_key, 0)
        outs = []
        for h in range(heads):
            total = total_s[h]
            outs.append(acc_s[h] / total)
            lse_ref[0, c, h : h + 1] = top_s[h] + jnp.log(total)
        whole = jnp.concatenate(outs, axis=0)
        ot_ref[0, c] = whole
        mixed_ref[c, 0] = whole.T.astype(BF)
        return 0

    lax.fori_loop(0, n, per_query, 0)


def attention_specs(q, extras):
    n, rows, count, wide = q.shape
    smem = pl.BlockSpec(memory_space=pltpu.SMEM)
    begin = pl.BlockSpec((1, n, 1, count), lambda r: (r, 0, 0, 0))
    tokens = pl.BlockSpec((n, 1, count, wide), lambda r: (0, r, 0, 0))
    return n, rows, count, wide, smem, begin, tokens


def attend(need, base, begin, q, kvs, heads):
    extras = len(kvs) - 1
    n, rows, count, wide, smem, begin_spec, tokens = attention_specs(q, extras)
    blocks = n * (1 + extras)
    narrow = heads * HEAD_DIM
    return pl.pallas_call(
        partial(attend_kernel, heads, extras),
        grid=(rows,),
        in_specs=[smem, smem, begin_spec, tokens] + [tokens] * (1 + extras),
        out_specs=[
            pl.BlockSpec((n, 1, count, narrow), lambda r: (0, r, 0, 0)),
            pl.BlockSpec((1, n, narrow, count), lambda r: (r, 0, 0, 0)),
            pl.BlockSpec((1, n, heads, count), lambda r: (r, 0, 0, 0)),
        ],
        out_shape=[
            jax.ShapeDtypeStruct((n, rows, count, narrow), BF),
            jax.ShapeDtypeStruct((rows, n, narrow, count), F32),
            jax.ShapeDtypeStruct((rows, n, heads, count), F32),
        ],
        scratch_shapes=[
            pltpu.VMEM((blocks, count, wide), BF),
            pltpu.VMEM((blocks, heads, HEAD_DIM, count), BF),
            pltpu.VMEM((heads, 1, count), F32),
            pltpu.VMEM((heads, 1, count), F32),
            pltpu.VMEM((heads, HEAD_DIM, count), F32),
        ],
        compiler_params=params(),
        name="attend",
    )(need, base, begin, q, *kvs)


def attend_back_kernel(
    heads, extras, need_ref, base_ref, begin_ref, q_ref, do_ref, lse_ref, ot_ref, *refs
):
    kv_refs = refs[: 1 + extras]
    dq_ref = refs[1 + extras]
    dkv_refs = refs[2 + extras : 3 + 2 * extras]
    kv_s, kt_s, dkv_s, dqt_s, delta_s = refs[3 + 2 * extras :]
    n, _, count, _ = q_ref.shape
    blocks = n * (1 + extras)
    row = pl.program_id(0)
    load_pairs(kv_refs, kv_s)

    def turn(kb, _):
        for h in range(heads):
            tile = kv_s[kb, :, h * LANES : (h + 1) * LANES].astype(F32)
            kt_s[kb, h] = tile.T[:HEAD_DIM].astype(BF)
        dkv_s[kb] = jnp.zeros(dkv_s.shape[1:], F32)
        return 0

    lax.fori_loop(0, blocks, turn, 0)

    def per_query(c, _):
        dqt_s[...] = jnp.zeros(dqt_s.shape, F32)
        for h in range(heads):
            cols = slice(h * LANES, (h + 1) * LANES)
            dot_t = do_ref[c, 0, :, cols].astype(F32).T[HEAD_DIM:]
            out_t = ot_ref[0, c, h * HEAD_DIM : (h + 1) * HEAD_DIM]
            delta_s[h] = jnp.sum(dot_t * out_t, axis=0, keepdims=True)

        def per_key(kb, _):
            @pl.when(need_ref[row, c * blocks + kb] > 0)
            def _():
                allowed = allowed_pairs(
                    base_ref, begin_ref, kb, c, n, blocks, (count, count)
                )
                for h in range(heads):
                    cols = slice(h * LANES, (h + 1) * LANES)
                    pair = kv_s[kb, :, cols]
                    query = q_ref[c, 0, :, cols]
                    grad = do_ref[c, 0, :, cols]
                    scores = jnp.where(allowed, dot_nt(pair, query), MASKED)
                    probs = jnp.exp(scores - lse_ref[0, c, h : h + 1])
                    steps = probs * (dot_nt(pair, grad) - delta_s[h])
                    steps = steps.astype(BF)
                    dqt_s[h] += dot(kt_s[kb, h], steps)
                    dkv_s[kb, :, cols] += dot(steps, query) + dot(probs.astype(BF), grad)

            return 0

        lax.fori_loop(0, blocks, per_key, 0)
        for h in range(heads):
            tile = jnp.concatenate([dqt_s[h], jnp.zeros((HEAD_DIM, count), F32)], axis=0)
            dq_ref[c, 0, :, h * LANES : (h + 1) * LANES] = tile.T * SCALE
        return 0

    lax.fori_loop(0, n, per_query, 0)
    for e, ref in enumerate(dkv_refs):
        for c in range(n):
            ref[c, 0] = dkv_s[e * n + c].astype(ref.dtype)


def attend_back(need, base, begin, q, do, lse, ot, kvs, heads):
    extras = len(kvs) - 1
    n, rows, count, wide, smem, begin_spec, tokens = attention_specs(q, extras)
    blocks = n * (1 + extras)
    narrow = heads * HEAD_DIM
    return pl.pallas_call(
        partial(attend_back_kernel, heads, extras),
        grid=(rows,),
        in_specs=[smem, smem, begin_spec, tokens, tokens]
        + [
            pl.BlockSpec((1, n, heads, count), lambda r: (r, 0, 0, 0)),
            pl.BlockSpec((1, n, narrow, count), lambda r: (r, 0, 0, 0)),
        ]
        + [tokens] * (1 + extras),
        out_specs=[tokens] * (2 + extras),
        out_shape=[jax.ShapeDtypeStruct(q.shape, F32)] * 2
        + [jax.ShapeDtypeStruct(q.shape, BF)] * extras,
        scratch_shapes=[
            pltpu.VMEM((blocks, count, wide), BF),
            pltpu.VMEM((blocks, heads, HEAD_DIM, count), BF),
            pltpu.VMEM((blocks, count, wide), F32),
            pltpu.VMEM((heads, HEAD_DIM, count), F32),
            pltpu.VMEM((heads, 1, count), F32),
        ],
        compiler_params=params(),
        name="attend_back",
    )(need, base, begin, q, do, lse, ot, *kvs)


def feed_back_kernel(
    g_ref, x_ref, slope_ref, up_ref, down_ref, vec_ref, gh_ref, scaled_ref, sums_ref
):
    width = g_ref.shape[-1]

    @pl.when(pl.program_id(0) == 0)
    def _():
        sums_ref[...] = jnp.zeros(sums_ref.shape, F32)

    down = down_ref[...].reshape(-1, width)
    grad_hidden = (dot_nt(g_ref[0], down) * slope_ref[0].astype(F32)).astype(BF)
    gh_ref[0] = grad_hidden
    grad_second = dot_nt(grad_hidden, up_ref[...].reshape(width, -1))
    unit = unit_of(x_ref[0])
    sums_ref[0:1] += jnp.sum(grad_second * unit, axis=0, keepdims=True)
    sums_ref[1:2] += jnp.sum(grad_second, axis=0, keepdims=True)
    sums_ref[2:3] += jnp.sum(grad_hidden.astype(F32), axis=0, keepdims=True)
    scaled_ref[0] = grad_second * vec_ref[1:2]


def feed_back(g, xs, slope, gathered, k, vec):
    n, tokens, width = g.shape
    shards, _, ff = gathered.shape
    token = lambda w: pl.BlockSpec((1, tokens, w), lambda c: (c, 0, 0))
    weight = lambda j: pl.BlockSpec((shards, k, ff), lambda c: (0, j, 0))
    fixed = pl.BlockSpec((8, width), lambda c: (0, 0))
    return pl.pallas_call(
        feed_back_kernel,
        grid=(n,),
        in_specs=[token(width), token(width), token(ff), weight(0), weight(1), fixed],
        out_specs=[token(ff), token(width), fixed],
        out_shape=[
            jax.ShapeDtypeStruct((n, tokens, ff), BF),
            jax.ShapeDtypeStruct((n, tokens, width), F32),
            jax.ShapeDtypeStruct((8, width), F32),
        ],
        compiler_params=params(),
        name="feed_back",
    )(g, xs, slope, gathered, gathered, vec)


def exit_kernel(
    heads, extras, dq_ref, dkv_ref, *refs
):
    got_refs = refs[:extras]
    cos_ref, sa_ref, sb_ref, x_ref, mix_ref, vec_ref, scaled_ref, gp_ref, part_ref, sums_ref = refs[
        extras:
    ]
    width = x_ref.shape[-1]

    @pl.when(pl.program_id(0) == 0)
    def _():
        sums_ref[...] = jnp.zeros(sums_ref.shape, F32)

    cosine, sine_a, sine_b = cos_ref[0], sa_ref[0], sb_ref[0]
    for h in range(heads):
        cols = slice(h * LANES, (h + 1) * LANES)
        pair = dkv_ref[0, :, cols]
        for ref in got_refs:
            pair = pair + ref[0, :, cols].astype(F32)
        gp_ref[0, :, cols] = unrotated(pair, cosine, sine_a, sine_b).astype(BF)
        qcols = slice((heads + h) * LANES, (heads + h + 1) * LANES)
        gp_ref[0, :, qcols] = unrotated(dq_ref[0, :, cols], cosine, sine_a, sine_b).astype(BF)
    gp = gp_ref[0]
    grad_first = dot_nt(gp, mix_ref[...].reshape(width, -1))
    unit = unit_of(x_ref[0])
    sums_ref[0:1] += jnp.sum(grad_first * unit, axis=0, keepdims=True)
    sums_ref[1:2] += jnp.sum(grad_first, axis=0, keepdims=True)
    sums_ref[2:3] += jnp.sum(gp.astype(F32), axis=0, keepdims=True)
    part_ref[0] = (grad_first * vec_ref[0:1] + scaled_ref[0]).astype(BF)


def exit_pass(dq, dkv, got, tables, xs, gathered, k, vec, scaled, heads):
    n, tokens, width = xs.shape
    shards, _, ff = gathered.shape
    wide = heads * LANES
    token = lambda w: pl.BlockSpec((1, tokens, w), lambda c: (c, 0, 0))
    weight = lambda j: pl.BlockSpec((shards, k, ff), lambda c: (0, j, 0))
    fixed = pl.BlockSpec((8, width), lambda c: (0, 0))
    flat = lambda a: a.reshape(n, tokens, wide)
    return pl.pallas_call(
        partial(exit_kernel, heads, len(got)),
        grid=(n,),
        in_specs=[token(wide)] * (2 + len(got))
        + [token(LANES)] * 3
        + [token(width), weight(2), fixed, token(width)],
        out_specs=[token(2 * wide), token(width), fixed],
        out_shape=[
            jax.ShapeDtypeStruct((n, tokens, 2 * wide), BF),
            jax.ShapeDtypeStruct((n, tokens, width), BF),
            jax.ShapeDtypeStruct((8, width), F32),
        ],
        compiler_params=params(),
        name="exit_pass",
    )(flat(dq), flat(dkv), *[flat(a) for a in got], *tables, xs, gathered, vec, scaled)


def mix_columns(weight, heads):
    lead = weight.shape[:-1]
    split = weight.reshape(lead + (heads, 3, HEAD_DIM))
    pairs = split[..., 1:, :].reshape(lead + (heads * LANES,))
    query = jnp.concatenate([split[..., 0, :], jnp.zeros_like(split[..., 0, :])], axis=-1)
    return jnp.concatenate([pairs, query.reshape(lead + (heads * LANES,))], axis=-1)


def unmix_columns(grad, heads):
    lead = grad.shape[:-1]
    split = grad.reshape(lead + (2, heads, 2, HEAD_DIM))
    order = [split[..., 1, :, 0, :], split[..., 0, :, 0, :], split[..., 0, :, 1, :]]
    return jnp.stack(order, axis=-2).reshape(lead + (heads * 3 * HEAD_DIM,))


def pack_layer(mix_w, mix_b, dense_w, up_w, up_b, down_w, heads):
    width = up_w.shape[1]
    mix = mix_columns(mix_w, heads)
    wide = lambda v: jnp.pad(v, (0, width - v.shape[0]))[None]
    rows = [up_w, down_w, jnp.pad(mix, ((0, 0), (0, width - mix.shape[1]))), dense_w]
    rows += [wide(up_b), wide(mix_b)]
    total = sum(r.shape[0] for r in rows)
    rows.append(jnp.zeros((-total % 8, width), up_w.dtype))
    return jnp.concatenate(rows, axis=0)


def shards(
    block_input, seq_lengths, project_weight, project_bias, dense_weight, up_weight, up_bias,
    down_weight, norm_gains, shift_vectors, cotangent,
):
    rows, _, own_count, width = block_input.shape
    n = lax.axis_size("tensor")
    places = lax.axis_size("ctx")
    extras = places - 1
    place = lax.axis_index("ctx")
    me = lax.axis_index("tensor")
    block_len = own_count * n
    tokens = rows * own_count
    heads = project_weight.shape[2] // (3 * HEAD_DIM)
    wide = heads * LANES
    k_rows = up_weight.shape[1]
    d_rows = dense_weight.shape[1]
    f_own = up_bias.shape[1]
    m_own = project_bias.shape[1]
    shard_count = lax.axis_size("dp") * places

    ends = jnp.cumsum(seq_lengths, axis=1)
    order = (me + jnp.arange(n, dtype=jnp.int32)) % n
    query_base = place * block_len + order * own_count
    slots = query_base[:, None] + jnp.arange(own_count, dtype=jnp.int32)[None]
    passed = (ends[:, None, None, :] <= slots[None, :, :, None]).astype(jnp.int32)
    begin = jnp.sum(passed * seq_lengths[:, None, None, :], axis=3)
    position = (slots[None] - begin).transpose(1, 0, 2).reshape(-1)
    frequency = 1.0 / 10000.0 ** (jnp.arange(0, ROTARY, 2, dtype=F32) / ROTARY)
    angle = frequency[:, None] * position.astype(F32)[None, :]
    cosine, sine = lax.optimization_barrier((jnp.cos(angle), jnp.sin(angle)))
    cosine, sine = cosine.T, sine.T
    ones = jnp.ones((cosine.shape[0], LANES - ROTARY), F32)
    zero8 = jnp.zeros_like(sine)
    tables = (
        jnp.concatenate([cosine, cosine, ones], axis=1).reshape(n, tokens, LANES),
        jnp.concatenate([-sine, zero8, ones * 0.0], axis=1).reshape(n, tokens, LANES),
        jnp.concatenate([zero8, sine, ones * 0.0], axis=1).reshape(n, tokens, LANES),
    )
    key_base = jnp.concatenate(
        [
            jnp.where(place >= e, (place - e) * block_len + order * own_count, FAR)
            for e in range(places)
        ]
    )
    base = jnp.concatenate([query_base, key_base])
    need = (key_base[None, None, :] <= query_base[None, :, None] + own_count - 1) & (
        key_base[None, None, :] + own_count - 1 >= begin[:, :, :1]
    )
    need = need.astype(jnp.int32).reshape(rows, -1)
    begin = begin.reshape(rows, n, 1, own_count)

    gains = norm_gains.astype(F32)
    shifts = shift_vectors.astype(F32)
    packed = [
        pack_layer(
            project_weight[l], project_bias[l], dense_weight[l], up_weight[l], up_bias[l],
            down_weight[l], heads,
        )
        for l in range(LAYERS)
    ]
    gathered = [
        lax.all_gather(packed[l], ("dp", "ctx"), axis=0, tiled=False) for l in range(LAYERS)
    ]
    vecs, biases, dense_ws, down_ws = [], [], [], []
    for l in range(LAYERS):
        full = gathered[l]
        vec = jnp.concatenate([gains[l].T, shifts[l].T, jnp.zeros((2, width), F32)], axis=0)
        vecs.append(vec)
        b_row = 3 * k_rows + d_rows
        up_b = full[:, b_row, :f_own].reshape(-1).astype(F32)
        mix_b = mix_columns(full[:, b_row + 1, :m_own].reshape(-1).astype(F32), heads)
        size = max(up_b.shape[0], mix_b.shape[0])
        biases.append(
            jnp.stack([jnp.pad(up_b, (0, size - up_b.shape[0])), jnp.pad(mix_b, (0, size - mix_b.shape[0]))])
        )
        dense_ws.append(full[:, 3 * k_rows : 3 * k_rows + d_rows].reshape(-1, width))
        down_ws.append(full[:, k_rows : 2 * k_rows].reshape(-1, width))

    flat = lambda a: a.reshape(n * tokens, -1)
    by_row = lambda a: a.reshape(n, rows, own_count, -1)
    stack = lambda chunks: jnp.stack(chunks)
    residual = block_input[:, 0].reshape(tokens, width).astype(F32)
    sent = block_input[:, 0].reshape(tokens, width)
    cot = cotangent[:, 0].reshape(tokens, width)
    stored = []
    for l in range(LAYERS):
        xs = stack(z_gather(sent))
        first, second, q, kv, active, slope = entry(
            xs, gathered[l], k_rows, biases[l], vecs[l], tables, heads
        )
        q, kv = by_row(q), by_row(kv)
        kvs = [kv] + [
            lax.ppermute(kv, "ctx", [(s, s + e) for s in range(places - e)])
            for e in range(1, places)
        ]
        mixed, ot, lse = attend(need, base, begin, q, kvs, heads)
        mixed = flat(mixed)
        branch = (dot(mixed, dense_ws[l]) + dot(flat(active), down_ws[l])).astype(BF)
        branch = branch.reshape(n, tokens, width)
        share = z_scatter([branch[c] for c in range(n)])
        residual = residual + share + shifts[l, :, 2] + shifts[l, :, 3]
        sent = residual.astype(BF)
        stored.append((xs, first, second, q, kvs, active, slope, mixed, ot, lse))

    grad = cot
    weight_out, small = [None] * LAYERS, [None] * LAYERS
    for l in reversed(range(LAYERS)):
        xs, first, second, q, kvs, active, slope, mixed, ot, lse = stored[l]
        gs = stack(z_gather(grad.astype(BF)))
        gf = flat(gs)
        token_sum = jnp.sum(grad, axis=0)
        gh, scaled, sums_b = feed_back(gs, xs, slope, gathered[l], k_rows, vecs[l])
        dense_pad = jnp.pad(
            dense_ws[l].reshape(heads, HEAD_DIM, width), ((0, 0), (HEAD_DIM, 0), (0, 0))
        ).reshape(wide, width)
        do = dot_nt(gf, dense_pad).astype(BF)
        dq, dkv, *send_back = attend_back(
            need, base, begin, q, by_row(do), lse, ot, kvs, heads
        )
        got = [
            lax.ppermute(send_back[e - 1], "ctx", [(s, s - e) for s in range(e, places)])
            for e in range(1, places)
        ]
        gp, part, sums_a = exit_pass(
            dq, dkv, got, tables, xs, gathered[l], k_rows, vecs[l], scaled, heads
        )
        summed = z_scatter([part[c] for c in range(n)])
        tn = lambda a, b: lax.dot_general(
            flat(a), flat(b), (((0,), (0,)), ((), ())), preferred_element_type=F32
        )
        down_g = tn(active, gs).reshape(shard_count, -1, width)
        up_g = tn(second, gh).reshape(shard_count, k_rows, -1)
        up_bg = jnp.pad(
            sums_b[2].reshape(shard_count, 1, -1), ((0, 0), (0, 7), (0, up_g.shape[2] - f_own))
        )
        dense_g = tn(mixed, gs).reshape(shard_count, d_rows, width)
        mix_g = tn(first, gp).reshape(shard_count, k_rows, -1)
        mix_bg = unmix_columns(sums_a[2, : 2 * wide], heads)
        mix_bg = jnp.pad(
            mix_bg.reshape(shard_count, 1, -1), ((0, 0), (0, 7), (0, width - m_own))
        )
        up_all = scatter_weights(jnp.concatenate([up_g, up_bg], axis=1), False)
        down_s = scatter_weights(down_g, True)
        mix_s = scatter_weights(mix_g, True)
        dense_all = scatter_weights(jnp.concatenate([dense_g, mix_bg], axis=1), False)
        weight_out[l] = (
            unmix_columns(mix_s, heads),
            dense_all[d_rows, :m_own],
            dense_all[:d_rows],
            up_all[:k_rows],
            up_all[k_rows, :f_own],
            down_s,
        )
        small[l] = jnp.stack([sums_a[0], sums_b[0], sums_a[1], sums_b[1], token_sum])
        unit_own = unit_of(xs[0])
        inverse = lax.rsqrt(jnp.var(xs[0].astype(F32), axis=-1, keepdims=True) + EPSILON)
        mean_s = jnp.mean(summed, axis=-1, keepdims=True)
        mean_su = jnp.mean(summed * unit_own, axis=-1, keepdims=True)
        grad = grad + inverse * (summed - mean_s - unit_own * mean_su)

    sums = jnp.stack(small)
    own_cols = width // (n * shard_count)
    sums = sums.reshape(LAYERS * 5, n, shard_count, own_cols).transpose(1, 2, 0, 3)
    pieces = [lax.dynamic_index_in_dim(sums, (me + c) % n, 0, keepdims=False) for c in range(n)]
    total = pieces[0]
    for c in range(1, n):
        total = total + lax.ppermute(pieces[c], "tensor", [(s, (s + c) % n) for s in range(n)])
    total = scatter_weights(total, False, F32).reshape(LAYERS, 5, own_cols)
    gains_out = total[:, :2].transpose(0, 2, 1)
    shifts_out = jnp.stack([total[:, 2], total[:, 3], total[:, 4], total[:, 4]], axis=-1)
    outs = [jnp.stack([weight_out[l][j] for l in range(LAYERS)]) for j in range(6)]
    shape = (rows, 1, own_count, width)
    return (residual.reshape(shape), grad.reshape(shape), *outs, gains_out, shifts_out)


def solution(mesh):
    in_specs = (
        P("dp", "ctx", "tensor", None),
        P("dp", None),
        P(None, ("dp", "ctx"), "tensor"),
        P(None, ("tensor", "dp", "ctx")),
        P(None, ("tensor", "dp", "ctx"), None),
        P(None, ("dp", "ctx"), "tensor"),
        P(None, ("tensor", "dp", "ctx")),
        P(None, ("tensor", "dp", "ctx"), None),
        P(),
        P(),
        P("dp", "ctx", "tensor", None),
    )
    out_specs = (
        P("dp", "ctx", "tensor", None),
        P("dp", "ctx", "tensor", None),
        P(None, ("dp", "ctx"), "tensor"),
        P(None, ("tensor", "dp", "ctx")),
        P(None, ("tensor", "dp", "ctx"), None),
        P(None, ("dp", "ctx"), "tensor"),
        P(None, ("tensor", "dp", "ctx")),
        P(None, ("tensor", "dp", "ctx"), None),
        P(None, ("tensor", "dp", "ctx"), None),
        P(None, ("tensor", "dp", "ctx"), None),
    )
    return jax.shard_map(shards, mesh=mesh, in_specs=in_specs, out_specs=out_specs, check_vma=False)
```

```python
from functools import partial

import jax
import jax.numpy as jnp
from jax import lax
from jax.experimental import pallas as pl
from jax.experimental.pallas import tpu as pltpu
from jax.sharding import PartitionSpec as P

HEAD_DIM = 64
ROTARY = 16
LAYERS = 2
EPSILON = 1e-05
MASKED = -1e30
LANES = 128
SCALE = HEAD_DIM ** (-0.5)
FAR = 1 << 24
BF = jnp.bfloat16
F32 = jnp.float32
NT = (((1,), (1,)), ((), ()))


def dot(a, b):
    return jnp.dot(a, b, preferred_element_type=F32)


def dot_nt(a, b):
    return lax.dot_general(a, b, NT, preferred_element_type=F32)


COST = pl.CostEstimate(flops=1024, transcendentals=0, bytes_accessed=1024)


def params(mib=56):
    return pltpu.CompilerParams(vmem_limit_bytes=mib << 20)


def z_gather(own):
    n = lax.axis_size("tensor")
    return [own] + [
        lax.ppermute(own, "tensor", [(s, (s - c) % n) for s in range(n)]) for c in range(1, n)
    ]


def z_scatter(parts):
    n = lax.axis_size("tensor")
    total = parts[0].astype(F32)
    for c in range(1, n):
        got = lax.ppermute(parts[c].astype(BF), "tensor", [(s, (s + c) % n) for s in range(n)])
        total = total + got.astype(F32)
    return total


def after(value, *needed):
    return lax.optimization_barrier((value,) + needed)[0]


def bits_of(axis):
    return lax.axis_size(axis).bit_length() - 1


def scatter_weights(value, first_y, wire=BF):
    nd, nc = lax.axis_size("dp"), lax.axis_size("ctx")
    kd, kc = bits_of("dp"), bits_of("ctx")
    if nd != 1 << kd or nc != 1 << kc:
        flat = value.astype(wire)
        return lax.psum_scatter(flat, ("dp", "ctx"), scatter_dimension=0, tiled=True)[0].astype(F32)
    labels = [("dp", b) for b in reversed(range(kd))] + [("ctx", b) for b in reversed(range(kc))]
    core = [("dp", 0)] if kd else []
    y_steps = [("dp", b) for b in range(1, kd)]
    x_steps = [("ctx", b) for b in range(kc)]
    order = core + (y_steps + x_steps if first_y else x_steps + y_steps)
    rest = value.shape[1:]
    value = value.reshape((2,) * (kd + kc) + rest)
    for axis, bit in order:
        dim = labels.index((axis, bit))
        mine = (lax.axis_index(axis) >> bit) & 1
        send = lax.dynamic_index_in_dim(value, 1 - mine, dim, keepdims=False).astype(wire)
        keep = lax.dynamic_index_in_dim(value, mine, dim, keepdims=False)
        size = lax.axis_size(axis)
        got = lax.ppermute(send, axis, [(s, s ^ (1 << bit)) for s in range(size)])
        value = keep + got.astype(F32)
        labels.pop(dim)
    return value


def rotated(tile, cosine, sine_a, sine_b):
    return tile * cosine + pltpu.roll(tile, LANES - 8, 1) * sine_a + pltpu.roll(tile, 8, 1) * sine_b


def unrotated(tile, cosine, sine_a, sine_b):
    return tile * cosine - pltpu.roll(tile, LANES - 8, 1) * sine_a - pltpu.roll(tile, 8, 1) * sine_b


def unit_of(x):
    values = x.astype(F32)
    centre = values - jnp.mean(values, axis=-1, keepdims=True)
    inverse = lax.rsqrt(jnp.mean(centre * centre, axis=-1, keepdims=True) + EPSILON)
    return centre * inverse


def mix_kernel(
    heads, x_ref, mix_ref, bias_ref, vec_ref, cos_ref, sa_ref, sb_ref, first_ref, q_ref, kv_ref
):
    width = x_ref.shape[-1]
    first = (unit_of(x_ref[0]) * vec_ref[0:1] + vec_ref[2:3]).astype(BF)
    first_ref[0] = first
    mixw = mix_ref[...].reshape(width, -1)
    proj = dot(first, mixw) + bias_ref[1:2, : mixw.shape[1]]
    cosine, sine_a, sine_b = cos_ref[0], sa_ref[0], sb_ref[0]
    for h in range(heads):
        cols = slice(h * LANES, (h + 1) * LANES)
        kv_ref[0, :, cols] = rotated(proj[:, cols], cosine, sine_a, sine_b).astype(BF)
        qcols = slice((heads + h) * LANES, (heads + h + 1) * LANES)
        q_ref[0, :, cols] = (rotated(proj[:, qcols], cosine, sine_a, sine_b) * SCALE).astype(BF)


def feed_kernel(
    x_ref, up_ref, down_ref, bias_ref, vec_ref, second_ref, active_ref, slope_ref, part_ref
):
    width = x_ref.shape[-1]
    second = (unit_of(x_ref[0]) * vec_ref[1:2] + vec_ref[3:4]).astype(BF)
    second_ref[0] = second
    upw = up_ref[...].reshape(width, -1)
    hidden = dot(second, upw) + bias_ref[0:1, : upw.shape[1]]
    half = 0.5 * (1.0 + lax.erf(hidden * (0.5**0.5)))
    active = (hidden * half).astype(BF)
    active_ref[0] = active
    bell = jnp.exp(hidden * hidden * -0.5) * 0.3989422804014327
    slope_ref[0] = (half + hidden * bell).astype(BF)
    part_ref[0] = dot(active, down_ref[...].reshape(-1, width)).astype(BF)


def chunk_specs(n, tokens, gathered, k):
    shards, _, ff = gathered.shape
    token = lambda w: pl.BlockSpec((1, tokens, w), lambda c: (c, 0, 0))
    whole = lambda a: pl.BlockSpec(a.shape, lambda c: (0,) * a.ndim)
    weight = lambda j: pl.BlockSpec((shards, k, ff), lambda c: (0, j, 0))
    out = lambda w: jax.ShapeDtypeStruct((n, tokens, w), BF)
    return token, whole, weight, out


def mix_pass(xs, gathered, k, bias, vec, tables, heads):
    n, tokens, width = xs.shape
    wide = heads * LANES
    token, whole, weight, out = chunk_specs(n, tokens, gathered, k)
    return pl.pallas_call(
        partial(mix_kernel, heads),
        grid=(n,),
        in_specs=[token(width), weight(2), whole(bias), whole(vec)] + [token(LANES)] * 3,
        out_specs=[token(width), token(wide), token(wide)],
        out_shape=[out(width), out(wide), out(wide)],
        compiler_params=params(),
        cost_estimate=COST,
        name="mix_pass",
    )(xs, gathered, bias, vec, *tables)


def feed_pass(me, xs, gathered, k, bias, vec):
    n, tokens, width = xs.shape
    shards, _, ff = gathered.shape
    token = lambda w: pl.BlockSpec((1, tokens, w), lambda c, s: (c, 0, 0))
    whole = lambda a: pl.BlockSpec(a.shape, lambda c, s: (0,) * a.ndim)
    weight = lambda j: pl.BlockSpec((shards, k, ff), lambda c, s: (0, j, 0))
    owner = pl.BlockSpec((1, tokens, width), lambda c, s: ((s[0] + c) % n, 0, 0))
    out = lambda w: jax.ShapeDtypeStruct((n, tokens, w), BF)
    return pl.pallas_call(
        lambda _, *refs: feed_kernel(*refs),
        grid_spec=pltpu.PrefetchScalarGridSpec(
            num_scalar_prefetch=1,
            grid=(n,),
            in_specs=[token(width), weight(0), weight(1), whole(bias), whole(vec)],
            out_specs=[token(width), token(ff), token(ff), owner],
        ),
        out_shape=[out(width), out(ff), out(ff), out(width)],
        compiler_params=params(),
        cost_estimate=COST,
        name="feed_pass",
    )(me.reshape(1), xs, gathered, gathered, bias, vec)


def load_pairs(kv_refs, kv_s):
    n = kv_refs[0].shape[0]
    for e, ref in enumerate(kv_refs):
        for c in range(n):
            kv_s[e * n + c] = ref[c, 0]


def allowed_pairs(base_ref, begin_ref, kb, c, n, blocks, shape):
    key_slot = base_ref[n + kb] + lax.broadcasted_iota(jnp.int32, shape, 0)
    query_slot = base_ref[c] + lax.broadcasted_iota(jnp.int32, shape, 1)
    return (key_slot >= begin_ref[0, c]) & (key_slot <= query_slot)


def attend_kernel(
    heads, extras, need_ref, base_ref, begin_ref, q_ref, *refs
):
    kv_refs = refs[: 1 + extras]
    mixed_ref, ot_ref, lse_ref, kv_s, vt_s, top_s, total_s, acc_s = refs[1 + extras :]
    n, _, count, _ = q_ref.shape
    blocks = n * (1 + extras)
    row = pl.program_id(0)
    load_pairs(kv_refs, kv_s)

    def turn(kb, _):
        for h in range(heads):
            tile = kv_s[kb, :, h * LANES : (h + 1) * LANES].astype(F32)
            vt_s[kb, h] = tile.T[HEAD_DIM:].astype(BF)
        return 0

    lax.fori_loop(0, blocks, turn, 0)

    def per_query(c, _):
        top_s[...] = jnp.full(top_s.shape, MASKED, F32)
        total_s[...] = jnp.zeros(total_s.shape, F32)
        acc_s[...] = jnp.zeros(acc_s.shape, F32)

        def per_key(kb, _):
            @pl.when(need_ref[row, c * blocks + kb] > 0)
            def _():
                allowed = allowed_pairs(
                    base_ref, begin_ref, kb, c, n, blocks, (count, count)
                )
                for h in range(heads):
                    cols = slice(h * LANES, (h + 1) * LANES)
                    scores = dot_nt(kv_s[kb, :, cols], q_ref[c, 0, :, cols])
                    scores = jnp.where(allowed, scores, MASKED)
                    old = top_s[h]
                    new = jnp.maximum(old, jnp.max(scores, axis=0, keepdims=True))
                    fade = jnp.exp(old - new)
                    weights = jnp.exp(scores - new)
                    top_s[h] = new
                    total_s[h] = total_s[h] * fade + jnp.sum(weights, axis=0, keepdims=True)
                    acc_s[h] = acc_s[h] * fade + dot(vt_s[kb, h], weights.astype(BF))

            return 0

        lax.fori_loop(0, blocks, per_key, 0)
        outs = []
        for h in range(heads):
            total = total_s[h]
            outs.append(acc_s[h] / total)
            lse_ref[0, c, h : h + 1] = top_s[h] + jnp.log(total)
        whole = jnp.concatenate(outs, axis=0)
        ot_ref[0, c] = whole
        mixed_ref[c, 0] = whole.T.astype(BF)
        return 0

    lax.fori_loop(0, n, per_query, 0)


def attention_specs(q, extras):
    n, rows, count, wide = q.shape
    smem = pl.BlockSpec(memory_space=pltpu.SMEM)
    begin = pl.BlockSpec((1, n, 1, count), lambda r: (r, 0, 0, 0))
    tokens = pl.BlockSpec((n, 1, count, wide), lambda r: (0, r, 0, 0))
    return n, rows, count, wide, smem, begin, tokens


def attend(need, base, begin, q, kvs, heads):
    extras = len(kvs) - 1
    n, rows, count, wide, smem, begin_spec, tokens = attention_specs(q, extras)
    blocks = n * (1 + extras)
    narrow = heads * HEAD_DIM
    return pl.pallas_call(
        partial(attend_kernel, heads, extras),
        grid=(rows,),
        in_specs=[smem, smem, begin_spec, tokens] + [tokens] * (1 + extras),
        out_specs=[
            pl.BlockSpec((n, 1, count, narrow), lambda r: (0, r, 0, 0)),
            pl.BlockSpec((1, n, narrow, count), lambda r: (r, 0, 0, 0)),
            pl.BlockSpec((1, n, heads, count), lambda r: (r, 0, 0, 0)),
        ],
        out_shape=[
            jax.ShapeDtypeStruct((n, rows, count, narrow), BF),
            jax.ShapeDtypeStruct((rows, n, narrow, count), F32),
            jax.ShapeDtypeStruct((rows, n, heads, count), F32),
        ],
        scratch_shapes=[
            pltpu.VMEM((blocks, count, wide), BF),
            pltpu.VMEM((blocks, heads, HEAD_DIM, count), BF),
            pltpu.VMEM((heads, 1, count), F32),
            pltpu.VMEM((heads, 1, count), F32),
            pltpu.VMEM((heads, HEAD_DIM, count), F32),
        ],
        compiler_params=params(),
        cost_estimate=COST,
        name="attend",
    )(need, base, begin, q, *kvs)


def attend_back_kernel(
    heads, extras, need_ref, base_ref, begin_ref, q_ref, do_ref, lse_ref, ot_ref, *refs
):
    kv_refs = refs[: 1 + extras]
    dq_ref = refs[1 + extras]
    dkv_refs = refs[2 + extras : 3 + 2 * extras]
    kv_s, kt_s, dkv_s, dqt_s, delta_s, do_s = refs[3 + 2 * extras :]
    n, _, count, _ = q_ref.shape
    blocks = n * (1 + extras)
    row = pl.program_id(0)
    load_pairs(kv_refs, kv_s)

    def turn(kb, _):
        for h in range(heads):
            tile = kv_s[kb, :, h * LANES : (h + 1) * LANES].astype(F32)
            kt_s[kb, h] = tile.T[:HEAD_DIM].astype(BF)
        dkv_s[kb] = jnp.zeros(dkv_s.shape[1:], F32)
        return 0

    lax.fori_loop(0, blocks, turn, 0)

    def per_query(c, _):
        dqt_s[...] = jnp.zeros(dqt_s.shape, F32)
        for h in range(heads):
            cols = slice(h * LANES, (h + 1) * LANES)
            grad = do_ref[c, 0, :, h * HEAD_DIM : (h + 1) * HEAD_DIM].astype(F32)
            grad = jnp.concatenate([jnp.zeros((count, HEAD_DIM), F32), grad], axis=1)
            do_s[:, cols] = grad.astype(BF)
            dot_t = grad.T[HEAD_DIM:]
            out_t = ot_ref[0, c, h * HEAD_DIM : (h + 1) * HEAD_DIM]
            delta_s[h] = jnp.sum(dot_t * out_t, axis=0, keepdims=True)

        def per_key(kb, _):
            @pl.when(need_ref[row, c * blocks + kb] > 0)
            def _():
                allowed = allowed_pairs(
                    base_ref, begin_ref, kb, c, n, blocks, (count, count)
                )
                for h in range(heads):
                    cols = slice(h * LANES, (h + 1) * LANES)
                    pair = kv_s[kb, :, cols]
                    query = q_ref[c, 0, :, cols]
                    grad = do_s[:, cols]
                    scores = jnp.where(allowed, dot_nt(pair, query), MASKED)
                    probs = jnp.exp(scores - lse_ref[0, c, h : h + 1])
                    steps = probs * (dot_nt(pair, grad) - delta_s[h])
                    steps = steps.astype(BF)
                    dqt_s[h] += dot(kt_s[kb, h], steps)
                    dkv_s[kb, :, cols] += dot(steps, query) + dot(probs.astype(BF), grad)

            return 0

        lax.fori_loop(0, blocks, per_key, 0)
        for h in range(heads):
            tile = jnp.concatenate([dqt_s[h], jnp.zeros((HEAD_DIM, count), F32)], axis=0)
            dq_ref[c, 0, :, h * LANES : (h + 1) * LANES] = tile.T * SCALE
        return 0

    lax.fori_loop(0, n, per_query, 0)
    for e, ref in enumerate(dkv_refs):
        for c in range(n):
            ref[c, 0] = dkv_s[e * n + c].astype(ref.dtype)


def attend_back(need, base, begin, q, do, lse, ot, kvs, heads):
    extras = len(kvs) - 1
    n, rows, count, wide, smem, begin_spec, tokens = attention_specs(q, extras)
    blocks = n * (1 + extras)
    narrow = heads * HEAD_DIM
    return pl.pallas_call(
        partial(attend_back_kernel, heads, extras),
        grid=(rows,),
        in_specs=[smem, smem, begin_spec, tokens]
        + [
            pl.BlockSpec((n, 1, count, narrow), lambda r: (0, r, 0, 0)),
            pl.BlockSpec((1, n, heads, count), lambda r: (r, 0, 0, 0)),
            pl.BlockSpec((1, n, narrow, count), lambda r: (r, 0, 0, 0)),
        ]
        + [tokens] * (1 + extras),
        out_specs=[tokens] * (2 + extras),
        out_shape=[jax.ShapeDtypeStruct(q.shape, F32)] * 2
        + [jax.ShapeDtypeStruct(q.shape, BF)] * extras,
        scratch_shapes=[
            pltpu.VMEM((blocks, count, wide), BF),
            pltpu.VMEM((blocks, heads, HEAD_DIM, count), BF),
            pltpu.VMEM((blocks, count, wide), F32),
            pltpu.VMEM((heads, HEAD_DIM, count), F32),
            pltpu.VMEM((heads, 1, count), F32),
            pltpu.VMEM((count, wide), BF),
        ],
        compiler_params=params(),
        cost_estimate=COST,
        name="attend_back",
    )(need, base, begin, q, do, lse, ot, *kvs)


def feed_back_kernel(
    g_ref, x_ref, slope_ref, up_ref, down_ref, vec_ref, gh_ref, scaled_ref, sums_ref
):
    width = g_ref.shape[-1]

    @pl.when(pl.program_id(0) == 0)
    def _():
        sums_ref[...] = jnp.zeros(sums_ref.shape, F32)

    down = down_ref[...].reshape(-1, width)
    grad_hidden = (dot_nt(g_ref[0], down) * slope_ref[0].astype(F32)).astype(BF)
    gh_ref[0] = grad_hidden
    grad_second = dot_nt(grad_hidden, up_ref[...].reshape(width, -1))
    unit = unit_of(x_ref[0])
    sums_ref[0:1] += jnp.sum(grad_second * unit, axis=0, keepdims=True)
    sums_ref[1:2] += jnp.sum(grad_second, axis=0, keepdims=True)
    sums_ref[2:3] += jnp.sum(grad_hidden.astype(F32), axis=0, keepdims=True)
    scaled_ref[0] = grad_second * vec_ref[1:2]


def feed_back(g, xs, slope, gathered, k, vec):
    n, tokens, width = g.shape
    shards, _, ff = gathered.shape
    token = lambda w: pl.BlockSpec((1, tokens, w), lambda c: (c, 0, 0))
    weight = lambda j: pl.BlockSpec((shards, k, ff), lambda c: (0, j, 0))
    fixed = pl.BlockSpec((8, width), lambda c: (0, 0))
    return pl.pallas_call(
        feed_back_kernel,
        grid=(n,),
        in_specs=[token(width), token(width), token(ff), weight(0), weight(1), fixed],
        out_specs=[token(ff), token(width), fixed],
        out_shape=[
            jax.ShapeDtypeStruct((n, tokens, ff), BF),
            jax.ShapeDtypeStruct((n, tokens, width), F32),
            jax.ShapeDtypeStruct((8, width), F32),
        ],
        compiler_params=params(),
        cost_estimate=COST,
        name="feed_back",
    )(g, xs, slope, gathered, gathered, vec)


def exit_kernel(
    heads, extras, dq_ref, dkv_ref, *refs
):
    got_refs = refs[:extras]
    cos_ref, sa_ref, sb_ref, x_ref, mix_ref, vec_ref, scaled_ref, gp_ref, part_ref, sums_ref = refs[
        extras:
    ]
    width = x_ref.shape[-1]

    @pl.when(pl.program_id(0) == 0)
    def _():
        sums_ref[...] = jnp.zeros(sums_ref.shape, F32)

    cosine, sine_a, sine_b = cos_ref[0], sa_ref[0], sb_ref[0]
    for h in range(heads):
        cols = slice(h * LANES, (h + 1) * LANES)
        pair = dkv_ref[0, :, cols]
        for ref in got_refs:
            pair = pair + ref[0, :, cols].astype(F32)
        gp_ref[0, :, cols] = unrotated(pair, cosine, sine_a, sine_b).astype(BF)
        qcols = slice((heads + h) * LANES, (heads + h + 1) * LANES)
        gp_ref[0, :, qcols] = unrotated(dq_ref[0, :, cols], cosine, sine_a, sine_b).astype(BF)
    gp = gp_ref[0]
    grad_first = dot_nt(gp, mix_ref[...].reshape(width, -1))
    unit = unit_of(x_ref[0])
    sums_ref[0:1] += jnp.sum(grad_first * unit, axis=0, keepdims=True)
    sums_ref[1:2] += jnp.sum(grad_first, axis=0, keepdims=True)
    sums_ref[2:3] += jnp.sum(gp.astype(F32), axis=0, keepdims=True)
    part_ref[0] = (grad_first * vec_ref[0:1] + scaled_ref[0]).astype(BF)


def exit_pass(dq, dkv, got, tables, xs, gathered, k, vec, scaled, heads):
    n, tokens, width = xs.shape
    shards, _, ff = gathered.shape
    wide = heads * LANES
    token = lambda w: pl.BlockSpec((1, tokens, w), lambda c: (c, 0, 0))
    weight = lambda j: pl.BlockSpec((shards, k, ff), lambda c: (0, j, 0))
    fixed = pl.BlockSpec((8, width), lambda c: (0, 0))
    flat = lambda a: a.reshape(n, tokens, wide)
    return pl.pallas_call(
        partial(exit_kernel, heads, len(got)),
        grid=(n,),
        in_specs=[token(wide)] * (2 + len(got))
        + [token(LANES)] * 3
        + [token(width), weight(2), fixed, token(width)],
        out_specs=[token(2 * wide), token(width), fixed],
        out_shape=[
            jax.ShapeDtypeStruct((n, tokens, 2 * wide), BF),
            jax.ShapeDtypeStruct((n, tokens, width), BF),
            jax.ShapeDtypeStruct((8, width), F32),
        ],
        compiler_params=params(),
        cost_estimate=COST,
        name="exit_pass",
    )(flat(dq), flat(dkv), *[flat(a) for a in got], *tables, xs, gathered, vec, scaled)


def mix_columns(weight, heads):
    lead = weight.shape[:-1]
    split = weight.reshape(lead + (heads, 3, HEAD_DIM))
    pairs = split[..., 1:, :].reshape(lead + (heads * LANES,))
    query = jnp.concatenate([split[..., 0, :], jnp.zeros_like(split[..., 0, :])], axis=-1)
    return jnp.concatenate([pairs, query.reshape(lead + (heads * LANES,))], axis=-1)


def unmix_columns(grad, heads):
    lead = grad.shape[:-1]
    split = grad.reshape(lead + (2, heads, 2, HEAD_DIM))
    order = [split[..., 1, :, 0, :], split[..., 0, :, 0, :], split[..., 0, :, 1, :]]
    return jnp.stack(order, axis=-2).reshape(lead + (heads * 3 * HEAD_DIM,))


def pack_layer(mix_w, mix_b, dense_w, up_w, up_b, down_w, heads):
    width = up_w.shape[1]
    mix = mix_columns(mix_w, heads)
    wide = lambda v: jnp.pad(v, (0, width - v.shape[0]))[None]
    rows = [up_w, down_w, jnp.pad(mix, ((0, 0), (0, width - mix.shape[1]))), dense_w]
    rows += [wide(up_b), wide(mix_b)]
    total = sum(r.shape[0] for r in rows)
    rows.append(jnp.zeros((-total % 8, width), up_w.dtype))
    return jnp.concatenate(rows, axis=0)


def shards(
    block_input, seq_lengths, project_weight, project_bias, dense_weight, up_weight, up_bias,
    down_weight, norm_gains, shift_vectors, cotangent,
):
    rows, _, own_count, width = block_input.shape
    n = lax.axis_size("tensor")
    places = lax.axis_size("ctx")
    extras = places - 1
    place = lax.axis_index("ctx")
    me = lax.axis_index("tensor")
    block_len = own_count * n
    tokens = rows * own_count
    heads = project_weight.shape[2] // (3 * HEAD_DIM)
    wide = heads * LANES
    k_rows = up_weight.shape[1]
    d_rows = dense_weight.shape[1]
    f_own = up_bias.shape[1]
    m_own = project_bias.shape[1]
    shard_count = lax.axis_size("dp") * places

    ends = jnp.cumsum(seq_lengths, axis=1)
    order = (me + jnp.arange(n, dtype=jnp.int32)) % n
    query_base = place * block_len + order * own_count
    slots = query_base[:, None] + jnp.arange(own_count, dtype=jnp.int32)[None]
    passed = (ends[:, None, None, :] <= slots[None, :, :, None]).astype(jnp.int32)
    begin = jnp.sum(passed * seq_lengths[:, None, None, :], axis=3)
    position = (slots[None] - begin).transpose(1, 0, 2).reshape(-1)
    frequency = 1.0 / 10000.0 ** (jnp.arange(0, ROTARY, 2, dtype=F32) / ROTARY)
    angle = frequency[:, None] * position.astype(F32)[None, :]
    cosine, sine = lax.optimization_barrier((jnp.cos(angle), jnp.sin(angle)))
    cosine, sine = cosine.T, sine.T
    ones = jnp.ones((cosine.shape[0], LANES - ROTARY), F32)
    zero8 = jnp.zeros_like(sine)
    tables = (
        jnp.concatenate([cosine, cosine, ones], axis=1).reshape(n, tokens, LANES),
        jnp.concatenate([-sine, zero8, ones * 0.0], axis=1).reshape(n, tokens, LANES),
        jnp.concatenate([zero8, sine, ones * 0.0], axis=1).reshape(n, tokens, LANES),
    )
    key_base = jnp.concatenate(
        [
            jnp.where(place >= e, (place - e) * block_len + order * own_count, FAR)
            for e in range(places)
        ]
    )
    base = jnp.concatenate([query_base, key_base])
    need = (key_base[None, None, :] <= query_base[None, :, None] + own_count - 1) & (
        key_base[None, None, :] + own_count - 1 >= begin[:, :, :1]
    )
    need = need.astype(jnp.int32).reshape(rows, -1)
    begin = begin.reshape(rows, n, 1, own_count)

    gains = norm_gains.astype(F32)
    shifts = shift_vectors.astype(F32)
    packed = [
        pack_layer(
            project_weight[l], project_bias[l], dense_weight[l], up_weight[l], up_bias[l],
            down_weight[l], heads,
        )
        for l in range(LAYERS)
    ]
    flat = lambda a: a.reshape(n * tokens, -1)
    by_row = lambda a: a.reshape(n, rows, own_count, -1)
    stack = lambda chunks: jnp.stack(chunks)
    shift_to = lambda v, c: lax.ppermute(v, "tensor", [(s, (s + c) % n) for s in range(n)])
    sent = block_input[:, 0].reshape(tokens, width)
    residual = sent.astype(F32)
    cot = cotangent[:, 0].reshape(tokens, width)

    xs0 = stack(z_gather(sent))
    gather_all = lambda v: lax.all_gather(v, ("dp", "ctx"), axis=0, tiled=False)
    relative = lambda v: jnp.stack(
        [lax.dynamic_index_in_dim(v, (me + c) % n, 0, keepdims=False) for c in range(n)]
    )
    absolute = lambda v: jnp.stack(
        [lax.dynamic_index_in_dim(v, (c - me) % n, 0, keepdims=False) for c in range(n)]
    )
    gathered = [gather_all(packed[0])]
    dense0 = gathered[0][:, 3 * k_rows : 3 * k_rows + d_rows].reshape(-1, width)
    dense_all = lax.all_gather(after(dense0, xs0), "tensor", axis=0, tiled=False)

    vecs, biases, dense_ws = [], [], []

    def unpack(l):
        full = gathered[l]
        vec = jnp.concatenate([gains[l].T, shifts[l].T, jnp.zeros((2, width), F32)], axis=0)
        vecs.append(vec)
        b_row = 3 * k_rows + d_rows
        up_b = full[:, b_row, :f_own].reshape(-1).astype(F32)
        mix_b = mix_columns(full[:, b_row + 1, :m_own].reshape(-1).astype(F32), heads)
        size = max(up_b.shape[0], mix_b.shape[0])
        biases.append(
            jnp.stack([jnp.pad(up_b, (0, size - up_b.shape[0])), jnp.pad(mix_b, (0, size - mix_b.shape[0]))])
        )
        dense_ws.append(full[:, 3 * k_rows : 3 * k_rows + d_rows].reshape(-1, width))

    unpack(0)

    def exchange_pairs(kv):
        return [kv] + [
            lax.ppermute(kv, "ctx", [(s, s + e) for s in range(places - e)])
            for e in range(1, places)
        ]

    first0, q0, kv0 = mix_pass(xs0, gathered[0], k_rows, biases[0], vecs[0], tables, heads)
    q0, kv0 = by_row(q0), by_row(kv0)
    kvs0 = exchange_pairs(kv0)
    second0, active0, slope0, part0 = feed_pass(
        me, after(xs0, kv0), gathered[0], k_rows, biases[0], vecs[0]
    )
    share = lax.psum_scatter(part0, "tensor", scatter_dimension=0, tiled=True)[0].astype(F32)
    later = gather_all(after(packed[1], part0))
    mixed0, ot0, lse0 = attend(need, base, begin, after(q0, part0), kvs0, heads)
    mixed0 = mixed0.reshape(n, tokens, -1)
    dense_all = relative(after(dense_all, mixed0))
    branch = dot(mixed0[0], dense_all[0])
    for c in range(1, n):
        branch = branch + dot(shift_to(mixed0[c], c), dense_all[n - c])
    residual = residual + branch + share + shifts[0, :, 2] + shifts[0, :, 3]

    xs1 = stack(z_gather(residual.astype(BF)))
    gathered.append(after(later, xs1))
    unpack(1)
    cots = lax.all_gather(after(cot.astype(BF), xs1), "tensor", axis=0, tiled=False)
    first1, q1, kv1 = mix_pass(xs1, gathered[1], k_rows, biases[1], vecs[1], tables, heads)
    q1, kv1 = by_row(q1), by_row(kv1)
    kvs1 = exchange_pairs(kv1)
    second1, active1, slope1, part1 = feed_pass(
        me, after(xs1, kv1), gathered[1], k_rows, biases[1], vecs[1]
    )
    cots = relative(after(cots, part1))
    gh1, scaled1, sums_b1 = feed_back(cots, xs1, slope1, gathered[1], k_rows, vecs[1])
    do1 = dot_nt(flat(cots), dense_ws[1]).astype(BF)
    mixed1, ot1, lse1 = attend(need, base, begin, after(q1, part1), kvs1, heads)
    dq1, dkv1, *send_back = attend_back(
        need, base, begin, q1, by_row(do1), lse1, ot1, kvs1, heads
    )

    def return_pairs(sends):
        return [
            lax.ppermute(sends[e - 1], "ctx", [(s, s - e) for s in range(e, places)])
            for e in range(1, places)
        ]

    def own_back(grad, summed, x_own):
        unit = unit_of(x_own)
        values = x_own.astype(F32)
        inverse = lax.rsqrt(jnp.var(values, axis=-1, keepdims=True) + EPSILON)
        mean_s = jnp.mean(summed, axis=-1, keepdims=True)
        mean_su = jnp.mean(summed * unit, axis=-1, keepdims=True)
        return grad + inverse * (summed - mean_s - unit * mean_su)

    tn = lambda a, b: lax.dot_general(
        flat(a), flat(b), (((0,), (0,)), ((), ())), preferred_element_type=F32
    )

    def feed_grads(second, active, gs, gh, sums_b):
        down_g = tn(active, gs).reshape(shard_count, -1, width)
        up_g = tn(second, gh).reshape(shard_count, k_rows, -1)
        up_bg = jnp.pad(
            sums_b[2].reshape(shard_count, 1, -1), ((0, 0), (0, 7), (0, up_g.shape[2] - f_own))
        )
        return [up_g, down_g, up_bg]

    def mix_grads(first, mixed, gs, gp, sums_a):
        dense_g = tn(mixed, gs).reshape(shard_count, d_rows, width)
        mix_g = tn(first, gp).reshape(shard_count, k_rows, -1)
        mix_bg = unmix_columns(sums_a[2, : 2 * wide], heads)
        mix_bg = jnp.pad(
            mix_bg.reshape(shard_count, 1, -1), ((0, 0), (0, 7), (0, width - m_own))
        )
        return [mix_g, dense_g, mix_bg]

    def scatter_whole(parts):
        total = jnp.concatenate([p.astype(BF) for p in parts], axis=1)
        return lax.psum_scatter(
            total, ("dp", "ctx"), scatter_dimension=0, tiled=True
        )[0].astype(F32)

    def feed_out(total):
        f_rows = total.shape[0] - 8 - k_rows
        down = total[k_rows : k_rows + f_rows]
        return total[:k_rows], total[k_rows + f_rows, :f_own], down

    def mix_out(total):
        dense = total[k_rows : k_rows + d_rows]
        return unmix_columns(total[:k_rows], heads), total[k_rows + d_rows, :m_own], dense

    def small_sums(sums_a, sums_b, grad):
        return jnp.stack(
            [sums_a[0], sums_b[0], sums_a[1], sums_b[1], jnp.sum(grad, axis=0)]
        )

    got1 = return_pairs(send_back)
    gp1, parts, sums_a1 = exit_pass(
        dq1, dkv1, got1, tables, xs1, gathered[1], k_rows, vecs[1], scaled1, heads
    )
    summed = z_scatter([parts[c] for c in range(n)])
    mixed1 = after(mixed1, dq1)
    branch1 = dot(flat(absolute(mixed1.reshape(n, tokens, -1))), dense_ws[1])
    branch1 = (branch1 + flat(part1).astype(F32)).astype(BF)
    share1 = lax.psum_scatter(branch1, "tensor", scatter_dimension=0, tiled=True)
    block_output = residual + share1.astype(F32) + shifts[1, :, 2] + shifts[1, :, 3]
    grads1 = feed_grads(second1, active1, after(cots, dq1), gh1, sums_b1)
    grads1 += mix_grads(first1, mixed1, after(cots, dq1), gp1, sums_a1)
    total1 = scatter_whole(grads1)
    cut = total1.shape[0] - (8 + d_rows + k_rows)
    weights1 = (feed_out(total1[:cut]), mix_out(total1[cut:]))
    grad = own_back(cot, summed, xs1[0])

    grad_own = grad.astype(BF)
    pieces = [dot_nt(grad_own, dense_all[c]).astype(BF) for c in range(n)]
    do0 = [pieces[0]] + [None] * (n - 1)
    for c in range(1, n):
        do0[n - c] = shift_to(pieces[c], c)
    do0 = stack(do0)
    gs = lax.all_gather(after(grad_own, *pieces), "tensor", axis=0, tiled=False)
    dq0, dkv0, *send_back = attend_back(
        need, base, begin, q0, by_row(do0), lse0, ot0, kvs0, heads
    )
    got0 = return_pairs(send_back)
    gs = relative(after(gs, dq0))
    gh0, scaled0, sums_b0 = feed_back(
        gs, xs0, slope0, gathered[0], k_rows, vecs[0]
    )
    gp0, parts, sums_a0 = exit_pass(
        dq0, dkv0, got0, tables, xs0, gathered[0], k_rows, vecs[0], scaled0, heads
    )
    summed = z_scatter([parts[c] for c in range(n)])
    feed0 = scatter_whole(feed_grads(second0, active0, gs, gh0, sums_b0))
    mix_g, dense_g, mix_bg = mix_grads(first0, mixed0, gs, gp0, sums_a0)
    mix_s = scatter_weights(mix_g, True)
    dense_s = scatter_weights(jnp.concatenate([dense_g, mix_bg], axis=1), False)
    weights0 = (feed_out(feed0), mix_out(jnp.concatenate([mix_s, dense_s], axis=0)))
    input_grad = own_back(grad, summed, xs0[0])
    small = [small_sums(sums_a0, sums_b0, grad), small_sums(sums_a1, sums_b1, cot)]
    weight_out = []
    for (up_s, up_bs, down_s), (mix_s, mix_bs, dense_s) in (weights0, weights1):
        weight_out.append((mix_s, mix_bs, dense_s, up_s, up_bs, down_s))

    sums = jnp.stack(small)
    own_cols = width // (n * shard_count)
    sums = sums.reshape(LAYERS * 5, n, shard_count, own_cols).transpose(1, 2, 0, 3)
    pieces = [lax.dynamic_index_in_dim(sums, (me + c) % n, 0, keepdims=False) for c in range(n)]
    total = pieces[0]
    for c in range(1, n):
        total = total + shift_to(pieces[c], c)
    total = scatter_weights(total, False, F32).reshape(LAYERS, 5, own_cols)
    gains_out = total[:, :2].transpose(0, 2, 1)
    shifts_out = jnp.stack([total[:, 2], total[:, 3], total[:, 4], total[:, 4]], axis=-1)
    outs = [jnp.stack([weight_out[l][j] for l in range(LAYERS)]) for j in range(6)]
    shape = (rows, 1, own_count, width)
    return (block_output.reshape(shape), input_grad.reshape(shape), *outs, gains_out, shifts_out)


def solution(mesh):
    in_specs = (
        P("dp", "ctx", "tensor", None),
        P("dp", None),
        P(None, ("dp", "ctx"), "tensor"),
        P(None, ("tensor", "dp", "ctx")),
        P(None, ("tensor", "dp", "ctx"), None),
        P(None, ("dp", "ctx"), "tensor"),
        P(None, ("tensor", "dp", "ctx")),
        P(None, ("tensor", "dp", "ctx"), None),
        P(),
        P(),
        P("dp", "ctx", "tensor", None),
    )
    out_specs = (
        P("dp", "ctx", "tensor", None),
        P("dp", "ctx", "tensor", None),
        P(None, ("dp", "ctx"), "tensor"),
        P(None, ("tensor", "dp", "ctx")),
        P(None, ("tensor", "dp", "ctx"), None),
        P(None, ("dp", "ctx"), "tensor"),
        P(None, ("tensor", "dp", "ctx")),
        P(None, ("tensor", "dp", "ctx"), None),
        P(None, ("tensor", "dp", "ctx"), None),
        P(None, ("tensor", "dp", "ctx"), None),
    )
    return jax.shard_map(shards, mesh=mesh, in_specs=in_specs, out_specs=out_specs, check_vma=False)
```

```python
from functools import partial

import jax
import jax.numpy as jnp
from jax import lax
from jax.experimental import pallas as pl
from jax.experimental.pallas import tpu as pltpu
from jax.sharding import PartitionSpec as P

HEAD_DIM = 64
ROTARY = 16
LAYERS = 2
EPSILON = 1e-05
MASKED = -1e30
LANES = 128
SCALE = HEAD_DIM ** (-0.5)
FAR = 1 << 24
BF = jnp.bfloat16
F32 = jnp.float32
NT = (((1,), (1,)), ((), ()))


def dot(a, b):
    return jnp.dot(a, b, preferred_element_type=F32)


def dot_nt(a, b):
    return lax.dot_general(a, b, NT, preferred_element_type=F32)


def cost(micros):
    return pl.CostEstimate(
        flops=int(micros * 1.1e9), transcendentals=0, bytes_accessed=int(micros * 3.6e6)
    )


def params(mib=56):
    return pltpu.CompilerParams(vmem_limit_bytes=mib << 20)


def z_gather(own):
    n = lax.axis_size("tensor")
    return [own] + [
        lax.ppermute(own, "tensor", [(s, (s - c) % n) for s in range(n)]) for c in range(1, n)
    ]


def z_scatter(parts):
    n = lax.axis_size("tensor")
    return [parts[0]] + [
        lax.ppermute(parts[c], "tensor", [(s, (s + c) % n) for s in range(n)]) for c in range(1, n)
    ]


def after(value, *needed):
    return lax.optimization_barrier((value,) + needed)[0]


def bits_of(axis):
    return lax.axis_size(axis).bit_length() - 1


def scatter_weights(value, first_y, wire=BF, gate=None):
    nd, nc = lax.axis_size("dp"), lax.axis_size("ctx")
    kd, kc = bits_of("dp"), bits_of("ctx")
    if nd != 1 << kd or nc != 1 << kc:
        flat = value.astype(wire)
        return lax.psum_scatter(flat, ("dp", "ctx"), scatter_dimension=0, tiled=True)[0].astype(F32)
    labels = [("dp", b) for b in reversed(range(kd))] + [("ctx", b) for b in reversed(range(kc))]
    core = [("dp", 0)] if kd else []
    y_steps = [("dp", b) for b in range(1, kd)]
    x_steps = [("ctx", b) for b in range(kc)]
    order = core + (y_steps + x_steps if first_y else x_steps + y_steps)
    rest = value.shape[1:]
    value = value.reshape((2,) * (kd + kc) + rest)
    for number, (axis, bit) in enumerate(order):
        if number == 1 and gate is not None:
            value = after(value, *gate)
        dim = labels.index((axis, bit))
        mine = (lax.axis_index(axis) >> bit) & 1
        send = lax.dynamic_index_in_dim(value, 1 - mine, dim, keepdims=False).astype(wire)
        keep = lax.dynamic_index_in_dim(value, mine, dim, keepdims=False)
        size = lax.axis_size(axis)
        got = lax.ppermute(send, axis, [(s, s ^ (1 << bit)) for s in range(size)])
        value = keep + got.astype(F32)
        labels.pop(dim)
    return value


def rotated(tile, cosine, sine_a, sine_b):
    return tile * cosine + pltpu.roll(tile, LANES - 8, 1) * sine_a + pltpu.roll(tile, 8, 1) * sine_b


def unrotated(tile, cosine, sine_a, sine_b):
    return tile * cosine - pltpu.roll(tile, LANES - 8, 1) * sine_a - pltpu.roll(tile, 8, 1) * sine_b


def unit_of(x):
    values = x.astype(F32)
    centre = values - jnp.mean(values, axis=-1, keepdims=True)
    inverse = lax.rsqrt(jnp.mean(centre * centre, axis=-1, keepdims=True) + EPSILON)
    return centre * inverse


def mix_kernel(n, heads, *refs):
    chunk_refs = refs[:n]
    mix_ref, bias_ref, vec_ref, cos_ref, sa_ref, sb_ref, xs_ref, first_ref, q_ref, kv_ref = refs[n:]
    load_chunk(chunk_refs, xs_ref.at[0])
    width = xs_ref.shape[-1]
    first = (unit_of(xs_ref[0]) * vec_ref[0:1] + vec_ref[2:3]).astype(BF)
    first_ref[0] = first
    mixw = mix_ref[...].reshape(width, -1)
    proj = dot(first, mixw) + bias_ref[1:2, : mixw.shape[1]]
    cosine, sine_a, sine_b = cos_ref[0], sa_ref[0], sb_ref[0]
    for h in range(heads):
        cols = slice(h * LANES, (h + 1) * LANES)
        kv_ref[0, :, cols] = rotated(proj[:, cols], cosine, sine_a, sine_b).astype(BF)
        qcols = slice((heads + h) * LANES, (heads + h + 1) * LANES)
        q_ref[0, :, cols] = (rotated(proj[:, qcols], cosine, sine_a, sine_b) * SCALE).astype(BF)


def store_chunk(refs, value):
    for j, ref in enumerate(refs):

        @pl.when(pl.program_id(0) == j)
        def _(ref=ref):
            ref[...] = value


def load_chunk(refs, held):
    for j, ref in enumerate(refs):

        @pl.when(pl.program_id(0) == j)
        def _(ref=ref):
            held[...] = ref[...]


def feed_kernel(
    x_ref, up_ref, down_ref, bias_ref, vec_ref, second_ref, active_ref, slope_ref, *part_refs
):
    width = x_ref.shape[-1]
    second = (unit_of(x_ref[0]) * vec_ref[1:2] + vec_ref[3:4]).astype(BF)
    second_ref[0] = second
    upw = up_ref[...].reshape(width, -1)
    hidden = dot(second, upw) + bias_ref[0:1, : upw.shape[1]]
    half = 0.5 * (1.0 + lax.erf(hidden * (0.5**0.5)))
    active = (hidden * half).astype(BF)
    active_ref[0] = active
    bell = jnp.exp(hidden * hidden * -0.5) * 0.3989422804014327
    slope_ref[0] = (half + hidden * bell).astype(BF)
    store_chunk(part_refs, dot(active, down_ref[...].reshape(-1, width)).astype(BF))


def chunk_specs(n, tokens, gathered, k):
    shards, _, ff = gathered.shape
    token = lambda w: pl.BlockSpec((1, tokens, w), lambda c: (c, 0, 0))
    whole = lambda a: pl.BlockSpec(a.shape, lambda c: (0,) * a.ndim)
    weight = lambda j: pl.BlockSpec((shards, k, ff), lambda c: (0, j, 0))
    out = lambda w: jax.ShapeDtypeStruct((n, tokens, w), BF)
    return token, whole, weight, out


def mix_pass(chunks, gathered, k, bias, vec, tables, heads):
    n = len(chunks)
    tokens, width = chunks[0].shape
    wide = heads * LANES
    token, whole, weight, out = chunk_specs(n, tokens, gathered, k)
    return pl.pallas_call(
        partial(mix_kernel, n, heads),
        grid=(n,),
        in_specs=[whole(chunks[0])] * n
        + [weight(2), whole(bias), whole(vec)]
        + [token(LANES)] * 3,
        out_specs=[token(width), token(width), token(wide), token(wide)],
        out_shape=[out(width), out(width), out(wide), out(wide)],
        compiler_params=params(),
        cost_estimate=cost(6.5),
        name="mix_pass",
    )(*chunks, gathered, bias, vec, *tables)


def feed_pass(xs, gathered, k, bias, vec):
    n, tokens, width = xs.shape
    ff = gathered.shape[2]
    token, whole, weight, out = chunk_specs(n, tokens, gathered, k)
    second, active, slope, *parts = pl.pallas_call(
        feed_kernel,
        grid=(n,),
        in_specs=[token(width), weight(0), weight(1), whole(bias), whole(vec)],
        out_specs=[token(width), token(ff), token(ff)]
        + [pl.BlockSpec((tokens, width), lambda c: (0, 0))] * n,
        out_shape=[out(width), out(ff), out(ff)]
        + [jax.ShapeDtypeStruct((tokens, width), BF)] * n,
        compiler_params=params(),
        cost_estimate=cost(8),
        name="feed_pass",
    )(xs, gathered, gathered, bias, vec)
    return second, active, slope, parts


def middle_kernel(n, mixed_ref, dense_ref, *refs):
    part_refs, grad_refs, do_ref, out_refs = refs[:n], refs[n : 2 * n], refs[2 * n], refs[2 * n + 1 :]
    for c in range(n):
        total = dot(mixed_ref[c], dense_ref[...]) + part_refs[c][...].astype(F32)
        out_refs[c][...] = total.astype(BF)
        do_ref[c] = dot_nt(grad_refs[c][...], dense_ref[...]).astype(BF)


def middle(mixed, dense_w, parts, grads):
    n = len(parts)
    do, *outs = pl.pallas_call(
        partial(middle_kernel, n),
        out_shape=[jax.ShapeDtypeStruct(mixed.shape, BF)]
        + [jax.ShapeDtypeStruct(parts[0].shape, BF)] * n,
        compiler_params=params(),
        cost_estimate=cost(4),
        name="middle",
    )(mixed, dense_w, *parts, *grads)
    return do, outs


def load_pairs(kv_refs, kv_s):
    n = kv_refs[0].shape[0]
    for e, ref in enumerate(kv_refs):
        for c in range(n):
            kv_s[e * n + c] = ref[c, 0]


def allowed_pairs(base_ref, begin_ref, kb, c, n, blocks, shape):
    key_slot = base_ref[n + kb] + lax.broadcasted_iota(jnp.int32, shape, 0)
    query_slot = base_ref[c] + lax.broadcasted_iota(jnp.int32, shape, 1)
    return (key_slot >= begin_ref[0, c]) & (key_slot <= query_slot)


def attend_kernel(
    heads, extras, need_ref, base_ref, begin_ref, q_ref, *refs
):
    kv_refs = refs[: 1 + extras]
    mixed_ref, ot_ref, lse_ref, kv_s, vt_s, top_s, total_s, acc_s = refs[1 + extras :]
    n, _, count, _ = q_ref.shape
    blocks = n * (1 + extras)
    row = pl.program_id(0)
    load_pairs(kv_refs, kv_s)

    def turn(kb, _):
        for h in range(heads):
            tile = kv_s[kb, :, h * LANES : (h + 1) * LANES].astype(F32)
            vt_s[kb, h] = tile.T[HEAD_DIM:].astype(BF)
        return 0

    lax.fori_loop(0, blocks, turn, 0)

    def per_query(c, _):
        top_s[...] = jnp.full(top_s.shape, MASKED, F32)
        total_s[...] = jnp.zeros(total_s.shape, F32)
        acc_s[...] = jnp.zeros(acc_s.shape, F32)

        def per_key(kb, _):
            @pl.when(need_ref[row, c * blocks + kb] > 0)
            def _():
                allowed = allowed_pairs(
                    base_ref, begin_ref, kb, c, n, blocks, (count, count)
                )
                for h in range(heads):
                    cols = slice(h * LANES, (h + 1) * LANES)
                    scores = dot_nt(kv_s[kb, :, cols], q_ref[c, 0, :, cols])
                    scores = jnp.where(allowed, scores, MASKED)
                    old = top_s[h]
                    new = jnp.maximum(old, jnp.max(scores, axis=0, keepdims=True))
                    fade = jnp.exp(old - new)
                    weights = jnp.exp(scores - new)
                    top_s[h] = new
                    total_s[h] = total_s[h] * fade + jnp.sum(weights, axis=0, keepdims=True)
                    acc_s[h] = acc_s[h] * fade + dot(vt_s[kb, h], weights.astype(BF))

            return 0

        lax.fori_loop(0, blocks, per_key, 0)
        outs = []
        for h in range(heads):
            total = total_s[h]
            outs.append(acc_s[h] / total)
            lse_ref[0, c, h : h + 1] = top_s[h] + jnp.log(total)
        whole = jnp.concatenate(outs, axis=0)
        ot_ref[0, c] = whole
        mixed_ref[lax.rem(base_ref[n + blocks] + c, n), 0] = whole.T.astype(BF)
        return 0

    lax.fori_loop(0, n, per_query, 0)


def attention_specs(q, extras):
    n, rows, count, wide = q.shape
    smem = pl.BlockSpec(memory_space=pltpu.SMEM)
    begin = pl.BlockSpec((1, n, 1, count), lambda r: (r, 0, 0, 0))
    tokens = pl.BlockSpec((n, 1, count, wide), lambda r: (0, r, 0, 0))
    return n, rows, count, wide, smem, begin, tokens


def attend(need, base, begin, q, kvs, heads):
    extras = len(kvs) - 1
    n, rows, count, wide, smem, begin_spec, tokens = attention_specs(q, extras)
    blocks = n * (1 + extras)
    narrow = heads * HEAD_DIM
    return pl.pallas_call(
        partial(attend_kernel, heads, extras),
        grid=(rows,),
        in_specs=[smem, smem, begin_spec, tokens] + [tokens] * (1 + extras),
        out_specs=[
            pl.BlockSpec((n, 1, count, narrow), lambda r: (0, r, 0, 0)),
            pl.BlockSpec((1, n, narrow, count), lambda r: (r, 0, 0, 0)),
            pl.BlockSpec((1, n, heads, count), lambda r: (r, 0, 0, 0)),
        ],
        out_shape=[
            jax.ShapeDtypeStruct((n, rows, count, narrow), BF),
            jax.ShapeDtypeStruct((rows, n, narrow, count), F32),
            jax.ShapeDtypeStruct((rows, n, heads, count), F32),
        ],
        scratch_shapes=[
            pltpu.VMEM((blocks, count, wide), BF),
            pltpu.VMEM((blocks, heads, HEAD_DIM, count), BF),
            pltpu.VMEM((heads, 1, count), F32),
            pltpu.VMEM((heads, 1, count), F32),
            pltpu.VMEM((heads, HEAD_DIM, count), F32),
        ],
        compiler_params=params(),
        cost_estimate=cost(400),
        name="attend",
    )(need, base, begin, q, *kvs)


def attend_back_kernel(
    heads, extras, need_ref, base_ref, begin_ref, q_ref, do_ref, lse_ref, ot_ref, *refs
):
    kv_refs = refs[: 1 + extras]
    dq_ref = refs[1 + extras]
    dkv_refs = refs[2 + extras : 3 + 2 * extras]
    kv_s, kt_s, dkv_s, dqt_s, delta_s, do_s = refs[3 + 2 * extras :]
    n, _, count, _ = q_ref.shape
    blocks = n * (1 + extras)
    row = pl.program_id(0)
    load_pairs(kv_refs, kv_s)

    def turn(kb, _):
        for h in range(heads):
            tile = kv_s[kb, :, h * LANES : (h + 1) * LANES].astype(F32)
            kt_s[kb, h] = tile.T[:HEAD_DIM].astype(BF)
        dkv_s[kb] = jnp.zeros(dkv_s.shape[1:], F32)
        return 0

    lax.fori_loop(0, blocks, turn, 0)

    def per_query(c, _):
        dqt_s[...] = jnp.zeros(dqt_s.shape, F32)
        for h in range(heads):
            cols = slice(h * LANES, (h + 1) * LANES)
            owner = lax.rem(base_ref[n + blocks] + c, n)
            grad = do_ref[owner, 0, :, h * HEAD_DIM : (h + 1) * HEAD_DIM].astype(F32)
            grad = jnp.concatenate([jnp.zeros((count, HEAD_DIM), F32), grad], axis=1)
            do_s[:, cols] = grad.astype(BF)
            dot_t = grad.T[HEAD_DIM:]
            out_t = ot_ref[0, c, h * HEAD_DIM : (h + 1) * HEAD_DIM]
            delta_s[h] = jnp.sum(dot_t * out_t, axis=0, keepdims=True)

        def per_key(kb, _):
            @pl.when(need_ref[row, c * blocks + kb] > 0)
            def _():
                allowed = allowed_pairs(
                    base_ref, begin_ref, kb, c, n, blocks, (count, count)
                )
                for h in range(heads):
                    cols = slice(h * LANES, (h + 1) * LANES)
                    pair = kv_s[kb, :, cols]
                    query = q_ref[c, 0, :, cols]
                    grad = do_s[:, cols]
                    scores = jnp.where(allowed, dot_nt(pair, query), MASKED)
                    probs = jnp.exp(scores - lse_ref[0, c, h : h + 1])
                    steps = probs * (dot_nt(pair, grad) - delta_s[h])
                    steps = steps.astype(BF)
                    dqt_s[h] += dot(kt_s[kb, h], steps)
                    dkv_s[kb, :, cols] += dot(steps, query) + dot(probs.astype(BF), grad)

            return 0

        lax.fori_loop(0, blocks, per_key, 0)
        for h in range(heads):
            tile = jnp.concatenate([dqt_s[h], jnp.zeros((HEAD_DIM, count), F32)], axis=0)
            dq_ref[c, 0, :, h * LANES : (h + 1) * LANES] = tile.T * SCALE
        return 0

    lax.fori_loop(0, n, per_query, 0)
    for e, ref in enumerate(dkv_refs):
        for c in range(n):
            ref[c, 0] = dkv_s[e * n + c].astype(ref.dtype)


def attend_back(need, base, begin, q, do, lse, ot, kvs, heads):
    extras = len(kvs) - 1
    n, rows, count, wide, smem, begin_spec, tokens = attention_specs(q, extras)
    blocks = n * (1 + extras)
    narrow = heads * HEAD_DIM
    return pl.pallas_call(
        partial(attend_back_kernel, heads, extras),
        grid=(rows,),
        in_specs=[smem, smem, begin_spec, tokens]
        + [
            pl.BlockSpec((n, 1, count, narrow), lambda r: (0, r, 0, 0)),
            pl.BlockSpec((1, n, heads, count), lambda r: (r, 0, 0, 0)),
            pl.BlockSpec((1, n, narrow, count), lambda r: (r, 0, 0, 0)),
        ]
        + [tokens] * (1 + extras),
        out_specs=[tokens] * (2 + extras),
        out_shape=[jax.ShapeDtypeStruct(q.shape, F32)] * 2
        + [jax.ShapeDtypeStruct(q.shape, BF)] * extras,
        scratch_shapes=[
            pltpu.VMEM((blocks, count, wide), BF),
            pltpu.VMEM((blocks, heads, HEAD_DIM, count), BF),
            pltpu.VMEM((blocks, count, wide), F32),
            pltpu.VMEM((heads, HEAD_DIM, count), F32),
            pltpu.VMEM((heads, 1, count), F32),
            pltpu.VMEM((count, wide), BF),
        ],
        compiler_params=params(),
        cost_estimate=cost(400),
        name="attend_back",
    )(need, base, begin, q, do, lse, ot, *kvs)


TN = (((0,), (0,)), ((), ()))


def dot_tn(a, b):
    return lax.dot_general(a, b, TN, preferred_element_type=F32)


def feed_back_kernel(n, *refs):
    grad_refs = refs[:n]
    x_ref, slope_ref, second_ref, active_ref, up_ref, down_ref, vec_ref = refs[n : n + 7]
    scaled_ref, sums_ref, grads_ref, up_s, down_s, grad_s = refs[n + 7 :]
    width = x_ref.shape[-1]
    last = pl.program_id(0) == pl.num_programs(0) - 1

    @pl.when(pl.program_id(0) == 0)
    def _():
        sums_ref[...] = jnp.zeros(sums_ref.shape, F32)
        up_s[...] = jnp.zeros(up_s.shape, F32)
        down_s[...] = jnp.zeros(down_s.shape, F32)

    load_chunk(grad_refs, grad_s)
    down = down_ref[...].reshape(-1, width)
    grad = grad_s[...]
    grad_hidden = (dot_nt(grad, down) * slope_ref[0].astype(F32)).astype(BF)
    grad_second = dot_nt(grad_hidden, up_ref[...].reshape(width, -1))
    unit = unit_of(x_ref[0])
    sums_ref[0:1] += jnp.sum(grad_second * unit, axis=0, keepdims=True)
    sums_ref[1:2] += jnp.sum(grad_second, axis=0, keepdims=True)
    sums_ref[2:3] += jnp.sum(grad_hidden.astype(F32), axis=0, keepdims=True)
    scaled_ref[0] = grad_second * vec_ref[1:2]
    down_s[...] += dot_tn(active_ref[0], grad)
    up_s[...] += dot_tn(second_ref[0], grad_hidden)

    @pl.when(last)
    def _():
        shards, _, k = up_ref.shape[0], None, up_ref.shape[1]
        f = down_s.shape[0] // shards
        grads_ref[:, :k] = up_s[...].astype(BF).reshape(shards, k, -1)
        grads_ref[:, k : k + f] = down_s[...].astype(BF).reshape(shards, f, -1)
        own = up_s.shape[1] // shards
        for s in range(shards):
            tail = jnp.broadcast_to(sums_ref[2:3, s * own : (s + 1) * own], (8, own))
            pad = jnp.zeros((8, width - own), F32)
            grads_ref[s, k + f :] = jnp.concatenate([tail, pad], axis=1).astype(BF)


def feed_back(gs, xs, slope, second, active, gathered, k, vec):
    n, tokens, width = xs.shape
    shards, _, ff = gathered.shape
    f = ff // shards
    token, whole, weight, _ = chunk_specs(n, tokens, gathered, k)
    fixed = pl.BlockSpec((8, width), lambda c: (0, 0))
    grads = (shards, k + f + 8, width)
    return pl.pallas_call(
        partial(feed_back_kernel, n),
        grid=(n,),
        in_specs=[whole(gs[0])] * n
        + [token(width), token(ff), token(width), token(ff), weight(0), weight(1), fixed],
        out_specs=[token(width), fixed, pl.BlockSpec(grads, lambda c: (0, 0, 0))],
        scratch_shapes=[
            pltpu.VMEM((width, ff), F32),
            pltpu.VMEM((ff, width), F32),
            pltpu.VMEM((tokens, width), BF),
        ],
        out_shape=[
            jax.ShapeDtypeStruct((n, tokens, width), F32),
            jax.ShapeDtypeStruct((8, width), F32),
            jax.ShapeDtypeStruct(grads, BF),
        ],
        compiler_params=params(),
        cost_estimate=cost(12),
        name="feed_back",
    )(*gs, xs, slope, second, active, gathered, gathered, vec)


def mix_back_kernel(n, *refs):
    first_ref, gp_ref, mixed_ref, bias_ref = refs[1:5]
    grad_refs = refs[5 : 5 + n]
    grads_ref, mix_s, dense_s, grad_s = refs[5 + n :]
    last = pl.program_id(0) == pl.num_programs(0) - 1

    @pl.when(pl.program_id(0) == 0)
    def _():
        mix_s[...] = jnp.zeros(mix_s.shape, F32)
        dense_s[...] = jnp.zeros(dense_s.shape, F32)

    load_chunk(grad_refs, grad_s)
    mix_s[...] += dot_tn(first_ref[0], gp_ref[0])
    dense_s[...] += dot_tn(mixed_ref[0], grad_s[...])

    @pl.when(last)
    def _():
        shards = grads_ref.shape[0]
        k = mix_s.shape[0] // shards
        d = dense_s.shape[0] // shards
        grads_ref[:, :k] = mix_s[...].astype(BF).reshape(shards, k, -1)
        for s in range(shards):
            low = dense_s[s * d : (s + 1) * d]
            grads_ref[s, k:] = jnp.concatenate([low, bias_ref[s]], axis=0).astype(BF)


def mix_back(turned, first, gp, mixed, gs, bias):
    n, tokens, width = first.shape
    shards = bias.shape[0]
    narrow = mixed.shape[-1]
    token = lambda w: pl.BlockSpec((1, tokens, w), lambda c, s: (c, 0, 0))
    whole = lambda a: pl.BlockSpec(a.shape, lambda c, s: (0,) * a.ndim)
    grads = (shards, width // shards + narrow // shards + 8, width)
    return pl.pallas_call(
        partial(mix_back_kernel, n),
        grid_spec=pltpu.PrefetchScalarGridSpec(
            num_scalar_prefetch=1,
            grid=(n,),
            in_specs=[
                token(width),
                token(gp.shape[-1]),
                pl.BlockSpec((1, tokens, narrow), lambda c, s: ((s[0] + c) % n, 0, 0)),
                whole(bias),
            ]
            + [whole(gs[0])] * n,
            out_specs=pl.BlockSpec(grads, lambda c, s: (0, 0, 0)),
            scratch_shapes=[
                pltpu.VMEM((width, gp.shape[-1]), F32),
                pltpu.VMEM((narrow, width), F32),
                pltpu.VMEM((tokens, width), BF),
            ],
        ),
        out_shape=jax.ShapeDtypeStruct(grads, BF),
        compiler_params=params(),
        cost_estimate=cost(30),
        name="mix_back",
    )(turned, first, gp, mixed, bias, *gs)


def join_kernel(n, mixed_ref, dense_ref, residual_ref, vec_ref, *refs):
    share_refs, out_ref, sent_ref = refs[:n], refs[n], refs[n + 1]
    total = residual_ref[...] + vec_ref[4:5] + vec_ref[5:6]
    for j in range(n):
        total = total + share_refs[j][...].astype(F32) + dot(mixed_ref[j], dense_ref[j])
    out_ref[...] = total
    sent_ref[...] = total.astype(BF)


def join(mixed, dense_all, shares, residual, vec):
    shape = residual.shape
    return pl.pallas_call(
        partial(join_kernel, len(shares)),
        out_shape=[jax.ShapeDtypeStruct(shape, F32), jax.ShapeDtypeStruct(shape, BF)],
        compiler_params=params(),
        cost_estimate=cost(3),
        name="join",
    )(mixed, dense_all, residual, vec, *shares)


def turn_kernel(n, *refs):
    summed = refs[0][...].astype(F32)
    for ref in refs[1:n]:
        summed = summed + ref[...].astype(F32)
    grad_ref, x_ref = refs[n : n + 2]
    refs = refs[n + 2 :]
    values = x_ref[...].astype(F32)
    centre = values - jnp.mean(values, axis=-1, keepdims=True)
    inverse = lax.rsqrt(jnp.mean(centre * centre, axis=-1, keepdims=True) + EPSILON)
    unit = centre * inverse
    mean_s = jnp.mean(summed, axis=-1, keepdims=True)
    mean_su = jnp.mean(summed * unit, axis=-1, keepdims=True)
    grad = grad_ref[...] + inverse * (summed - mean_s - unit * mean_su)
    if len(refs) == 1:
        refs[0][...] = grad
        return
    dense_ref, out_ref, sent_ref, pieces_ref, sums_ref = refs
    out_ref[...] = grad
    sent = grad.astype(BF)
    sent_ref[...] = sent
    for j in range(dense_ref.shape[0]):
        pieces_ref[j] = dot_nt(sent, dense_ref[j]).astype(BF)
    sums_ref[...] = jnp.broadcast_to(jnp.sum(grad, axis=0, keepdims=True), sums_ref.shape)


def turn(parts, grad, x_own, dense_all=None):
    shape = grad.shape
    outs = [jax.ShapeDtypeStruct(shape, F32)]
    more = []
    if dense_all is not None:
        more = [dense_all]
        outs += [
            jax.ShapeDtypeStruct(shape, BF),
            jax.ShapeDtypeStruct((dense_all.shape[0], shape[0], dense_all.shape[1]), BF),
            jax.ShapeDtypeStruct((8, shape[1]), F32),
        ]
    return pl.pallas_call(
        partial(turn_kernel, len(parts)),
        out_shape=outs,
        compiler_params=params(),
        cost_estimate=cost(3),
        name="turn",
    )(*parts, grad, x_own, *more)


def exit_kernel(
    heads, extras, dq_ref, dkv_ref, *refs
):
    got_refs = refs[:extras]
    cos_ref, sa_ref, sb_ref, x_ref, mix_ref, vec_ref, scaled_ref, gp_ref, sums_ref = refs[
        extras : extras + 9
    ]
    part_refs = refs[extras + 9 :]
    width = x_ref.shape[-1]

    @pl.when(pl.program_id(0) == 0)
    def _():
        sums_ref[...] = jnp.zeros(sums_ref.shape, F32)

    cosine, sine_a, sine_b = cos_ref[0], sa_ref[0], sb_ref[0]
    for h in range(heads):
        cols = slice(h * LANES, (h + 1) * LANES)
        pair = dkv_ref[0, :, cols]
        for ref in got_refs:
            pair = pair + ref[0, :, cols].astype(F32)
        gp_ref[0, :, cols] = unrotated(pair, cosine, sine_a, sine_b).astype(BF)
        qcols = slice((heads + h) * LANES, (heads + h + 1) * LANES)
        gp_ref[0, :, qcols] = unrotated(dq_ref[0, :, cols], cosine, sine_a, sine_b).astype(BF)
    gp = gp_ref[0]
    grad_first = dot_nt(gp, mix_ref[...].reshape(width, -1))
    unit = unit_of(x_ref[0])
    sums_ref[0:1] += jnp.sum(grad_first * unit, axis=0, keepdims=True)
    sums_ref[1:2] += jnp.sum(grad_first, axis=0, keepdims=True)
    sums_ref[2:3] += jnp.sum(gp.astype(F32), axis=0, keepdims=True)
    part = (grad_first * vec_ref[0:1] + scaled_ref[0]).astype(BF)
    store_chunk(part_refs, part)


def exit_pass(dq, dkv, got, tables, xs, gathered, k, vec, scaled, heads):
    n, tokens, width = xs.shape
    shards, _, ff = gathered.shape
    wide = heads * LANES
    token = lambda w: pl.BlockSpec((1, tokens, w), lambda c: (c, 0, 0))
    weight = lambda j: pl.BlockSpec((shards, k, ff), lambda c: (0, j, 0))
    fixed = pl.BlockSpec((8, width), lambda c: (0, 0))
    part = pl.BlockSpec((tokens, width), lambda c: (0, 0))
    flat = lambda a: a.reshape(n, tokens, wide)
    gp, sums, *parts = pl.pallas_call(
        partial(exit_kernel, heads, len(got)),
        grid=(n,),
        in_specs=[token(wide)] * (2 + len(got))
        + [token(LANES)] * 3
        + [token(width), weight(2), fixed, token(width)],
        out_specs=[token(2 * wide), fixed] + [part] * n,
        out_shape=[
            jax.ShapeDtypeStruct((n, tokens, 2 * wide), BF),
            jax.ShapeDtypeStruct((8, width), F32),
        ]
        + [jax.ShapeDtypeStruct((tokens, width), BF)] * n,
        compiler_params=params(),
        cost_estimate=cost(100),
        name="exit_pass",
    )(flat(dq), flat(dkv), *[flat(a) for a in got], *tables, xs, gathered, vec, scaled)
    return gp, parts, sums


def mix_columns(weight, heads):
    lead = weight.shape[:-1]
    split = weight.reshape(lead + (heads, 3, HEAD_DIM))
    pairs = split[..., 1:, :].reshape(lead + (heads * LANES,))
    query = jnp.concatenate([split[..., 0, :], jnp.zeros_like(split[..., 0, :])], axis=-1)
    return jnp.concatenate([pairs, query.reshape(lead + (heads * LANES,))], axis=-1)


def unmix_columns(grad, heads):
    lead = grad.shape[:-1]
    split = grad.reshape(lead + (2, heads, 2, HEAD_DIM))
    order = [split[..., 1, :, 0, :], split[..., 0, :, 0, :], split[..., 0, :, 1, :]]
    return jnp.stack(order, axis=-2).reshape(lead + (heads * 3 * HEAD_DIM,))


def pack_layer(mix_w, mix_b, dense_w, up_w, up_b, down_w, heads):
    width = up_w.shape[1]
    mix = mix_columns(mix_w, heads)
    wide = lambda v: jnp.pad(v, (0, width - v.shape[0]))[None]
    rows = [up_w, down_w, jnp.pad(mix, ((0, 0), (0, width - mix.shape[1]))), dense_w]
    rows += [wide(up_b), wide(mix_b)]
    total = sum(r.shape[0] for r in rows)
    rows.append(jnp.zeros((-total % 8, width), up_w.dtype))
    return jnp.concatenate(rows, axis=0)


def shards(
    block_input, seq_lengths, project_weight, project_bias, dense_weight, up_weight, up_bias,
    down_weight, norm_gains, shift_vectors, cotangent,
):
    rows, _, own_count, width = block_input.shape
    n = lax.axis_size("tensor")
    places = lax.axis_size("ctx")
    extras = places - 1
    place = lax.axis_index("ctx")
    me = lax.axis_index("tensor")
    me1 = me.reshape(1)
    block_len = own_count * n
    tokens = rows * own_count
    heads = project_weight.shape[2] // (3 * HEAD_DIM)
    wide = heads * LANES
    k_rows = up_weight.shape[1]
    d_rows = dense_weight.shape[1]
    f_own = up_bias.shape[1]
    m_own = project_bias.shape[1]
    shard_count = lax.axis_size("dp") * places

    ends = jnp.cumsum(seq_lengths, axis=1)
    order = (me + jnp.arange(n, dtype=jnp.int32)) % n
    query_base = place * block_len + order * own_count
    slots = query_base[:, None] + jnp.arange(own_count, dtype=jnp.int32)[None]
    passed = (ends[:, None, None, :] <= slots[None, :, :, None]).astype(jnp.int32)
    begin = jnp.sum(passed * seq_lengths[:, None, None, :], axis=3)
    position = (slots[None] - begin).transpose(1, 0, 2).reshape(-1)
    frequency = 1.0 / 10000.0 ** (jnp.arange(0, ROTARY, 2, dtype=F32) / ROTARY)
    angle = frequency[:, None] * position.astype(F32)[None, :]
    cosine, sine = lax.optimization_barrier((jnp.cos(angle), jnp.sin(angle)))
    cosine, sine = cosine.T, sine.T
    ones = jnp.ones((cosine.shape[0], LANES - ROTARY), F32)
    zero8 = jnp.zeros_like(sine)
    tables = (
        jnp.concatenate([cosine, cosine, ones], axis=1).reshape(n, tokens, LANES),
        jnp.concatenate([-sine, zero8, ones * 0.0], axis=1).reshape(n, tokens, LANES),
        jnp.concatenate([zero8, sine, ones * 0.0], axis=1).reshape(n, tokens, LANES),
    )
    key_base = jnp.concatenate(
        [
            jnp.where(place >= e, (place - e) * block_len + order * own_count, FAR)
            for e in range(places)
        ]
    )
    base = jnp.concatenate([query_base, key_base, me1])
    need = (key_base[None, None, :] <= query_base[None, :, None] + own_count - 1) & (
        key_base[None, None, :] + own_count - 1 >= begin[:, :, :1]
    )
    need = need.astype(jnp.int32).reshape(rows, -1)
    begin = begin.reshape(rows, n, 1, own_count)

    gains = norm_gains.astype(F32)
    shifts = shift_vectors.astype(F32)
    packed = [
        pack_layer(
            project_weight[l], project_bias[l], dense_weight[l], up_weight[l], up_bias[l],
            down_weight[l], heads,
        )
        for l in range(LAYERS)
    ]
    flat = lambda a: a.reshape(n * tokens, -1)
    by_row = lambda a: a.reshape(n, rows, own_count, -1)
    stack = lambda chunks: jnp.stack(chunks)
    shift_to = lambda v, c: lax.ppermute(v, "tensor", [(s, (s + c) % n) for s in range(n)])
    sent = block_input[:, 0].reshape(tokens, width)
    residual = sent.astype(F32)
    cot = cotangent[:, 0].reshape(tokens, width)

    chunks0 = z_gather(sent)
    gather_all = lambda v: lax.all_gather(v, ("dp", "ctx"), axis=0, tiled=False)
    gather_z = lambda v: lax.all_gather(v, "tensor", axis=0, tiled=False)
    swap_z = lambda v: lax.all_to_all(v, "tensor", 0, 0, tiled=True)
    gathered = [gather_all(packed[0])]
    dense0 = gathered[0][:, 3 * k_rows : 3 * k_rows + d_rows].reshape(-1, width)
    absolute = lambda v: jnp.stack(
        [lax.dynamic_index_in_dim(v, (c - me) % n, 0, keepdims=False) for c in range(n)]
    )
    dense_all = gather_z(after(dense0, *chunks0))

    vecs, biases, dense_ws = [], [], []

    def unpack(l):
        full = gathered[l]
        vec = jnp.concatenate([gains[l].T, shifts[l].T, jnp.zeros((2, width), F32)], axis=0)
        vecs.append(vec)
        b_row = 3 * k_rows + d_rows
        up_b = full[:, b_row, :f_own].reshape(-1).astype(F32)
        mix_b = mix_columns(full[:, b_row + 1, :m_own].reshape(-1).astype(F32), heads)
        size = max(up_b.shape[0], mix_b.shape[0])
        biases.append(
            jnp.stack([jnp.pad(up_b, (0, size - up_b.shape[0])), jnp.pad(mix_b, (0, size - mix_b.shape[0]))])
        )
        dense_ws.append(full[:, 3 * k_rows : 3 * k_rows + d_rows].reshape(-1, width))

    unpack(0)

    def exchange_pairs(kv):
        return [kv] + [
            lax.ppermute(kv, "ctx", [(s, s + e) for s in range(places - e)])
            for e in range(1, places)
        ]

    chunks0[0] = after(chunks0[0], packed[1], need, base, begin)
    xs0, first0, q0, kv0 = mix_pass(
        chunks0, gathered[0], k_rows, biases[0], vecs[0], tables, heads
    )
    later = gather_all(after(packed[1], kv0))
    q0, kv0 = by_row(q0), by_row(kv0)
    kvs0 = exchange_pairs(kv0)
    second0, active0, slope0, parts = feed_pass(xs0, gathered[0], k_rows, biases[0], vecs[0])
    shares = z_scatter(parts)
    mixed0, ot0, lse0 = attend(need, base, begin, after(q0, parts[0]), kvs0, heads)
    mixed0 = after(mixed0, *shares).reshape(n, tokens, -1)
    residual, sent = join(swap_z(mixed0), dense_all, shares, residual, vecs[0])

    chunks1 = z_gather(sent)
    gathered.append(after(later, sent))
    unpack(1)
    xs1, first1, q1, kv1 = mix_pass(
        chunks1, gathered[1], k_rows, biases[1], vecs[1], tables, heads
    )
    q1, kv1 = by_row(q1), by_row(kv1)
    kvs1 = exchange_pairs(kv1)
    second1, active1, slope1, parts = feed_pass(xs1, gathered[1], k_rows, biases[1], vecs[1])
    cots = z_gather(after(cot.astype(BF), parts[0]))
    base1 = base - base * (jnp.arange(base.shape[0]) == base.shape[0] - 1)
    mixed1, ot1, lse1 = attend(need, base1, begin, after(q1, parts[0]), kvs1, heads)
    mixed1 = mixed1.reshape(n, tokens, -1)
    do1, branches = middle(mixed1, dense_ws[1], parts, cots)
    shares = z_scatter(branches)
    dq1, dkv1, *send_back = attend_back(
        need, base1, begin, q1, by_row(do1), lse1, ot1, kvs1, heads
    )

    def return_pairs(sends):
        return [
            lax.ppermute(sends[e - 1], "ctx", [(s, s - e) for s in range(e, places)])
            for e in range(1, places)
        ]

    scatter_all = lambda v: lax.psum_scatter(v, ("dp", "ctx"), scatter_dimension=0, tiled=True)[0]

    own_cols = width // (n * shard_count)

    def extra_rows(sums_a, sums_b, token_sum):
        bias = unmix_columns(sums_a[2, : 2 * wide], heads).reshape(shard_count, 1, -1)
        bias = jnp.pad(bias, ((0, 0), (0, 0), (0, width - m_own)))
        sums = jnp.stack([sums_a[0], sums_b[0], sums_a[1], sums_b[1], token_sum])
        sums = sums.reshape(5, n, shard_count, own_cols).transpose(2, 1, 0, 3)
        sums = sums.reshape(shard_count, 1, -1)
        sums = jnp.pad(sums, ((0, 0), (0, 6), (0, width - sums.shape[2])))
        return jnp.concatenate([bias, sums], axis=1)

    def feed_out(total):
        total = total.astype(F32)
        return total[:k_rows], total[-8, :f_own], total[k_rows:-8]

    def mix_out(total):
        total = total.astype(F32)
        sums = total[-7, : n * 5 * own_cols].reshape(n, 5, own_cols)
        return unmix_columns(total[:k_rows], heads), total[-8, :m_own], total[k_rows:-8], sums

    got1 = return_pairs(send_back)
    cots[0] = after(cots[0], dq1)
    scaled1, sums_b1, feed_g1 = feed_back(
        cots, xs1, slope1, second1, active1, gathered[1], k_rows, vecs[1]
    )
    feed1 = scatter_all(feed_g1)
    shares[0] = after(shares[0], dq1)
    block_output = residual + shifts[1, :, 2] + shifts[1, :, 3]
    for share in shares:
        block_output = block_output + share.astype(F32)
    scaled1 = after(scaled1, block_output)
    gp1, parts1, sums_a1 = exit_pass(
        dq1, dkv1, got1, tables, xs1, gathered[1], k_rows, vecs[1], scaled1, heads
    )
    parts1 = z_scatter(parts1)
    rows1 = extra_rows(sums_a1, sums_b1, jnp.sum(cot, axis=0))
    mix_g1 = mix_back(me1 * 0, first1, gp1, mixed1, cots, rows1)

    grad, grad_own, pieces, token_sum0 = turn(
        parts1[:2] + [after(parts1[2], mix_g1, feed1)] + parts1[3:], cot, chunks1[0], dense_all
    )
    do0 = swap_z(pieces)
    mix1 = scatter_all(after(mix_g1, do0))
    gs = z_gather(after(grad_own, do0))
    dq0, dkv0, *send_back = attend_back(
        need, base, begin, q0, by_row(do0), lse0, ot0, kvs0, heads
    )
    got0 = return_pairs(send_back)
    gs[0] = after(gs[0], dq0, mix1)
    scaled0, sums_b0, feed_g0 = feed_back(
        gs, xs0, slope0, second0, active0, gathered[0], k_rows, vecs[0]
    )
    up_g0 = feed_g0[:, :k_rows].astype(F32)
    rest_g0 = feed_g0[:, k_rows:].astype(F32)
    gp0, parts0, sums_a0 = exit_pass(
        dq0, dkv0, got0, tables, xs0, gathered[0], k_rows, vecs[0], scaled0, heads
    )
    parts0 = absolute(jnp.stack(parts0))
    parts0 = [lax.psum_scatter(parts0, "tensor", scatter_dimension=0, tiled=True)[0]]
    rows0 = extra_rows(sums_a0, sums_b0, token_sum0[0])
    mix_g0 = mix_back(me1, first0, gp0, mixed0, gs, rows0)
    mix0 = mix_out(scatter_weights(mix_g0, False))
    up_s0 = scatter_weights(up_g0, False)
    rest_s0 = scatter_weights(rest_g0, True)
    feed0 = jnp.concatenate([up_s0, rest_s0], axis=0)
    mix1 = mix_out(mix1)
    (input_grad,) = turn(parts0, grad, chunks0[0])
    weight_out = []
    for feed_s, mix_s in ((feed_out(feed0), mix0), (feed_out(feed1), mix1)):
        weight_out.append((mix_s[0], mix_s[1], mix_s[2], feed_s[0], feed_s[1], feed_s[2]))

    sums = jnp.stack([mix0[3], mix1[3]], axis=1)
    if n & (n - 1):
        total = lax.psum_scatter(sums, "tensor", scatter_dimension=0, tiled=False)
    else:
        total = sums
        while total.shape[0] > 1:
            step = total.shape[0] // 2
            halves = total.reshape((2, step) + total.shape[1:])
            mine = (me // step) & 1
            send = lax.dynamic_index_in_dim(halves, 1 - mine, 0, keepdims=False)
            keep = lax.dynamic_index_in_dim(halves, mine, 0, keepdims=False)
            total = keep + lax.ppermute(send, "tensor", [(s, s ^ step) for s in range(n)])
        total = total[0]
    gains_out = total[:, :2].transpose(0, 2, 1)
    shifts_out = jnp.stack([total[:, 2], total[:, 3], total[:, 4], total[:, 4]], axis=-1)
    outs = [jnp.stack([weight_out[l][j] for l in range(LAYERS)]) for j in range(6)]
    shape = (rows, 1, own_count, width)
    return (block_output.reshape(shape), input_grad.reshape(shape), *outs, gains_out, shifts_out)


def solution(mesh):
    in_specs = (
        P("dp", "ctx", "tensor", None),
        P("dp", None),
        P(None, ("dp", "ctx"), "tensor"),
        P(None, ("tensor", "dp", "ctx")),
        P(None, ("tensor", "dp", "ctx"), None),
        P(None, ("dp", "ctx"), "tensor"),
        P(None, ("tensor", "dp", "ctx")),
        P(None, ("tensor", "dp", "ctx"), None),
        P(),
        P(),
        P("dp", "ctx", "tensor", None),
    )
    out_specs = (
        P("dp", "ctx", "tensor", None),
        P("dp", "ctx", "tensor", None),
        P(None, ("dp", "ctx"), "tensor"),
        P(None, ("tensor", "dp", "ctx")),
        P(None, ("tensor", "dp", "ctx"), None),
        P(None, ("dp", "ctx"), "tensor"),
        P(None, ("tensor", "dp", "ctx")),
        P(None, ("tensor", "dp", "ctx"), None),
        P(None, ("tensor", "dp", "ctx"), None),
        P(None, ("tensor", "dp", "ctx"), None),
    )
    return jax.shard_map(shards, mesh=mesh, in_specs=in_specs, out_specs=out_specs, check_vma=False)
```

```python
from functools import partial

import jax
import jax.numpy as jnp
from jax import lax
from jax.experimental import pallas as pl
from jax.experimental.pallas import tpu as pltpu
from jax.sharding import PartitionSpec as P

HEAD_DIM = 64
ROTARY = 16
LAYERS = 2
EPSILON = 1e-05
MASKED = -1e30
LANES = 128
SCALE = HEAD_DIM ** (-0.5)
FAR = 1 << 24
BF = jnp.bfloat16
F32 = jnp.float32
NT = (((1,), (1,)), ((), ()))


def dot(a, b):
    return jnp.dot(a, b, preferred_element_type=F32)


def dot_nt(a, b):
    return lax.dot_general(a, b, NT, preferred_element_type=F32)


def cost(micros):
    return pl.CostEstimate(
        flops=int(micros * 1.1e9), transcendentals=0, bytes_accessed=int(micros * 3.6e6)
    )


def params(mib=56):
    return pltpu.CompilerParams(vmem_limit_bytes=mib << 20)


def z_gather(own):
    n = lax.axis_size("tensor")
    return [own] + [
        lax.ppermute(own, "tensor", [(s, (s - c) % n) for s in range(n)]) for c in range(1, n)
    ]


def z_scatter(parts):
    n = lax.axis_size("tensor")
    return [parts[0]] + [
        lax.ppermute(parts[c], "tensor", [(s, (s + c) % n) for s in range(n)]) for c in range(1, n)
    ]


def after(value, *needed):
    return lax.optimization_barrier((value,) + needed)[0]


def bits_of(axis):
    return lax.axis_size(axis).bit_length() - 1


def scatter_weights(value, first_y, wire=BF, gate=None):
    nd, nc = lax.axis_size("dp"), lax.axis_size("ctx")
    kd, kc = bits_of("dp"), bits_of("ctx")
    if nd != 1 << kd or nc != 1 << kc:
        flat = value.astype(wire)
        return lax.psum_scatter(flat, ("dp", "ctx"), scatter_dimension=0, tiled=True)[0].astype(F32)
    labels = [("dp", b) for b in reversed(range(kd))] + [("ctx", b) for b in reversed(range(kc))]
    core = [("dp", 0)] if kd else []
    y_steps = [("dp", b) for b in range(1, kd)]
    x_steps = [("ctx", b) for b in range(kc)]
    order = core + (y_steps + x_steps if first_y else x_steps + y_steps)
    rest = value.shape[1:]
    value = value.reshape((2,) * (kd + kc) + rest)
    for number, (axis, bit) in enumerate(order):
        if number == 1 and gate is not None:
            value = after(value, *gate)
        dim = labels.index((axis, bit))
        mine = (lax.axis_index(axis) >> bit) & 1
        send = lax.dynamic_index_in_dim(value, 1 - mine, dim, keepdims=False).astype(wire)
        keep = lax.dynamic_index_in_dim(value, mine, dim, keepdims=False)
        size = lax.axis_size(axis)
        got = lax.ppermute(send, axis, [(s, s ^ (1 << bit)) for s in range(size)])
        value = keep + got.astype(F32)
        labels.pop(dim)
    return value


def rotated(tile, cosine, sine_a, sine_b):
    return tile * cosine + pltpu.roll(tile, LANES - 8, 1) * sine_a + pltpu.roll(tile, 8, 1) * sine_b


def unrotated(tile, cosine, sine_a, sine_b):
    return tile * cosine - pltpu.roll(tile, LANES - 8, 1) * sine_a - pltpu.roll(tile, 8, 1) * sine_b


def unit_of(x):
    values = x.astype(F32)
    centre = values - jnp.mean(values, axis=-1, keepdims=True)
    inverse = lax.rsqrt(jnp.mean(centre * centre, axis=-1, keepdims=True) + EPSILON)
    return centre * inverse


def gathered_row(tail_ref, row, own):
    shards = tail_ref.shape[0]
    return jnp.concatenate(
        [tail_ref[s].astype(F32)[row : row + 1, :own] for s in range(shards)], axis=1
    )


def mix_kernel(n, heads, own, *refs):
    chunk_refs = refs[:n]
    mix_ref, tail_ref, vec_ref, cos_ref, sa_ref, sb_ref = refs[n : n + 6]
    xs_ref, first_ref, q_ref, kv_ref, bias_s = refs[-5:]
    load_chunk(chunk_refs, xs_ref.at[0])
    width = xs_ref.shape[-1]

    @pl.when(pl.program_id(0) == 0)
    def _():
        raw = gathered_row(tail_ref, 1, own)
        size = 3 * HEAD_DIM
        pieces = [raw[:, h * size + HEAD_DIM : (h + 1) * size] for h in range(heads)]
        blank = jnp.zeros((1, HEAD_DIM), F32)
        for h in range(heads):
            pieces += [raw[:, h * size : h * size + HEAD_DIM], blank]
        bias_s[...] = jnp.concatenate(pieces, axis=1)

    first = (unit_of(xs_ref[0]) * vec_ref[0:1] + vec_ref[2:3]).astype(BF)
    first_ref[0] = first
    proj = dot(first, mix_ref[...].reshape(width, -1)[:, : 2 * heads * LANES]) + bias_s[...]
    cosine, sine_a, sine_b = cos_ref[0], sa_ref[0], sb_ref[0]
    for h in range(heads):
        cols = slice(h * LANES, (h + 1) * LANES)
        kv_ref[0, :, cols] = rotated(proj[:, cols], cosine, sine_a, sine_b).astype(BF)
        qcols = slice((heads + h) * LANES, (heads + h + 1) * LANES)
        q_ref[0, :, cols] = (rotated(proj[:, qcols], cosine, sine_a, sine_b) * SCALE).astype(BF)


def store_chunk(refs, value):
    for j, ref in enumerate(refs):

        @pl.when(pl.program_id(0) == j)
        def _(ref=ref):
            ref[...] = value


def load_chunk(refs, held):
    for j, ref in enumerate(refs):

        @pl.when(pl.program_id(0) == j)
        def _(ref=ref):
            held[...] = ref[...]


def feed_kernel(own, *refs):
    x_ref, up_ref, down_ref, tail_ref, vec_ref, second_ref, active_ref, slope_ref = refs[:8]
    part_refs, bias_s = refs[8:-1], refs[-1]

    @pl.when(pl.program_id(0) == 0)
    def _():
        bias_s[...] = gathered_row(tail_ref, 0, own)

    width = x_ref.shape[-1]
    second = (unit_of(x_ref[0]) * vec_ref[1:2] + vec_ref[3:4]).astype(BF)
    second_ref[0] = second
    upw = up_ref[...].reshape(width, -1)
    hidden = dot(second, upw) + bias_s[...]
    half = 0.5 * (1.0 + lax.erf(hidden * (0.5**0.5)))
    active = (hidden * half).astype(BF)
    active_ref[0] = active
    bell = jnp.exp(hidden * hidden * -0.5) * 0.3989422804014327
    slope_ref[0] = (half + hidden * bell).astype(BF)
    store_chunk(part_refs, dot(active, down_ref[...].reshape(-1, width)).astype(BF))


def chunk_specs(n, tokens, gathered, k):
    shards, _, ff = gathered.shape
    token = lambda w: pl.BlockSpec((1, tokens, w), lambda c: (c, 0, 0))
    whole = lambda a: pl.BlockSpec(a.shape, lambda c: (0,) * a.ndim)
    weight = lambda j: pl.BlockSpec((shards, k, ff), lambda c: (0, j, 0))
    out = lambda w: jax.ShapeDtypeStruct((n, tokens, w), BF)
    return token, whole, weight, out


def mix_pass(tokens, chunks, place, n, gathered, k, own, vec, tables, heads, held=()):
    width = chunks[0].shape[1]
    count = len(chunks)
    wide = heads * LANES
    shards, _, ff = gathered.shape
    whole = lambda a: pl.BlockSpec(a.shape, lambda c: (0,) * a.ndim)
    token = lambda w: pl.BlockSpec((1, tokens, w), lambda c: (place + c, 0, 0))
    weight = pl.BlockSpec((shards, k, ff), lambda c: (0, 2, 0))
    tail = pl.BlockSpec((shards, 8, ff), lambda c: (0, 3 * k // 8, 0))
    out = lambda m, w: jax.ShapeDtypeStruct((m, tokens, w), BF)
    first_held = count + 6
    return pl.pallas_call(
        partial(mix_kernel, count, heads, own),
        grid=(count,),
        in_specs=[pl.BlockSpec((tokens, width), lambda c: (0, 0))] * count
        + [weight, tail, whole(vec)]
        + [token(LANES)] * 3
        + [pl.BlockSpec(memory_space=pl.ANY)] * len(held),
        out_specs=[token(width), token(width), token(wide)]
        + [pl.BlockSpec((1, tokens, wide), lambda c: (c, 0, 0))],
        out_shape=[out(n, width), out(n, width), out(n, wide), out(count, wide)],
        input_output_aliases={first_held + i: i for i in range(len(held))},
        scratch_shapes=[pltpu.VMEM((1, 2 * wide), F32)],
        compiler_params=params(),
        cost_estimate=cost(12),
        name="mix_pass",
    )(*chunks, gathered, gathered, vec, *tables, *held)


def feed_pass(xs, gathered, k, own, vec):
    n, tokens, width = xs.shape
    ff = gathered.shape[2]
    token, whole, weight, out = chunk_specs(n, tokens, gathered, k)
    second, active, slope, *parts = pl.pallas_call(
        partial(feed_kernel, own),
        grid=(n,),
        in_specs=[token(width), weight(0), weight(1)]
        + [pl.BlockSpec((gathered.shape[0], 8, ff), lambda c: (0, 3 * k // 8, 0)), whole(vec)],
        out_specs=[token(width), token(ff), token(ff)]
        + [pl.BlockSpec((tokens, width), lambda c: (0, 0))] * n,
        out_shape=[out(width), out(ff), out(ff)]
        + [jax.ShapeDtypeStruct((tokens, width), BF)] * n,
        scratch_shapes=[pltpu.VMEM((1, ff), F32)],
        compiler_params=params(),
        cost_estimate=cost(20),
        name="feed_pass",
    )(xs, gathered, gathered, gathered, vec)
    return second, active, slope, parts


def middle_kernel(n, me_ref, dense_ref, grads_ref, *refs):
    mixed_refs, part_refs = refs[:n], refs[n : 2 * n]
    do_refs, out_refs = refs[2 * n : 3 * n], refs[3 * n :]
    for c in range(n):
        total = dot(mixed_refs[c][...], dense_ref[...]) + part_refs[c][...].astype(F32)
        out_refs[c][...] = total.astype(BF)
        grad = grads_ref[lax.rem(me_ref[0] + c, n)]
        do_refs[c][...] = dot_nt(grad, dense_ref[...]).astype(BF)


def middle(me1, mixed, dense_w, parts, grads):
    n = len(parts)
    vmem = pl.BlockSpec(memory_space=pltpu.VMEM)
    outs = pl.pallas_call(
        partial(middle_kernel, n),
        in_specs=[pl.BlockSpec(memory_space=pltpu.SMEM)] + [vmem] * (2 + 2 * n),
        out_specs=[vmem] * (2 * n),
        out_shape=[jax.ShapeDtypeStruct(mixed[0].shape, BF)] * n
        + [jax.ShapeDtypeStruct(parts[0].shape, BF)] * n,
        compiler_params=params(),
        cost_estimate=cost(4),
        name="middle",
    )(me1, dense_w, grads, *mixed, *parts)
    return outs[:n], outs[n:]


def load_pairs(kv_refs, kv_s):
    place = 0
    for ref in kv_refs:
        for c in range(ref.shape[0]):
            kv_s[place] = ref[c, 0]
            place += 1


def allowed_pairs(base_ref, begin_ref, kb, c, n, blocks, shape):
    key_slot = base_ref[n + kb] + lax.broadcasted_iota(jnp.int32, shape, 0)
    query_slot = base_ref[c] + lax.broadcasted_iota(jnp.int32, shape, 1)
    return (key_slot >= begin_ref[0, c]) & (key_slot <= query_slot)


def attend_kernel(heads, extras, groups, need_ref, base_ref, begin_ref, q_ref, *refs):
    kv_refs = refs[:groups]
    n, _, count, _ = q_ref.shape
    mixed_refs = refs[groups : groups + n]
    ot_ref, lse_ref, kv_s, vt_s, top_s, total_s, acc_s, mixed_s = refs[groups + n :]
    blocks = n * (1 + extras)
    row = pl.program_id(0)
    load_pairs(kv_refs, kv_s)

    def turn(kb, _):
        for h in range(heads):
            tile = kv_s[kb, :, h * LANES : (h + 1) * LANES].astype(F32)
            vt_s[kb, h] = tile.T[HEAD_DIM:].astype(BF)
        return 0

    lax.fori_loop(0, blocks, turn, 0)

    def per_query(c, _):
        top_s[...] = jnp.full(top_s.shape, MASKED, F32)
        total_s[...] = jnp.zeros(total_s.shape, F32)
        acc_s[...] = jnp.zeros(acc_s.shape, F32)

        def per_key(kb, _):
            @pl.when(need_ref[row, c * blocks + kb] > 0)
            def _():
                allowed = allowed_pairs(
                    base_ref, begin_ref, kb, c, n, blocks, (count, count)
                )
                column = lambda h: slice(h * LANES, (h + 1) * LANES)
                held = [
                    dot_nt(kv_s[kb, :, column(h)], q_ref[c, 0, :, column(h)]) for h in range(heads)
                ]
                low, fades = [], []
                for h in range(heads):
                    scores = jnp.where(allowed, held[h], MASKED)
                    old = top_s[h]
                    new = jnp.maximum(old, jnp.max(scores, axis=0, keepdims=True))
                    fade = jnp.exp(old - new)
                    weights = jnp.exp(scores - new)
                    top_s[h] = new
                    total_s[h] = total_s[h] * fade + jnp.sum(weights, axis=0, keepdims=True)
                    low.append(weights.astype(BF))
                    fades.append(fade)
                for h in range(heads):
                    acc_s[h] = acc_s[h] * fades[h] + dot(vt_s[kb, h], low[h])

            return 0

        lax.fori_loop(0, blocks, per_key, 0)
        outs = []
        for h in range(heads):
            total = total_s[h]
            outs.append(acc_s[h] / total)
            lse_ref[0, c, h : h + 1] = top_s[h] + jnp.log(total)
        whole = jnp.concatenate(outs, axis=0)
        ot_ref[0, c] = whole
        mixed_s[c] = whole.T.astype(BF)
        return 0

    lax.fori_loop(0, n, per_query, 0)
    for c in range(n):
        mixed_refs[c][0] = mixed_s[c]


def attention_specs(q, kvs):
    n, rows, count, wide = q.shape
    smem = pl.BlockSpec(memory_space=pltpu.SMEM)
    begin = pl.BlockSpec((1, n, 1, count), lambda r: (r, 0, 0, 0))
    tokens = lambda a: pl.BlockSpec((a.shape[0], 1, count, wide), lambda r: (0, r, 0, 0))
    flat = [a for group in kvs for a in group]
    return n, rows, count, wide, smem, begin, tokens, flat


def attend(need, base, begin, q, kvs, heads):
    extras = len(kvs) - 1
    n, rows, count, wide, smem, begin_spec, tokens, flat = attention_specs(q, kvs)
    blocks = n * (1 + extras)
    narrow = heads * HEAD_DIM
    outs = pl.pallas_call(
        partial(attend_kernel, heads, extras, len(flat)),
        grid=(rows,),
        in_specs=[smem, smem, begin_spec, tokens(q)] + [tokens(a) for a in flat],
        out_specs=[pl.BlockSpec((1, count, narrow), lambda r: (r, 0, 0))] * n
        + [
            pl.BlockSpec((1, n, narrow, count), lambda r: (r, 0, 0, 0)),
            pl.BlockSpec((1, n, heads, count), lambda r: (r, 0, 0, 0)),
        ],
        out_shape=[jax.ShapeDtypeStruct((rows, count, narrow), BF)] * n
        + [
            jax.ShapeDtypeStruct((rows, n, narrow, count), F32),
            jax.ShapeDtypeStruct((rows, n, heads, count), F32),
        ],
        scratch_shapes=[
            pltpu.VMEM((blocks, count, wide), BF),
            pltpu.VMEM((blocks, heads, HEAD_DIM, count), BF),
            pltpu.VMEM((heads, 1, count), F32),
            pltpu.VMEM((heads, 1, count), F32),
            pltpu.VMEM((heads, HEAD_DIM, count), F32),
            pltpu.VMEM((n, count, narrow), BF),
        ],
        compiler_params=params(),
        cost_estimate=cost(400),
        name="attend",
    )(need, base, begin, q, *flat)
    return [a.reshape(rows * count, narrow) for a in outs[:n]], outs[n], outs[n + 1]


def attend_back_kernel(heads, extras, groups, need_ref, base_ref, begin_ref, q_ref, *refs):
    n, _, count, _ = q_ref.shape
    do_refs, lse_ref, ot_ref = refs[:n], refs[n], refs[n + 1]
    kv_refs = refs[n + 2 : n + 2 + groups]
    dq_ref = refs[n + 2 + groups]
    dkv_refs = refs[n + 3 + groups : n + 4 + groups + extras]
    kv_s, kt_s, dkv_s, dqt_s, delta_s, do_s, narrow_s = refs[n + 4 + groups + extras :]
    blocks = n * (1 + extras)
    row = pl.program_id(0)
    load_pairs(kv_refs, kv_s)
    for c in range(n):
        narrow_s[c] = do_refs[c][0]

    def turn(kb, _):
        for h in range(heads):
            tile = kv_s[kb, :, h * LANES : (h + 1) * LANES].astype(F32)
            kt_s[kb, h] = tile.T[:HEAD_DIM].astype(BF)
        dkv_s[kb] = jnp.zeros(dkv_s.shape[1:], F32)
        return 0

    lax.fori_loop(0, blocks, turn, 0)

    def per_query(c, _):
        dqt_s[...] = jnp.zeros(dqt_s.shape, F32)
        for h in range(heads):
            cols = slice(h * LANES, (h + 1) * LANES)
            grad = narrow_s[c, :, h * HEAD_DIM : (h + 1) * HEAD_DIM].astype(F32)
            grad = jnp.concatenate([jnp.zeros((count, HEAD_DIM), F32), grad], axis=1)
            do_s[:, cols] = grad.astype(BF)
            dot_t = grad.T[HEAD_DIM:]
            out_t = ot_ref[0, c, h * HEAD_DIM : (h + 1) * HEAD_DIM]
            delta_s[h] = jnp.sum(dot_t * out_t, axis=0, keepdims=True)

        def per_key(kb, _):
            @pl.when(need_ref[row, c * blocks + kb] > 0)
            def _():
                allowed = allowed_pairs(
                    base_ref, begin_ref, kb, c, n, blocks, (count, count)
                )
                column = lambda h: slice(h * LANES, (h + 1) * LANES)
                pairs = [kv_s[kb, :, column(h)] for h in range(heads)]
                queries = [q_ref[c, 0, :, column(h)] for h in range(heads)]
                grads = [do_s[:, column(h)] for h in range(heads)]
                held = [
                    (dot_nt(pairs[h], queries[h]), dot_nt(pairs[h], grads[h])) for h in range(heads)
                ]
                low = []
                for h in range(heads):
                    scores = jnp.where(allowed, held[h][0], MASKED)
                    probs = jnp.exp(scores - lse_ref[0, c, h : h + 1])
                    steps = probs * (held[h][1] - delta_s[h])
                    low.append((steps.astype(BF), probs.astype(BF)))
                for h in range(heads):
                    dqt_s[h] += dot(kt_s[kb, h], low[h][0])
                    dkv_s[kb, :, column(h)] += dot(low[h][0], queries[h]) + dot(low[h][1], grads[h])

            return 0

        lax.fori_loop(0, blocks, per_key, 0)
        for h in range(heads):
            tile = jnp.concatenate([dqt_s[h], jnp.zeros((HEAD_DIM, count), F32)], axis=0)
            dq_ref[c, 0, :, h * LANES : (h + 1) * LANES] = tile.T * SCALE
        return 0

    lax.fori_loop(0, n, per_query, 0)
    for e, ref in enumerate(dkv_refs):
        for c in range(n):
            ref[c, 0] = dkv_s[e * n + c].astype(ref.dtype)


def attend_back(need, base, begin, q, do, lse, ot, kvs, heads):
    extras = len(kvs) - 1
    n, rows, count, wide, smem, begin_spec, tokens, flat = attention_specs(q, kvs)
    blocks = n * (1 + extras)
    narrow = heads * HEAD_DIM
    return pl.pallas_call(
        partial(attend_back_kernel, heads, extras, len(flat)),
        grid=(rows,),
        in_specs=[smem, smem, begin_spec, tokens(q)]
        + [pl.BlockSpec((1, count, narrow), lambda r: (r, 0, 0))] * n
        + [
            pl.BlockSpec((1, n, heads, count), lambda r: (r, 0, 0, 0)),
            pl.BlockSpec((1, n, narrow, count), lambda r: (r, 0, 0, 0)),
        ]
        + [tokens(a) for a in flat],
        out_specs=[tokens(q)] * (2 + extras),
        out_shape=[jax.ShapeDtypeStruct(q.shape, F32)] * 2
        + [jax.ShapeDtypeStruct(q.shape, BF)] * extras,
        scratch_shapes=[
            pltpu.VMEM((blocks, count, wide), BF),
            pltpu.VMEM((blocks, heads, HEAD_DIM, count), BF),
            pltpu.VMEM((blocks, count, wide), F32),
            pltpu.VMEM((heads, HEAD_DIM, count), F32),
            pltpu.VMEM((heads, 1, count), F32),
            pltpu.VMEM((count, wide), BF),
            pltpu.VMEM((n, count, narrow), BF),
        ],
        compiler_params=params(),
        cost_estimate=cost(40),
        name="attend_back",
    )(need, base, begin, q, *[a.reshape(rows, count, narrow) for a in do], lse, ot, *flat)


TN = (((0,), (0,)), ((), ()))


def dot_tn(a, b):
    return lax.dot_general(a, b, TN, preferred_element_type=F32)


def feed_back_kernel(n, gates, *refs):
    grad_refs = refs[:n]
    x_ref, slope_ref, second_ref, active_ref, up_ref, down_ref, vec_ref = refs[n : n + 7]
    refs = refs[n + 7 + gates :]
    scaled_ref, sums_ref, outs, (up_s, down_s, grad_s) = refs[0], refs[1], refs[2:-3], refs[-3:]
    width = x_ref.shape[-1]
    last = pl.program_id(0) == pl.num_programs(0) - 1

    @pl.when(pl.program_id(0) == 0)
    def _():
        sums_ref[...] = jnp.zeros(sums_ref.shape, F32)
        up_s[...] = jnp.zeros(up_s.shape, F32)
        down_s[...] = jnp.zeros(down_s.shape, F32)

    load_chunk(grad_refs, grad_s)
    down = down_ref[...].reshape(-1, width)
    grad = grad_s[...]
    grad_hidden = (dot_nt(grad, down) * slope_ref[0].astype(F32)).astype(BF)
    grad_second = dot_nt(grad_hidden, up_ref[...].reshape(width, -1))
    unit = unit_of(x_ref[0])
    sums_ref[0:1] += jnp.sum(grad_second * unit, axis=0, keepdims=True)
    sums_ref[1:2] += jnp.sum(grad_second, axis=0, keepdims=True)
    sums_ref[2:3] += jnp.sum(grad_hidden.astype(F32), axis=0, keepdims=True)
    scaled_ref[0] = grad_second * vec_ref[1:2]
    down_s[...] += dot_tn(active_ref[0], grad)
    up_s[...] += dot_tn(second_ref[0], grad_hidden)

    @pl.when(last)
    def _():
        shards, k = up_ref.shape[:2]
        f = down_s.shape[0] // shards
        skip = k if len(outs) == 1 else 0
        outs[0][:, :k] = up_s[...].astype(BF).reshape(shards, k, -1)
        outs[-1][:, skip : skip + f] = down_s[...].astype(BF).reshape(shards, f, -1)
        own = up_s.shape[1] // shards
        for s in range(shards):
            tail = jnp.broadcast_to(sums_ref[2:3, s * own : (s + 1) * own], (8, own))
            pad = jnp.zeros((8, width - own), F32)
            outs[-1][s, skip + f :] = jnp.concatenate([tail, pad], axis=1).astype(BF)


def feed_back(gs, xs, slope, second, active, gathered, k, vec, split, gates=()):
    n, tokens, width = xs.shape
    shards, _, ff = gathered.shape
    f = ff // shards
    token, whole, weight, _ = chunk_specs(n, tokens, gathered, k)
    fixed = pl.BlockSpec((8, width), lambda c: (0, 0))
    grads = [(shards, k, width), (shards, f + 8, width)] if split else [(shards, k + f + 8, width)]
    return pl.pallas_call(
        partial(feed_back_kernel, n, len(gates)),
        grid=(n,),
        in_specs=[whole(gs[0])] * n
        + [token(width), token(ff), token(width), token(ff), weight(0), weight(1), fixed]
        + [pl.BlockSpec(memory_space=pl.ANY)] * len(gates),
        out_specs=[token(width), fixed] + [pl.BlockSpec(g, lambda c: (0, 0, 0)) for g in grads],
        scratch_shapes=[
            pltpu.VMEM((width, ff), F32),
            pltpu.VMEM((ff, width), F32),
            pltpu.VMEM((tokens, width), BF),
        ],
        out_shape=[
            jax.ShapeDtypeStruct((n, tokens, width), F32),
            jax.ShapeDtypeStruct((8, width), F32),
        ]
        + [jax.ShapeDtypeStruct(g, BF) for g in grads],
        compiler_params=params(),
        cost_estimate=cost(12),
        name="feed_back",
    )(*gs, xs, slope, second, active, gathered, gathered, vec, *gates)


def mix_back_kernel(n, *refs):
    first_ref, gp_ref, bias_ref = refs[:3]
    mixed_refs, grad_refs = refs[3 : 3 + n], refs[3 + n : 3 + 2 * n]
    grads_ref, mix_s, dense_s, mixed_s, grad_s = refs[-5:]
    last = pl.program_id(0) == pl.num_programs(0) - 1

    @pl.when(pl.program_id(0) == 0)
    def _():
        mix_s[...] = jnp.zeros(mix_s.shape, F32)
        dense_s[...] = jnp.zeros(dense_s.shape, F32)

    load_chunk(grad_refs, grad_s)
    load_chunk(mixed_refs, mixed_s)
    mix_s[...] += dot_tn(first_ref[0], gp_ref[0])
    dense_s[...] += dot_tn(mixed_s[...], grad_s[...])

    @pl.when(last)
    def _():
        shards = grads_ref.shape[0]
        k = mix_s.shape[0] // shards
        d = dense_s.shape[0] // shards
        grads_ref[:, :k] = mix_s[...].astype(BF).reshape(shards, k, -1)
        for s in range(shards):
            low = dense_s[s * d : (s + 1) * d]
            grads_ref[s, k:] = jnp.concatenate([low, bias_ref[s]], axis=0).astype(BF)


def mix_back(first, gp, mixed, gs, bias, micros, gates=()):
    n, tokens, width = first.shape
    shards = bias.shape[0]
    narrow = mixed[0].shape[-1]
    token = lambda w: pl.BlockSpec((1, tokens, w), lambda c: (c, 0, 0))
    whole = lambda a: pl.BlockSpec(a.shape, lambda c: (0,) * a.ndim)
    grads = (shards, width // shards + narrow // shards + 8, width)
    return pl.pallas_call(
        partial(mix_back_kernel, n),
        grid=(n,),
        in_specs=[token(width), token(gp.shape[-1]), whole(bias)]
        + [whole(mixed[0])] * n
        + [whole(gs[0])] * n
        + [pl.BlockSpec(memory_space=pl.ANY)] * len(gates),
        out_specs=pl.BlockSpec(grads, lambda c: (0, 0, 0)),
        scratch_shapes=[
            pltpu.VMEM((width, gp.shape[-1]), F32),
            pltpu.VMEM((narrow, width), F32),
            pltpu.VMEM((tokens, narrow), BF),
            pltpu.VMEM((tokens, width), BF),
        ],
        out_shape=jax.ShapeDtypeStruct(grads, BF),
        compiler_params=params(),
        cost_estimate=cost(micros),
        name="mix_back",
    )(first, gp, bias, *mixed, *gs, *gates)


def join_kernel(n, me_ref, dense_ref, residual_ref, vec_ref, *refs):
    mixed_refs, share_refs, out_ref, sent_ref = refs[:n], refs[n : 2 * n], refs[2 * n], refs[2 * n + 1]
    total = residual_ref[...] + vec_ref[4:5] + vec_ref[5:6]
    for c in range(n):
        rows = dense_ref[:, (n - c) % n]
        rows = rows.reshape(-1, rows.shape[-1])
        total = total + share_refs[c][...].astype(F32) + dot(mixed_refs[c][...], rows)
    out_ref[...] = total
    sent_ref[...] = total.astype(BF)


def join(me1, mixed, dense_all, shares, residual, vec):
    shape = residual.shape
    vmem = pl.BlockSpec(memory_space=pltpu.VMEM)
    return pl.pallas_call(
        partial(join_kernel, len(shares)),
        in_specs=[pl.BlockSpec(memory_space=pltpu.SMEM)] + [vmem] * (3 + 2 * len(shares)),
        out_specs=[vmem, vmem],
        out_shape=[jax.ShapeDtypeStruct(shape, F32), jax.ShapeDtypeStruct(shape, BF)],
        compiler_params=params(),
        cost_estimate=cost(3),
        name="join",
    )(me1, dense_all, residual, vec, *mixed, *shares)


def turn_kernel(n, gates, me_ref, *refs):
    summed = refs[0][...].astype(F32)
    for ref in refs[1:n]:
        summed = summed + ref[...].astype(F32)
    grad_ref, x_ref = refs[n : n + 2]
    refs = refs[n + 2 :]
    values = x_ref[...].astype(F32)
    centre = values - jnp.mean(values, axis=-1, keepdims=True)
    inverse = lax.rsqrt(jnp.mean(centre * centre, axis=-1, keepdims=True) + EPSILON)
    unit = centre * inverse
    mean_s = jnp.mean(summed, axis=-1, keepdims=True)
    mean_su = jnp.mean(summed * unit, axis=-1, keepdims=True)
    grad = grad_ref[...] + inverse * (summed - mean_s - unit * mean_su)
    if len(refs) == gates + 1:
        refs[-1][...] = grad
        return
    dense_ref, out_ref, sent_ref, sums_ref = refs[0], *refs[gates + 1 : gates + 4]
    piece_refs = refs[gates + 4 :]
    out_ref[...] = grad
    sent = grad.astype(BF)
    sent_ref[...] = sent
    for c, piece_ref in enumerate(piece_refs):
        rows = dense_ref[:, c]
        piece_ref[...] = dot_nt(sent, rows.reshape(-1, rows.shape[-1])).astype(BF)
    sums_ref[...] = jnp.broadcast_to(jnp.sum(grad, axis=0, keepdims=True), sums_ref.shape)


def turn(me1, parts, grad, x_own, dense_all=None, gates=()):
    shape = grad.shape
    outs = [jax.ShapeDtypeStruct(shape, F32)]
    vmem = pl.BlockSpec(memory_space=pltpu.VMEM)
    more = []
    if dense_all is not None:
        more = [dense_all]
        outs += [jax.ShapeDtypeStruct(shape, BF), jax.ShapeDtypeStruct((8, shape[1]), F32)]
        narrow = dense_all.shape[0] * dense_all.shape[2]
        outs += [jax.ShapeDtypeStruct((shape[0], narrow), BF)] * dense_all.shape[1]
    return pl.pallas_call(
        partial(turn_kernel, len(parts), len(gates)),
        in_specs=[pl.BlockSpec(memory_space=pltpu.SMEM)]
        + [vmem] * (len(parts) + 2 + len(more))
        + [pl.BlockSpec(memory_space=pl.ANY)] * len(gates),
        out_specs=[vmem] * len(outs),
        out_shape=outs,
        compiler_params=params(),
        cost_estimate=cost(3),
        name="turn",
    )(me1, *parts, grad, x_own, *more, *gates)


def exit_kernel(heads, extras, gates, dq_ref, dkv_ref, *refs):
    got_refs = refs[:extras]
    cos_ref, sa_ref, sb_ref, x_ref, mix_ref, vec_ref, scaled_ref = refs[extras : extras + 7]
    gp_ref, sums_ref, *part_refs = refs[extras + 7 + gates :]
    width = x_ref.shape[-1]

    @pl.when(pl.program_id(0) == 0)
    def _():
        sums_ref[...] = jnp.zeros(sums_ref.shape, F32)

    cosine, sine_a, sine_b = cos_ref[0], sa_ref[0], sb_ref[0]
    for h in range(heads):
        cols = slice(h * LANES, (h + 1) * LANES)
        pair = dkv_ref[0, :, cols]
        for ref in got_refs:
            pair = pair + ref[0, :, cols].astype(F32)
        gp_ref[0, :, cols] = unrotated(pair, cosine, sine_a, sine_b).astype(BF)
        qcols = slice((heads + h) * LANES, (heads + h + 1) * LANES)
        gp_ref[0, :, qcols] = unrotated(dq_ref[0, :, cols], cosine, sine_a, sine_b).astype(BF)
    gp = gp_ref[0]
    grad_first = dot_nt(gp, mix_ref[...].reshape(width, -1))
    unit = unit_of(x_ref[0])
    sums_ref[0:1] += jnp.sum(grad_first * unit, axis=0, keepdims=True)
    sums_ref[1:2] += jnp.sum(grad_first, axis=0, keepdims=True)
    sums_ref[2:3] += jnp.sum(gp.astype(F32), axis=0, keepdims=True)
    part = (grad_first * vec_ref[0:1] + scaled_ref[0]).astype(BF)
    if len(part_refs) == 1:
        part_refs[0][0] = part
    else:
        store_chunk(part_refs, part)


def exit_pass(me1, dq, dkv, got, tables, xs, gathered, k, vec, scaled, heads, owners, gates=()):
    n, tokens, width = xs.shape
    shards, _, ff = gathered.shape
    wide = heads * LANES
    token = lambda w: pl.BlockSpec((1, tokens, w), lambda c, s: (c, 0, 0))
    weight = lambda j: pl.BlockSpec((shards, k, ff), lambda c, s: (0, j, 0))
    fixed = pl.BlockSpec((8, width), lambda c, s: (0, 0))
    flat = lambda a: a.reshape(n, tokens, wide)
    if owners:
        part_specs = [pl.BlockSpec((1, tokens, width), lambda c, s: ((s[0] + c) % n, 0, 0))]
        part_shapes = [jax.ShapeDtypeStruct((n, tokens, width), BF)]
    else:
        part_specs = [pl.BlockSpec((tokens, width), lambda c, s: (0, 0))] * n
        part_shapes = [jax.ShapeDtypeStruct((tokens, width), BF)] * n
    gp, sums, *parts = pl.pallas_call(
        lambda _, *refs: exit_kernel(heads, len(got), len(gates), *refs),
        grid_spec=pltpu.PrefetchScalarGridSpec(
            num_scalar_prefetch=1,
            grid=(n,),
            in_specs=[token(wide)] * (2 + len(got))
            + [token(LANES)] * 3
            + [token(width), weight(2), fixed, token(width)]
            + [pl.BlockSpec(memory_space=pl.ANY)] * len(gates),
            out_specs=[token(2 * wide), fixed] + part_specs,
        ),
        out_shape=[
            jax.ShapeDtypeStruct((n, tokens, 2 * wide), BF),
            jax.ShapeDtypeStruct((8, width), F32),
        ]
        + part_shapes,
        compiler_params=params(),
        cost_estimate=cost(100),
        name="exit_pass",
    )(me1, flat(dq), flat(dkv), *[flat(a) for a in got], *tables, xs, gathered, vec, scaled, *gates)
    return gp, parts, sums


def mix_columns(weight, heads):
    lead = weight.shape[:-1]
    split = weight.reshape(lead + (heads, 3, HEAD_DIM))
    pairs = split[..., 1:, :].reshape(lead + (heads * LANES,))
    query = jnp.concatenate([split[..., 0, :], jnp.zeros_like(split[..., 0, :])], axis=-1)
    return jnp.concatenate([pairs, query.reshape(lead + (heads * LANES,))], axis=-1)


def unmix_columns(grad, heads):
    lead = grad.shape[:-1]
    split = grad.reshape(lead + (2, heads, 2, HEAD_DIM))
    order = [split[..., 1, :, 0, :], split[..., 0, :, 0, :], split[..., 0, :, 1, :]]
    return jnp.stack(order, axis=-2).reshape(lead + (heads * 3 * HEAD_DIM,))


def pack_layer(mix_w, mix_b, dense_w, up_w, up_b, down_w, heads):
    width = up_w.shape[1]
    mix = mix_columns(mix_w, heads)
    wide = lambda v: jnp.pad(v, (0, width - v.shape[0]))[None]
    rows = [up_w, down_w, jnp.pad(mix, ((0, 0), (0, width - mix.shape[1])))]
    rows += [wide(up_b), wide(mix_b), jnp.zeros((6, width), up_w.dtype)]
    if dense_w is not None:
        rows += [dense_w, jnp.zeros((-dense_w.shape[0] % 8, width), up_w.dtype)]
    return jnp.concatenate(rows, axis=0)


def shards(
    block_input, seq_lengths, project_weight, project_bias, dense_weight, up_weight, up_bias,
    down_weight, norm_gains, shift_vectors, cotangent,
):
    rows, _, own_count, width = block_input.shape
    n = lax.axis_size("tensor")
    places = lax.axis_size("ctx")
    extras = places - 1
    place = lax.axis_index("ctx")
    me = lax.axis_index("tensor")
    me1 = me.reshape(1)
    block_len = own_count * n
    tokens = rows * own_count
    heads = project_weight.shape[2] // (3 * HEAD_DIM)
    wide = heads * LANES
    k_rows = up_weight.shape[1]
    d_rows = dense_weight.shape[1]
    f_own = up_bias.shape[1]
    m_own = project_bias.shape[1]
    shard_count = lax.axis_size("dp") * places

    ends = jnp.cumsum(seq_lengths, axis=1)
    order = (me + jnp.arange(n, dtype=jnp.int32)) % n
    query_base = place * block_len + order * own_count
    slots = query_base[:, None] + jnp.arange(own_count, dtype=jnp.int32)[None]
    passed = (ends[:, None, None, :] <= slots[None, :, :, None]).astype(jnp.int32)
    begin = jnp.sum(passed * seq_lengths[:, None, None, :], axis=3)
    position = (slots[None] - begin).transpose(1, 0, 2).reshape(-1)
    frequency = 1.0 / 10000.0 ** (jnp.arange(0, ROTARY, 2, dtype=F32) / ROTARY)
    angle = frequency[:, None] * position.astype(F32)[None, :]
    cosine, sine = lax.optimization_barrier((jnp.cos(angle), jnp.sin(angle)))
    cosine, sine = cosine.T, sine.T
    ones = jnp.ones((cosine.shape[0], LANES - ROTARY), F32)
    zero8 = jnp.zeros_like(sine)
    tables = (
        jnp.concatenate([cosine, cosine, ones], axis=1).reshape(n, tokens, LANES),
        jnp.concatenate([-sine, zero8, ones * 0.0], axis=1).reshape(n, tokens, LANES),
        jnp.concatenate([zero8, sine, ones * 0.0], axis=1).reshape(n, tokens, LANES),
    )
    key_base = jnp.concatenate(
        [
            jnp.where(place >= e, (place - e) * block_len + order * own_count, FAR)
            for e in range(places)
        ]
    )
    base = jnp.concatenate([query_base, key_base])
    need = (key_base[None, None, :] <= query_base[None, :, None] + own_count - 1) & (
        key_base[None, None, :] + own_count - 1 >= begin[:, :, :1]
    )
    need = need.astype(jnp.int32).reshape(rows, -1)
    begin = begin.reshape(rows, n, 1, own_count)

    gains = norm_gains.astype(F32)
    shifts = shift_vectors.astype(F32)
    packed = [
        pack_layer(
            project_weight[l], project_bias[l], dense_weight[l] if l else None, up_weight[l],
            up_bias[l], down_weight[l], heads,
        )
        for l in range(LAYERS)
    ]
    flat = lambda a: a.reshape(n * tokens, -1)
    by_row = lambda a: a.reshape(n, rows, own_count, -1)
    stack = lambda chunks: jnp.stack(chunks)
    shift_to = lambda v, c: lax.ppermute(v, "tensor", [(s, (s + c) % n) for s in range(n)])
    sent = block_input[:, 0].reshape(tokens, width)
    sent0 = sent
    residual = sent.astype(F32)
    cot = cotangent[:, 0].reshape(tokens, width)

    spare = jnp.zeros((-d_rows % 8, width), BF)
    chunks0 = z_gather(jnp.concatenate([sent, dense_weight[0], spare], axis=0))
    gather_all = lambda v: lax.all_gather(v, ("dp", "ctx"), axis=0, tiled=False)
    gathered = [gather_all(packed[0])]
    gather_z = lambda v: lax.all_gather(v, "tensor", axis=0, tiled=False)
    dense_all = jnp.stack([chunk[tokens : tokens + d_rows] for chunk in chunks0])
    dense_all = gather_all(after(dense_all, gathered[0]))
    vecs = [
        jnp.concatenate([gains[l].T, shifts[l].T, jnp.zeros((2, width), F32)], axis=0)
        for l in range(LAYERS)
    ]

    def mix_groups(chunks, l):
        cut = (n + 1) // 2
        tables_of = tables
        xs, first, q, kv_a = mix_pass(
            tokens, chunks[:cut], 0, n, gathered[l], k_rows, m_own, vecs[l], tables_of, heads
        )
        groups = [kv_a]
        if cut < n:
            xs, first, q, kv_b = mix_pass(
                tokens, chunks[cut:], cut, n, gathered[l], k_rows, m_own, vecs[l], tables_of, heads,
                (xs, first, q),
            )
            groups.append(kv_b)
        groups = [a.reshape(a.shape[0], rows, own_count, wide) for a in groups]
        kvs = [groups] + [
            [lax.ppermute(a, "ctx", [(s, s + e) for s in range(places - e)]) for a in groups]
            for e in range(1, places)
        ]
        return xs, first, by_row(q), kvs

    chunks0[0] = after(chunks0[0], packed[1], need, base, begin)
    xs0, first0, q0, kvs0 = mix_groups(chunks0, 0)
    second0, active0, slope0, parts = feed_pass(xs0, gathered[0], k_rows, f_own, vecs[0])
    later = gather_all(after(packed[1], parts[0]))
    shares = z_scatter(parts)
    mixed0, ot0, lse0 = attend(need, base, begin, after(q0, parts[0]), kvs0, heads)
    sent_mixed = [after(mixed0[0], *shares)] + mixed0[1:]
    sent_mixed = [sent_mixed[0]] + [shift_to(after(mixed0[c], *shares), c) for c in range(1, n)]
    residual, sent = join(me1, sent_mixed, dense_all, shares, residual, vecs[0])

    chunks1 = z_gather(sent)
    gathered.append(after(later, sent))
    dense1 = gathered[1][:, 3 * k_rows + 8 : 3 * k_rows + 8 + d_rows].reshape(-1, width)
    xs1, first1, q1, kvs1 = mix_groups(chunks1, 1)
    second1, active1, slope1, parts = feed_pass(xs1, gathered[1], k_rows, f_own, vecs[1])
    cots = gather_z(after(cot.astype(BF), kvs1[0][0]))
    mixed1, ot1, lse1 = attend(need, base, begin, after(q1, parts[0]), kvs1, heads)
    do1, branches = middle(me1, mixed1, dense1, parts, cots)
    shares = z_scatter(branches)
    dq1, dkv1, *send_back = attend_back(need, base, begin, q1, do1, lse1, ot1, kvs1, heads)

    def return_pairs(sends):
        return [
            lax.ppermute(sends[e - 1], "ctx", [(s, s - e) for s in range(e, places)])
            for e in range(1, places)
        ]

    scatter_all = lambda v: lax.psum_scatter(v, ("dp", "ctx"), scatter_dimension=0, tiled=True)[0]

    own_cols = width // (n * shard_count)

    def extra_rows(sums_a, sums_b, token_sum):
        bias = unmix_columns(sums_a[2, : 2 * wide], heads).reshape(shard_count, 1, -1)
        bias = jnp.pad(bias, ((0, 0), (0, 0), (0, width - m_own)))
        sums = jnp.stack([sums_a[0], sums_b[0], sums_a[1], sums_b[1], token_sum])
        sums = sums.reshape(5, n, shard_count, own_cols).transpose(2, 1, 0, 3)
        sums = sums.reshape(shard_count, 1, -1)
        sums = jnp.pad(sums, ((0, 0), (0, 6), (0, width - sums.shape[2])))
        return jnp.concatenate([bias, sums], axis=1)

    def feed_out(total):
        total = total.astype(F32)
        return total[:k_rows], total[-8, :f_own], total[k_rows:-8]

    def mix_out(total):
        total = total.astype(F32)
        sums = total[-7, : n * 5 * own_cols].reshape(n, 5, own_cols)
        return unmix_columns(total[:k_rows], heads), total[-8, :m_own], total[k_rows:-8], sums

    got1 = return_pairs(send_back)
    cots = after(cots, dq1)
    cots = [lax.dynamic_index_in_dim(cots, (me + c) % n, 0, keepdims=False) for c in range(n)]
    scaled1, sums_b1, feed_g1 = feed_back(
        cots, xs1, slope1, second1, active1, gathered[1], k_rows, vecs[1], False
    )
    feed1 = scatter_all(feed_g1)
    shares[0] = after(shares[0], dq1)
    block_output = residual + shifts[1, :, 2] + shifts[1, :, 3]
    for share in shares:
        block_output = block_output + share.astype(F32)
    scaled1 = after(scaled1, block_output)
    gp1, parts1, sums_a1 = exit_pass(
        me1, dq1, dkv1, got1, tables, xs1, gathered[1], k_rows, vecs[1], scaled1, heads, False
    )
    parts1 = z_scatter(parts1)
    rows1 = extra_rows(sums_a1, sums_b1, jnp.sum(cot, axis=0))
    mix_g1 = mix_back(first1, gp1, mixed1, cots, rows1, 30)

    grad, grad_own, token_sum0, *pieces = turn(
        me1, parts1, cot, chunks1[0], dense_all, (mix_g1, feed1)
    )
    do0 = [pieces[0]] + [None] * (n - 1)
    for c in range(1, n):
        do0[n - c] = shift_to(pieces[c], c)
    mix1 = scatter_all(after(mix_g1, *do0))
    gs = z_gather(after(grad_own, *do0))
    dq0, dkv0, *send_back = attend_back(need, base, begin, q0, do0, lse0, ot0, kvs0, heads)
    got0 = return_pairs(send_back)
    scaled0, sums_b0, up_g0, rest_g0 = feed_back(
        gs, xs0, slope0, second0, active0, gathered[0], k_rows, vecs[0], True, (dq0,)
    )
    gp0, (parts0,), sums_a0 = exit_pass(
        me1, dq0, dkv0, got0, tables, xs0, gathered[0], k_rows, vecs[0], scaled0, heads, True, (mix1,)
    )
    parts0 = [lax.psum_scatter(parts0, "tensor", scatter_dimension=0, tiled=True)[0]]
    rows0 = extra_rows(sums_a0, sums_b0, token_sum0[0])
    mix_g0 = mix_back(first0, gp0, mixed0, gs, rows0, 300)
    up_g0, rest_g0 = after((up_g0, rest_g0), gp0)
    mix0 = mix_out(scatter_weights(mix_g0, False))
    up_s0 = scatter_weights(up_g0, False)
    rest_s0 = scatter_weights(rest_g0, True)
    feed0 = jnp.concatenate([up_s0, rest_s0], axis=0)
    mix1 = mix_out(mix1)
    (input_grad,) = turn(me1, parts0, grad, sent0)
    weight_out = []
    for feed_s, mix_s in ((feed_out(feed0), mix0), (feed_out(feed1), mix1)):
        weight_out.append((mix_s[0], mix_s[1], mix_s[2], feed_s[0], feed_s[1], feed_s[2]))

    sums = jnp.stack([mix0[3], mix1[3]], axis=1)
    if n & (n - 1):
        total = lax.psum_scatter(sums, "tensor", scatter_dimension=0, tiled=False)
    else:
        total = sums
        while total.shape[0] > 1:
            step = total.shape[0] // 2
            halves = total.reshape((2, step) + total.shape[1:])
            mine = (me // step) & 1
            send = lax.dynamic_index_in_dim(halves, 1 - mine, 0, keepdims=False)
            keep = lax.dynamic_index_in_dim(halves, mine, 0, keepdims=False)
            total = keep + lax.ppermute(send, "tensor", [(s, s ^ step) for s in range(n)])
        total = total[0]
    gains_out = total[:, :2].transpose(0, 2, 1)
    shifts_out = jnp.stack([total[:, 2], total[:, 3], total[:, 4], total[:, 4]], axis=-1)
    outs = [jnp.stack([weight_out[l][j] for l in range(LAYERS)]) for j in range(6)]
    shape = (rows, 1, own_count, width)
    return (block_output.reshape(shape), input_grad.reshape(shape), *outs, gains_out, shifts_out)


def solution(mesh):
    in_specs = (
        P("dp", "ctx", "tensor", None),
        P("dp", None),
        P(None, ("dp", "ctx"), "tensor"),
        P(None, ("tensor", "dp", "ctx")),
        P(None, ("tensor", "dp", "ctx"), None),
        P(None, ("dp", "ctx"), "tensor"),
        P(None, ("tensor", "dp", "ctx")),
        P(None, ("tensor", "dp", "ctx"), None),
        P(),
        P(),
        P("dp", "ctx", "tensor", None),
    )
    out_specs = (
        P("dp", "ctx", "tensor", None),
        P("dp", "ctx", "tensor", None),
        P(None, ("dp", "ctx"), "tensor"),
        P(None, ("tensor", "dp", "ctx")),
        P(None, ("tensor", "dp", "ctx"), None),
        P(None, ("dp", "ctx"), "tensor"),
        P(None, ("tensor", "dp", "ctx")),
        P(None, ("tensor", "dp", "ctx"), None),
        P(None, ("tensor", "dp", "ctx"), None),
        P(None, ("tensor", "dp", "ctx"), None),
    )
    return jax.shard_map(shards, mesh=mesh, in_specs=in_specs, out_specs=out_specs, check_vma=False)
```

```python
from functools import partial

import jax
import jax.numpy as jnp
from jax import lax
from jax.experimental import pallas as pl
from jax.experimental.pallas import tpu as pltpu
from jax.sharding import PartitionSpec as P

HEAD_DIM = 64
ROTARY = 16
LAYERS = 2
EPSILON = 1e-05
MASKED = -1e30
LANES = 128
SCALE = HEAD_DIM ** (-0.5)
FAR = 1 << 24
BF = jnp.bfloat16
F32 = jnp.float32
NT = (((1,), (1,)), ((), ()))


def dot(a, b):
    return jnp.dot(a, b, preferred_element_type=F32)


def dot_nt(a, b):
    return lax.dot_general(a, b, NT, preferred_element_type=F32)


def cost(micros):
    return pl.CostEstimate(
        flops=int(micros * 1.1e9), transcendentals=0, bytes_accessed=int(micros * 3.6e6)
    )


def params(mib=56):
    return pltpu.CompilerParams(vmem_limit_bytes=mib << 20)


def z_gather(own):
    n = lax.axis_size("tensor")
    return [own] + [
        lax.ppermute(own, "tensor", [(s, (s - c) % n) for s in range(n)]) for c in range(1, n)
    ]


def z_scatter(parts):
    n = lax.axis_size("tensor")
    return [parts[0]] + [
        lax.ppermute(parts[c], "tensor", [(s, (s + c) % n) for s in range(n)]) for c in range(1, n)
    ]


def after(value, *needed):
    return lax.optimization_barrier((value,) + needed)[0]


def bits_of(axis):
    return lax.axis_size(axis).bit_length() - 1


def power_of_two():
    sizes = [lax.axis_size(axis) for axis in ("tensor", "dp", "ctx")]
    return sizes[1] > 1 and all(size & (size - 1) == 0 for size in sizes)


def flip(send, step):
    axis, bit = step
    return lax.ppermute(send, axis, [(s, s ^ (1 << bit)) for s in range(lax.axis_size(axis))])


class Scatter:
    def __init__(self, value, first_y, axes=("dp", "ctx"), wire=BF):
        self.labels = [(axis, b) for axis in axes for b in reversed(range(bits_of(axis)))]
        y_steps = [("dp", b) for b in range(1, bits_of("dp"))]
        x_steps = [("ctx", b) for b in range(bits_of("ctx"))]
        self.order = [("tensor", b) for b in range(bits_of("tensor"))] if "tensor" in axes else []
        self.order += [("dp", 0)] + (y_steps + x_steps if first_y else x_steps + y_steps)
        if not isinstance(value, tuple):
            value = value.reshape((2,) * len(self.labels) + value.shape[len(axes) - 1 :])
        self.value, self.wire = value, wire

    def send(self):
        self.step = self.order.pop(0)
        axis, bit = self.step
        dim = self.labels.index(self.step)
        self.labels.pop(dim)
        if isinstance(self.value, tuple):
            lead = (2,) * len(self.labels)
            out, self.keep = (v.reshape(lead + v.shape[1:]) for v in self.value)
            return out
        mine = (lax.axis_index(axis) >> bit) & 1
        self.keep = lax.dynamic_index_in_dim(self.value, mine, dim, keepdims=False)
        out = lax.dynamic_index_in_dim(self.value, 1 - mine, dim, keepdims=False)
        return out.astype(self.wire)

    def receive(self, got):
        self.value = self.keep + got.astype(F32)


def advance(streams, *needed):
    streams = [stream for stream in streams if stream.order]
    sends = lax.optimization_barrier(tuple(stream.send() for stream in streams) + needed)
    gots = [flip(send, stream.step) for send, stream in zip(sends, streams)]
    for stream, got in zip(streams, gots):
        stream.receive(got)


def rotated(tile, cosine, sine_a, sine_b):
    return tile * cosine + pltpu.roll(tile, LANES - 8, 1) * sine_a + pltpu.roll(tile, 8, 1) * sine_b


def unrotated(tile, cosine, sine_a, sine_b):
    return tile * cosine - pltpu.roll(tile, LANES - 8, 1) * sine_a - pltpu.roll(tile, 8, 1) * sine_b


def unit_of(x):
    values = x.astype(F32)
    centre = values - jnp.mean(values, axis=-1, keepdims=True)
    inverse = lax.rsqrt(jnp.mean(centre * centre, axis=-1, keepdims=True) + EPSILON)
    return centre * inverse


def gathered_row(tail_ref, row, own):
    shards = tail_ref.shape[0]
    return jnp.concatenate(
        [tail_ref[s].astype(F32)[row : row + 1, :own] for s in range(shards)], axis=1
    )


def mix_kernel(n, heads, own, *refs):
    chunk_refs = refs[:n]
    mix_ref, tail_ref, vec_ref, cos_ref, sa_ref, sb_ref = refs[n : n + 6]
    xs_ref, first_ref, q_ref, kv_ref, bias_s = refs[-5:]
    load_chunk(chunk_refs, xs_ref.at[0])
    width = xs_ref.shape[-1]

    @pl.when(pl.program_id(0) == 0)
    def _():
        raw = gathered_row(tail_ref, 1, own)
        size = 3 * HEAD_DIM
        pieces = [raw[:, h * size + HEAD_DIM : (h + 1) * size] for h in range(heads)]
        blank = jnp.zeros((1, HEAD_DIM), F32)
        for h in range(heads):
            pieces += [raw[:, h * size : h * size + HEAD_DIM], blank]
        bias_s[...] = jnp.concatenate(pieces, axis=1)

    first = (unit_of(xs_ref[0]) * vec_ref[0:1] + vec_ref[2:3]).astype(BF)
    first_ref[0] = first
    proj = dot(first, mix_ref[...].reshape(width, -1)[:, : 2 * heads * LANES]) + bias_s[...]
    cosine, sine_a, sine_b = cos_ref[0], sa_ref[0], sb_ref[0]
    for h in range(heads):
        cols = slice(h * LANES, (h + 1) * LANES)
        kv_ref[0, :, cols] = rotated(proj[:, cols], cosine, sine_a, sine_b).astype(BF)
        qcols = slice((heads + h) * LANES, (heads + h + 1) * LANES)
        q_ref[0, :, cols] = (rotated(proj[:, qcols], cosine, sine_a, sine_b) * SCALE).astype(BF)


def store_chunk(refs, value):
    for j, ref in enumerate(refs):

        @pl.when(pl.program_id(0) == j)
        def _(ref=ref):
            ref[...] = value


def load_chunk(refs, held):
    for j, ref in enumerate(refs):

        @pl.when(pl.program_id(0) == j)
        def _(ref=ref):
            held[...] = ref[...]


def feed_kernel(own, *refs):
    x_ref, up_ref, down_ref, tail_ref, vec_ref, second_ref, active_ref, slope_ref = refs[:8]
    part_refs, bias_s = refs[8:-1], refs[-1]

    @pl.when(pl.program_id(0) == 0)
    def _():
        bias_s[...] = gathered_row(tail_ref, 0, own)

    width = x_ref.shape[-1]
    second = (unit_of(x_ref[0]) * vec_ref[1:2] + vec_ref[3:4]).astype(BF)
    second_ref[0] = second
    upw = up_ref[...].reshape(width, -1)
    hidden = dot(second, upw) + bias_s[...]
    half = 0.5 * (1.0 + lax.erf(hidden * (0.5**0.5)))
    active = (hidden * half).astype(BF)
    active_ref[0] = active
    bell = jnp.exp(hidden * hidden * -0.5) * 0.3989422804014327
    slope_ref[0] = (half + hidden * bell).astype(BF)
    store_chunk(part_refs, dot(active, down_ref[...].reshape(-1, width)).astype(BF))


def chunk_specs(n, tokens, gathered, k):
    shards, _, ff = gathered.shape
    token = lambda w: pl.BlockSpec((1, tokens, w), lambda c: (c, 0, 0))
    whole = lambda a: pl.BlockSpec(a.shape, lambda c: (0,) * a.ndim)
    weight = lambda j: pl.BlockSpec((shards, k, ff), lambda c: (0, j, 0))
    out = lambda w: jax.ShapeDtypeStruct((n, tokens, w), BF)
    return token, whole, weight, out


def mix_pass(tokens, chunks, place, n, gathered, k, own, vec, tables, heads, held=()):
    width = chunks[0].shape[1]
    count = len(chunks)
    wide = heads * LANES
    shards, _, ff = gathered.shape
    whole = lambda a: pl.BlockSpec(a.shape, lambda c: (0,) * a.ndim)
    token = lambda w: pl.BlockSpec((1, tokens, w), lambda c: (place + c, 0, 0))
    weight = pl.BlockSpec((shards, k, ff), lambda c: (0, 2, 0))
    tail = pl.BlockSpec((shards, 8, ff), lambda c: (0, 3 * k // 8, 0))
    out = lambda m, w: jax.ShapeDtypeStruct((m, tokens, w), BF)
    first_held = count + 6
    return pl.pallas_call(
        partial(mix_kernel, count, heads, own),
        grid=(count,),
        in_specs=[pl.BlockSpec((tokens, width), lambda c: (0, 0))] * count
        + [weight, tail, whole(vec)]
        + [token(LANES)] * 3
        + [pl.BlockSpec(memory_space=pl.ANY)] * len(held),
        out_specs=[token(width), token(width), token(wide)]
        + [pl.BlockSpec((1, tokens, wide), lambda c: (c, 0, 0))],
        out_shape=[out(n, width), out(n, width), out(n, wide), out(count, wide)],
        input_output_aliases={first_held + i: i for i in range(len(held))},
        scratch_shapes=[pltpu.VMEM((1, 2 * wide), F32)],
        compiler_params=params(),
        cost_estimate=cost(12),
        name="mix_pass",
    )(*chunks, gathered, gathered, vec, *tables, *held)


def feed_pass(xs, gathered, k, own, vec):
    n, tokens, width = xs.shape
    ff = gathered.shape[2]
    token, whole, weight, out = chunk_specs(n, tokens, gathered, k)
    second, active, slope, *parts = pl.pallas_call(
        partial(feed_kernel, own),
        grid=(n,),
        in_specs=[token(width), weight(0), weight(1)]
        + [pl.BlockSpec((gathered.shape[0], 8, ff), lambda c: (0, 3 * k // 8, 0)), whole(vec)],
        out_specs=[token(width), token(ff), token(ff)]
        + [pl.BlockSpec((tokens, width), lambda c: (0, 0))] * n,
        out_shape=[out(width), out(ff), out(ff)]
        + [jax.ShapeDtypeStruct((tokens, width), BF)] * n,
        scratch_shapes=[pltpu.VMEM((1, ff), F32)],
        compiler_params=params(),
        cost_estimate=cost(20),
        name="feed_pass",
    )(xs, gathered, gathered, gathered, vec)
    return second, active, slope, parts


def middle_kernel(n, me_ref, dense_ref, grads_ref, *refs):
    mixed_refs, part_refs = refs[:n], refs[n : 2 * n]
    do_refs, out_refs = refs[2 * n : 3 * n], refs[3 * n :]
    for c in range(n):
        total = dot(mixed_refs[c][...], dense_ref[...]) + part_refs[c][...].astype(F32)
        out_refs[c][...] = total.astype(BF)
        grad = grads_ref[lax.rem(me_ref[0] + c, n)]
        do_refs[c][...] = dot_nt(grad, dense_ref[...]).astype(BF)


def middle(me1, mixed, dense_w, parts, grads):
    n = len(parts)
    vmem = pl.BlockSpec(memory_space=pltpu.VMEM)
    outs = pl.pallas_call(
        partial(middle_kernel, n),
        in_specs=[pl.BlockSpec(memory_space=pltpu.SMEM)] + [vmem] * (2 + 2 * n),
        out_specs=[vmem] * (2 * n),
        out_shape=[jax.ShapeDtypeStruct(mixed[0].shape, BF)] * n
        + [jax.ShapeDtypeStruct(parts[0].shape, BF)] * n,
        compiler_params=params(),
        cost_estimate=cost(4),
        name="middle",
    )(me1, dense_w, grads, *mixed, *parts)
    return outs[:n], outs[n:]


def load_pairs(kv_refs, kv_s):
    place = 0
    for ref in kv_refs:
        for c in range(ref.shape[0]):
            kv_s[place] = ref[c, 0]
            place += 1


def each_block(plan_ref, row, c, blocks, take):
    start = c * (blocks + 1)
    count = plan_ref[row, start]

    def pair(t, _):
        take([plan_ref[row, start + 1 + 2 * t], plan_ref[row, start + 2 + 2 * t]])
        return 0

    lax.fori_loop(0, count // 2, pair, 0)

    @pl.when(count % 2 == 1)
    def _():
        take([plan_ref[row, start + count]])


def allowed_pairs(base_ref, begin_ref, kb, c, n, shape):
    key_slot = base_ref[n + kb] + lax.broadcasted_iota(jnp.int32, shape, 0)
    query_slot = base_ref[c] + lax.broadcasted_iota(jnp.int32, shape, 1)
    return (key_slot >= begin_ref[0, c]) & (key_slot <= query_slot)


def attend_kernel(heads, extras, groups, need_ref, base_ref, begin_ref, q_ref, *refs):
    kv_refs = refs[:groups]
    n, _, count, _ = q_ref.shape
    mixed_refs = refs[groups : groups + n]
    ot_ref, lse_ref, kv_s, vt_s, top_s, total_s, acc_s, mixed_s = refs[groups + n :]
    blocks = n * (1 + extras)
    row = pl.program_id(0)
    load_pairs(kv_refs, kv_s)

    def turn(kb, _):
        for h in range(heads):
            tile = kv_s[kb, :, h * LANES : (h + 1) * LANES].astype(F32)
            vt_s[kb, h] = tile.T[HEAD_DIM:].astype(BF)
        return 0

    lax.fori_loop(0, blocks, turn, 0)

    def per_query(c, _):
        top_s[...] = jnp.full(top_s.shape, MASKED, F32)
        total_s[...] = jnp.zeros(total_s.shape, F32)
        acc_s[...] = jnp.zeros(acc_s.shape, F32)

        def take(kbs):
            column = lambda h: slice(h * LANES, (h + 1) * LANES)
            held = [
                [dot_nt(kv_s[kb, :, column(h)], q_ref[c, 0, :, column(h)]) for h in range(heads)]
                for kb in kbs
            ]
            masks = [allowed_pairs(base_ref, begin_ref, kb, c, n, (count, count)) for kb in kbs]
            low, fades = [], []
            for h in range(heads):
                scores = [jnp.where(mask, own[h], MASKED) for mask, own in zip(masks, held)]
                old = top_s[h]
                new = old
                for score in scores:
                    new = jnp.maximum(new, jnp.max(score, axis=0, keepdims=True))
                fade = jnp.exp(old - new)
                total = total_s[h] * fade
                weights = []
                for score in scores:
                    weight = jnp.exp(score - new)
                    total = total + jnp.sum(weight, axis=0, keepdims=True)
                    weights.append(weight.astype(BF))
                top_s[h] = new
                total_s[h] = total
                low.append(weights)
                fades.append(fade)
            for h in range(heads):
                acc = acc_s[h] * fades[h]
                for kb, weight in zip(kbs, low[h]):
                    acc = acc + dot(vt_s[kb, h], weight)
                acc_s[h] = acc

        each_block(need_ref, row, c, blocks, take)
        outs = []
        for h in range(heads):
            total = total_s[h]
            outs.append(acc_s[h] / total)
            lse_ref[0, c, h : h + 1] = top_s[h] + jnp.log(total)
        whole = jnp.concatenate(outs, axis=0)
        ot_ref[0, c] = whole
        mixed_s[c] = whole.T.astype(BF)
        return 0

    lax.fori_loop(0, n, per_query, 0)
    for c in range(n):
        mixed_refs[c][0] = mixed_s[c]


def attention_specs(q, kvs):
    n, rows, count, wide = q.shape
    smem = pl.BlockSpec(memory_space=pltpu.SMEM)
    begin = pl.BlockSpec((1, n, 1, count), lambda r: (r, 0, 0, 0))
    tokens = lambda a: pl.BlockSpec((a.shape[0], 1, count, wide), lambda r: (0, r, 0, 0))
    flat = [a for group in kvs for a in group]
    return n, rows, count, wide, smem, begin, tokens, flat


def attend(need, base, begin, q, kvs, heads):
    extras = len(kvs) - 1
    n, rows, count, wide, smem, begin_spec, tokens, flat = attention_specs(q, kvs)
    blocks = n * (1 + extras)
    narrow = heads * HEAD_DIM
    outs = pl.pallas_call(
        partial(attend_kernel, heads, extras, len(flat)),
        grid=(rows,),
        in_specs=[smem, smem, begin_spec, tokens(q)] + [tokens(a) for a in flat],
        out_specs=[pl.BlockSpec((1, count, narrow), lambda r: (r, 0, 0))] * n
        + [
            pl.BlockSpec((1, n, narrow, count), lambda r: (r, 0, 0, 0)),
            pl.BlockSpec((1, n, heads, count), lambda r: (r, 0, 0, 0)),
        ],
        out_shape=[jax.ShapeDtypeStruct((rows, count, narrow), BF)] * n
        + [
            jax.ShapeDtypeStruct((rows, n, narrow, count), F32),
            jax.ShapeDtypeStruct((rows, n, heads, count), F32),
        ],
        scratch_shapes=[
            pltpu.VMEM((blocks, count, wide), BF),
            pltpu.VMEM((blocks, heads, HEAD_DIM, count), BF),
            pltpu.VMEM((heads, 1, count), F32),
            pltpu.VMEM((heads, 1, count), F32),
            pltpu.VMEM((heads, HEAD_DIM, count), F32),
            pltpu.VMEM((n, count, narrow), BF),
        ],
        compiler_params=params(),
        cost_estimate=cost(400),
        name="attend",
    )(need, base, begin, q, *flat)
    return [a.reshape(rows * count, narrow) for a in outs[:n]], outs[n], outs[n + 1]


def attend_back_kernel(heads, extras, groups, need_ref, base_ref, begin_ref, q_ref, *refs):
    n, _, count, _ = q_ref.shape
    do_refs, lse_ref, ot_ref = refs[:n], refs[n], refs[n + 1]
    kv_refs = refs[n + 2 : n + 2 + groups]
    dq_ref = refs[n + 2 + groups]
    dkv_refs = refs[n + 3 + groups : n + 4 + groups + extras]
    kv_s, kt_s, dkv_s, dqt_s, delta_s, do_s, narrow_s = refs[n + 4 + groups + extras :]
    blocks = n * (1 + extras)
    row = pl.program_id(0)
    load_pairs(kv_refs, kv_s)
    for c in range(n):
        narrow_s[c] = do_refs[c][0]

    def turn(kb, _):
        for h in range(heads):
            tile = kv_s[kb, :, h * LANES : (h + 1) * LANES].astype(F32)
            kt_s[kb, h] = tile.T[:HEAD_DIM].astype(BF)
        dkv_s[kb] = jnp.zeros(dkv_s.shape[1:], F32)
        return 0

    lax.fori_loop(0, blocks, turn, 0)

    def per_query(c, _):
        dqt_s[...] = jnp.zeros(dqt_s.shape, F32)
        for h in range(heads):
            cols = slice(h * LANES, (h + 1) * LANES)
            grad = narrow_s[c, :, h * HEAD_DIM : (h + 1) * HEAD_DIM].astype(F32)
            grad = jnp.concatenate([jnp.zeros((count, HEAD_DIM), F32), grad], axis=1)
            do_s[:, cols] = grad.astype(BF)
            dot_t = grad.T[HEAD_DIM:]
            out_t = ot_ref[0, c, h * HEAD_DIM : (h + 1) * HEAD_DIM]
            delta_s[h] = jnp.sum(dot_t * out_t, axis=0, keepdims=True)

        def take(kbs):
            column = lambda h: slice(h * LANES, (h + 1) * LANES)
            queries = [q_ref[c, 0, :, column(h)] for h in range(heads)]
            grads = [do_s[:, column(h)] for h in range(heads)]
            held = []
            for kb in kbs:
                pairs = [kv_s[kb, :, column(h)] for h in range(heads)]
                held.append(
                    [(dot_nt(pairs[h], queries[h]), dot_nt(pairs[h], grads[h])) for h in range(heads)]
                )
            low = []
            for kb, own in zip(kbs, held):
                allowed = allowed_pairs(base_ref, begin_ref, kb, c, n, (count, count))
                for h in range(heads):
                    scores = jnp.where(allowed, own[h][0], MASKED)
                    probs = jnp.exp(scores - lse_ref[0, c, h : h + 1])
                    steps = probs * (own[h][1] - delta_s[h])
                    low.append((steps.astype(BF), probs.astype(BF)))
            for i, kb in enumerate(kbs):
                for h in range(heads):
                    steps, probs = low[i * heads + h]
                    dqt_s[h] += dot(kt_s[kb, h], steps)
                    dkv_s[kb, :, column(h)] += dot(steps, queries[h]) + dot(probs, grads[h])

        each_block(need_ref, row, c, blocks, take)
        for h in range(heads):
            tile = jnp.concatenate([dqt_s[h], jnp.zeros((HEAD_DIM, count), F32)], axis=0)
            dq_ref[c, 0, :, h * LANES : (h + 1) * LANES] = tile.T * SCALE
        return 0

    lax.fori_loop(0, n, per_query, 0)
    for e, ref in enumerate(dkv_refs):
        for c in range(n):
            ref[c, 0] = dkv_s[e * n + c].astype(ref.dtype)


def attend_back(need, base, begin, q, do, lse, ot, kvs, heads):
    extras = len(kvs) - 1
    n, rows, count, wide, smem, begin_spec, tokens, flat = attention_specs(q, kvs)
    blocks = n * (1 + extras)
    narrow = heads * HEAD_DIM
    return pl.pallas_call(
        partial(attend_back_kernel, heads, extras, len(flat)),
        grid=(rows,),
        in_specs=[smem, smem, begin_spec, tokens(q)]
        + [pl.BlockSpec((1, count, narrow), lambda r: (r, 0, 0))] * n
        + [
            pl.BlockSpec((1, n, heads, count), lambda r: (r, 0, 0, 0)),
            pl.BlockSpec((1, n, narrow, count), lambda r: (r, 0, 0, 0)),
        ]
        + [tokens(a) for a in flat],
        out_specs=[tokens(q)] * (2 + extras),
        out_shape=[jax.ShapeDtypeStruct(q.shape, F32)] * 2
        + [jax.ShapeDtypeStruct(q.shape, BF)] * extras,
        scratch_shapes=[
            pltpu.VMEM((blocks, count, wide), BF),
            pltpu.VMEM((blocks, heads, HEAD_DIM, count), BF),
            pltpu.VMEM((blocks, count, wide), F32),
            pltpu.VMEM((heads, HEAD_DIM, count), F32),
            pltpu.VMEM((heads, 1, count), F32),
            pltpu.VMEM((count, wide), BF),
            pltpu.VMEM((n, count, narrow), BF),
        ],
        compiler_params=params(),
        cost_estimate=cost(40),
        name="attend_back",
    )(need, base, begin, q, *[a.reshape(rows, count, narrow) for a in do], lse, ot, *flat)


TN = (((0,), (0,)), ((), ()))


def dot_tn(a, b):
    return lax.dot_general(a, b, TN, preferred_element_type=F32)


def half_shard(place, inner, bit):
    return (place // inner * 2 + bit) * inner + place % inner


def store_shards(refs, core_ref, shards, inner, block):
    if len(refs) == 1:
        for s in range(shards):
            refs[0][s] = block(s)
        return
    mine = core_ref[0]
    for place in range(shards // 2):
        refs[0][place] = block(half_shard(place, inner, 1 - mine))
        refs[1][place] = block(half_shard(place, inner, mine))


def row_block(ref, s, size):
    start = s * size if isinstance(s, int) else pl.multiple_of(s * size, 8)
    return ref[pl.ds(start, size)]


def feed_back_kernel(n, gates, inner, split, core_ref, *refs):
    grad_refs = refs[:n]
    x_ref, slope_ref, second_ref, active_ref, up_ref, down_ref, vec_ref = refs[n : n + 7]
    refs = refs[n + 7 + gates :]
    scaled_ref, sums_ref, outs = refs[0], refs[1], refs[2:-4]
    up_s, down_s, grad_s, tail_s = refs[-4:]
    width = x_ref.shape[-1]
    last = pl.program_id(0) == pl.num_programs(0) - 1

    @pl.when(pl.program_id(0) == 0)
    def _():
        sums_ref[...] = jnp.zeros(sums_ref.shape, F32)
        up_s[...] = jnp.zeros(up_s.shape, F32)
        down_s[...] = jnp.zeros(down_s.shape, F32)

    load_chunk(grad_refs, grad_s)
    down = down_ref[...].reshape(-1, width)
    grad = grad_s[...]
    grad_hidden = (dot_nt(grad, down) * slope_ref[0].astype(F32)).astype(BF)
    grad_second = dot_nt(grad_hidden, up_ref[...].reshape(width, -1))
    unit = unit_of(x_ref[0])
    sums_ref[0:1] += jnp.sum(grad_second * unit, axis=0, keepdims=True)
    sums_ref[1:2] += jnp.sum(grad_second, axis=0, keepdims=True)
    sums_ref[2:3] += jnp.sum(grad_hidden.astype(F32), axis=0, keepdims=True)
    scaled_ref[0] = grad_second * vec_ref[1:2]
    down_s[...] += dot_tn(active_ref[0], grad)
    up_s[...] += dot_tn(second_ref[0], grad_hidden)

    @pl.when(last)
    def _():
        shards, k = up_ref.shape[:2]
        f = down_s.shape[0] // shards
        own = up_s.shape[1] // shards
        pad = jnp.zeros((8, width - own), F32)
        for s in range(shards):
            tail = jnp.broadcast_to(sums_ref[2:3, s * own : (s + 1) * own], (8, own))
            tail_s[s] = jnp.concatenate([tail, pad], axis=1)
        up_block = lambda s: row_block(up_s, s, k).astype(BF)
        rest_block = lambda s: jnp.concatenate(
            [row_block(down_s, s, f), tail_s[s]], axis=0
        ).astype(BF)
        if split:
            store_shards(outs[:2], core_ref, shards, inner, up_block)
            store_shards(outs[2:], core_ref, shards, inner, rest_block)
        else:
            store_shards(
                outs, core_ref, shards, inner,
                lambda s: jnp.concatenate([up_block(s), rest_block(s)], axis=0),
            )


def feed_back(core1, gs, xs, slope, second, active, gathered, k, vec, inner, split, gates=()):
    n, tokens, width = xs.shape
    shards, _, ff = gathered.shape
    f = ff // shards
    token, whole, weight, _ = chunk_specs(n, tokens, gathered, k)
    fixed = pl.BlockSpec((8, width), lambda c: (0, 0))
    grads = [(shards, k + f + 8, width)]
    if split:
        grads = [(shards // 2, k, width)] * 2 + [(shards // 2, f + 8, width)] * 2
    return pl.pallas_call(
        partial(feed_back_kernel, n, len(gates), inner, split),
        grid=(n,),
        in_specs=[pl.BlockSpec(memory_space=pltpu.SMEM)]
        + [whole(gs[0])] * n
        + [token(width), token(ff), token(width), token(ff), weight(0), weight(1), fixed]
        + [pl.BlockSpec(memory_space=pl.ANY)] * len(gates),
        out_specs=[token(width), fixed] + [pl.BlockSpec(g, lambda c: (0, 0, 0)) for g in grads],
        scratch_shapes=[
            pltpu.VMEM((width, ff), F32),
            pltpu.VMEM((ff, width), F32),
            pltpu.VMEM((tokens, width), BF),
            pltpu.VMEM((shards, 8, width), F32),
        ],
        out_shape=[
            jax.ShapeDtypeStruct((n, tokens, width), F32),
            jax.ShapeDtypeStruct((8, width), F32),
        ]
        + [jax.ShapeDtypeStruct(g, BF) for g in grads],
        compiler_params=params(),
        cost_estimate=cost(12),
        name="feed_back",
    )(core1, *gs, xs, slope, second, active, gathered, gathered, vec, *gates)


def mix_back_kernel(n, inner, outs, core_ref, *refs):
    first_ref, gp_ref, bias_ref = refs[:3]
    mixed_refs, grad_refs = refs[3 : 3 + n], refs[3 + n : 3 + 2 * n]
    grads_refs = refs[-4 - outs : -4]
    mix_s, dense_s, mixed_s, grad_s = refs[-4:]
    last = pl.program_id(0) == pl.num_programs(0) - 1

    @pl.when(pl.program_id(0) == 0)
    def _():
        mix_s[...] = jnp.zeros(mix_s.shape, F32)
        dense_s[...] = jnp.zeros(dense_s.shape, F32)

    load_chunk(grad_refs, grad_s)
    load_chunk(mixed_refs, mixed_s)
    mix_s[...] += dot_tn(first_ref[0], gp_ref[0])
    dense_s[...] += dot_tn(mixed_s[...], grad_s[...])

    @pl.when(last)
    def _():
        shards = bias_ref.shape[0]
        k = mix_s.shape[0] // shards
        d = dense_s.shape[0] // shards

        def block(s):
            rows = [row_block(mix_s, s, k), row_block(dense_s, s, d), bias_ref[s]]
            return jnp.concatenate(rows, axis=0).astype(BF)

        store_shards(grads_refs, core_ref, shards, inner, block)


def mix_back(core1, first, gp, mixed, gs, bias, inner, split, micros, gates=()):
    n, tokens, width = first.shape
    shards = bias.shape[0]
    narrow = mixed[0].shape[-1]
    token = lambda w: pl.BlockSpec((1, tokens, w), lambda c: (c, 0, 0))
    whole = lambda a: pl.BlockSpec(a.shape, lambda c: (0,) * a.ndim)
    count = 2 if split else 1
    grads = (shards // count, width // shards + narrow // shards + 8, width)
    return pl.pallas_call(
        partial(mix_back_kernel, n, inner, count),
        grid=(n,),
        in_specs=[pl.BlockSpec(memory_space=pltpu.SMEM), token(width), token(gp.shape[-1]), whole(bias)]
        + [whole(mixed[0])] * n
        + [whole(gs[0])] * n
        + [pl.BlockSpec(memory_space=pl.ANY)] * len(gates),
        out_specs=[pl.BlockSpec(grads, lambda c: (0, 0, 0))] * count,
        scratch_shapes=[
            pltpu.VMEM((width, gp.shape[-1]), F32),
            pltpu.VMEM((narrow, width), F32),
            pltpu.VMEM((tokens, narrow), BF),
            pltpu.VMEM((tokens, width), BF),
        ],
        out_shape=[jax.ShapeDtypeStruct(grads, BF)] * count,
        compiler_params=params(),
        cost_estimate=cost(micros),
        name="mix_back",
    )(core1, first, gp, bias, *mixed, *gs, *gates)


def join_kernel(n, me_ref, dense_ref, residual_ref, vec_ref, *refs):
    mixed_refs, share_refs, out_ref, sent_ref = refs[:n], refs[n : 2 * n], refs[2 * n], refs[2 * n + 1]
    total = residual_ref[...] + vec_ref[4:5] + vec_ref[5:6]
    for c in range(n):
        rows = dense_ref[:, (n - c) % n]
        rows = rows.reshape(-1, rows.shape[-1])
        total = total + share_refs[c][...].astype(F32) + dot(mixed_refs[c][...], rows)
    out_ref[...] = total
    sent_ref[...] = total.astype(BF)


def join(me1, mixed, dense_all, shares, residual, vec):
    shape = residual.shape
    vmem = pl.BlockSpec(memory_space=pltpu.VMEM)
    return pl.pallas_call(
        partial(join_kernel, len(shares)),
        in_specs=[pl.BlockSpec(memory_space=pltpu.SMEM)] + [vmem] * (3 + 2 * len(shares)),
        out_specs=[vmem, vmem],
        out_shape=[jax.ShapeDtypeStruct(shape, F32), jax.ShapeDtypeStruct(shape, BF)],
        compiler_params=params(),
        cost_estimate=cost(3),
        name="join",
    )(me1, dense_all, residual, vec, *mixed, *shares)


def turn_kernel(n, gates, me_ref, *refs):
    summed = refs[0][...].astype(F32)
    for ref in refs[1:n]:
        summed = summed + ref[...].astype(F32)
    grad_ref, x_ref = refs[n : n + 2]
    refs = refs[n + 2 :]
    values = x_ref[...].astype(F32)
    centre = values - jnp.mean(values, axis=-1, keepdims=True)
    inverse = lax.rsqrt(jnp.mean(centre * centre, axis=-1, keepdims=True) + EPSILON)
    unit = centre * inverse
    mean_s = jnp.mean(summed, axis=-1, keepdims=True)
    mean_su = jnp.mean(summed * unit, axis=-1, keepdims=True)
    grad = grad_ref[...] + inverse * (summed - mean_s - unit * mean_su)
    if len(refs) == gates + 1:
        refs[-1][...] = grad
        return
    dense_ref, out_ref, sent_ref, sums_ref = refs[0], *refs[gates + 1 : gates + 4]
    piece_refs = refs[gates + 4 :]
    out_ref[...] = grad
    sent = grad.astype(BF)
    sent_ref[...] = sent
    for c, piece_ref in enumerate(piece_refs):
        rows = dense_ref[:, c]
        piece_ref[...] = dot_nt(sent, rows.reshape(-1, rows.shape[-1])).astype(BF)
    sums_ref[...] = jnp.broadcast_to(jnp.sum(grad, axis=0, keepdims=True), sums_ref.shape)


def turn(me1, parts, grad, x_own, dense_all=None, gates=()):
    shape = grad.shape
    outs = [jax.ShapeDtypeStruct(shape, F32)]
    vmem = pl.BlockSpec(memory_space=pltpu.VMEM)
    more = []
    if dense_all is not None:
        more = [dense_all]
        outs += [jax.ShapeDtypeStruct(shape, BF), jax.ShapeDtypeStruct((8, shape[1]), F32)]
        narrow = dense_all.shape[0] * dense_all.shape[2]
        outs += [jax.ShapeDtypeStruct((shape[0], narrow), BF)] * dense_all.shape[1]
    return pl.pallas_call(
        partial(turn_kernel, len(parts), len(gates)),
        in_specs=[pl.BlockSpec(memory_space=pltpu.SMEM)]
        + [vmem] * (len(parts) + 2 + len(more))
        + [pl.BlockSpec(memory_space=pl.ANY)] * len(gates),
        out_specs=[vmem] * len(outs),
        out_shape=outs,
        compiler_params=params(),
        cost_estimate=cost(3),
        name="turn",
    )(me1, *parts, grad, x_own, *more, *gates)


def exit_kernel(n, heads, extras, gates, inner, outs, halves, _, core_ref, dq_ref, dkv_ref, *refs):
    got_refs = refs[:extras]
    cos_ref, sa_ref, sb_ref, x_ref, mix_ref, vec_ref, scaled_ref = refs[extras : extras + 7]
    refs = refs[extras + 7 :]
    fold = halves > 0
    if fold:
        first_ref, mixed_refs, grad_refs = refs[0], refs[1 : 1 + n], refs[1 + n : 1 + 2 * n]
        refs = refs[1 + 2 * n :]
    refs = refs[gates:]
    gp_ref, sums_ref, part_refs = refs[0], refs[1], refs[2 : 2 + outs]
    grads_refs, scratch = refs[2 + outs : 2 + outs + halves], refs[2 + outs + halves :]
    width = x_ref.shape[-1]

    @pl.when(pl.program_id(0) == 0)
    def _():
        sums_ref[...] = jnp.zeros(sums_ref.shape, F32)
        if fold:
            scratch[0][...] = jnp.zeros(scratch[0].shape, F32)
            scratch[1][...] = jnp.zeros(scratch[1].shape, F32)

    cosine, sine_a, sine_b = cos_ref[0], sa_ref[0], sb_ref[0]
    for h in range(heads):
        cols = slice(h * LANES, (h + 1) * LANES)
        pair = dkv_ref[0, :, cols]
        for ref in got_refs:
            pair = pair + ref[0, :, cols].astype(F32)
        gp_ref[0, :, cols] = unrotated(pair, cosine, sine_a, sine_b).astype(BF)
        qcols = slice((heads + h) * LANES, (heads + h + 1) * LANES)
        gp_ref[0, :, qcols] = unrotated(dq_ref[0, :, cols], cosine, sine_a, sine_b).astype(BF)
    gp = gp_ref[0]
    grad_first = dot_nt(gp, mix_ref[...].reshape(width, -1))
    if fold:
        mix_s, dense_s, mixed_s, grad_s, tail_s = scratch
        load_chunk(grad_refs, grad_s)
        load_chunk(mixed_refs, mixed_s)
        mix_s[...] += dot_tn(first_ref[0], gp)
        dense_s[...] += dot_tn(mixed_s[...], grad_s[...])
    unit = unit_of(x_ref[0])
    sums_ref[0:1] += jnp.sum(grad_first * unit, axis=0, keepdims=True)
    sums_ref[1:2] += jnp.sum(grad_first, axis=0, keepdims=True)
    sums_ref[2:3] += jnp.sum(gp.astype(F32), axis=0, keepdims=True)
    part = (grad_first * vec_ref[0:1] + scaled_ref[0]).astype(BF)
    if outs == 1:
        part_refs[0][0] = part
    else:
        store_chunk(part_refs, part)
    if not fold:
        return

    @pl.when(pl.program_id(0) == pl.num_programs(0) - 1)
    def _():
        shards = mix_ref.shape[0]
        k = mix_s.shape[0] // shards
        d = dense_s.shape[0] // shards
        row = sums_ref[2:3]
        pieces = []
        for h in range(heads):
            query = (heads + h) * LANES
            pieces.append(row[:, query : query + HEAD_DIM])
            pieces.append(row[:, h * LANES : (h + 1) * LANES])
        raw = jnp.concatenate(pieces, axis=1)
        own = raw.shape[1] // shards
        pad = jnp.zeros((8, width - own), F32)
        for s in range(shards):
            tail = jnp.broadcast_to(raw[:, s * own : (s + 1) * own], (8, own))
            tail_s[s] = jnp.concatenate([tail, pad], axis=1)

        def block(s):
            rows = [row_block(mix_s, s, k), row_block(dense_s, s, d), tail_s[s]]
            return jnp.concatenate(rows, axis=0).astype(BF)

        store_shards(grads_refs, core_ref, shards, inner, block)


def exit_pass(
    me1, core1, dq, dkv, got, tables, xs, gathered, k, vec, scaled, heads, inner, halves=0,
    fold=(), gates=(),
):
    n, tokens, width = xs.shape
    shards, _, ff = gathered.shape
    wide = heads * LANES
    narrow = heads * HEAD_DIM
    token = lambda w: pl.BlockSpec((1, tokens, w), lambda c, s: (c, 0, 0))
    weight = lambda j: pl.BlockSpec((shards, k, ff), lambda c, s: (0, j, 0))
    whole = lambda a: pl.BlockSpec(a.shape, lambda c, s: (0,) * a.ndim)
    fixed = pl.BlockSpec((8, width), lambda c, s: (0, 0))
    flat = lambda a: a.reshape(n, tokens, wide)
    fold_specs, grad_specs, grad_shapes, scratch = [], [], [], []
    if halves:
        part_specs = [pl.BlockSpec((1, tokens, width), lambda c, s: ((s[0] + c) % n, 0, 0))]
        part_shapes = [jax.ShapeDtypeStruct((n, tokens, width), BF)]
        fold_specs = [token(width)] + [whole(a) for a in fold[1:]]
        grads = (shards // halves, width // shards + narrow // shards + 8, width)
        grad_specs = [pl.BlockSpec(grads, lambda c, s: (0, 0, 0))] * halves
        grad_shapes = [jax.ShapeDtypeStruct(grads, BF)] * halves
        scratch = [
            pltpu.VMEM((width, 2 * wide), F32),
            pltpu.VMEM((narrow, width), F32),
            pltpu.VMEM((tokens, narrow), BF),
            pltpu.VMEM((tokens, width), BF),
            pltpu.VMEM((shards, 8, width), F32),
        ]
    else:
        part_specs = [pl.BlockSpec((tokens, width), lambda c, s: (0, 0))] * n
        part_shapes = [jax.ShapeDtypeStruct((tokens, width), BF)] * n
    outs = len(part_specs)
    gp, sums, *rest = pl.pallas_call(
        partial(exit_kernel, n, heads, len(got), len(gates), inner, outs, halves),
        grid_spec=pltpu.PrefetchScalarGridSpec(
            num_scalar_prefetch=1,
            grid=(n,),
            in_specs=[pl.BlockSpec(memory_space=pltpu.SMEM)]
            + [token(wide)] * (2 + len(got))
            + [token(LANES)] * 3
            + [token(width), weight(2), fixed, token(width)]
            + fold_specs
            + [pl.BlockSpec(memory_space=pl.ANY)] * len(gates),
            out_specs=[token(2 * wide), fixed] + part_specs + grad_specs,
            scratch_shapes=scratch,
        ),
        out_shape=[
            jax.ShapeDtypeStruct((n, tokens, 2 * wide), BF),
            jax.ShapeDtypeStruct((8, width), F32),
        ]
        + part_shapes
        + grad_shapes,
        compiler_params=params(),
        cost_estimate=cost(100),
        name="exit_pass",
    )(
        me1, core1, flat(dq), flat(dkv), *[flat(a) for a in got], *tables, xs, gathered, vec,
        scaled, *fold, *gates,
    )
    return gp, rest[:outs], sums, tuple(rest[outs:])


def mix_columns(weight, heads):
    lead = weight.shape[:-1]
    split = weight.reshape(lead + (heads, 3, HEAD_DIM))
    pairs = split[..., 1:, :].reshape(lead + (heads * LANES,))
    query = jnp.concatenate([split[..., 0, :], jnp.zeros_like(split[..., 0, :])], axis=-1)
    return jnp.concatenate([pairs, query.reshape(lead + (heads * LANES,))], axis=-1)


def unmix_columns(grad, heads):
    lead = grad.shape[:-1]
    split = grad.reshape(lead + (2, heads, 2, HEAD_DIM))
    order = [split[..., 1, :, 0, :], split[..., 0, :, 0, :], split[..., 0, :, 1, :]]
    return jnp.stack(order, axis=-2).reshape(lead + (heads * 3 * HEAD_DIM,))


def pack_layer(mix_w, mix_b, dense_w, up_w, up_b, down_w, heads):
    width = up_w.shape[1]
    mix = mix_columns(mix_w, heads)
    wide = lambda v: jnp.pad(v, (0, width - v.shape[0]))[None]
    rows = [up_w, down_w, jnp.pad(mix, ((0, 0), (0, width - mix.shape[1])))]
    rows += [wide(up_b), wide(mix_b), jnp.zeros((6, width), up_w.dtype)]
    if dense_w is not None:
        rows += [dense_w, jnp.zeros((-dense_w.shape[0] % 8, width), up_w.dtype)]
    return jnp.concatenate(rows, axis=0)


def shards(
    block_input, seq_lengths, project_weight, project_bias, dense_weight, up_weight, up_bias,
    down_weight, norm_gains, shift_vectors, cotangent,
):
    rows, _, own_count, width = block_input.shape
    n = lax.axis_size("tensor")
    places = lax.axis_size("ctx")
    extras = places - 1
    place = lax.axis_index("ctx")
    me = lax.axis_index("tensor")
    me1 = me.reshape(1)
    core1 = (lax.axis_index("dp") & 1).reshape(1)
    split = power_of_two()
    block_len = own_count * n
    tokens = rows * own_count
    heads = project_weight.shape[2] // (3 * HEAD_DIM)
    wide = heads * LANES
    k_rows = up_weight.shape[1]
    d_rows = dense_weight.shape[1]
    f_own = up_bias.shape[1]
    m_own = project_bias.shape[1]
    shard_count = lax.axis_size("dp") * places

    ends = jnp.cumsum(seq_lengths, axis=1)
    order = (me + jnp.arange(n, dtype=jnp.int32)) % n
    query_base = place * block_len + order * own_count
    slots = query_base[:, None] + jnp.arange(own_count, dtype=jnp.int32)[None]
    passed = (ends[:, None, None, :] <= slots[None, :, :, None]).astype(jnp.int32)
    begin = jnp.sum(passed * seq_lengths[:, None, None, :], axis=3)
    position = (slots[None] - begin).transpose(1, 0, 2).reshape(-1)
    frequency = 1.0 / 10000.0 ** (jnp.arange(0, ROTARY, 2, dtype=F32) / ROTARY)
    angle = frequency[:, None] * position.astype(F32)[None, :]
    cosine, sine = lax.optimization_barrier((jnp.cos(angle), jnp.sin(angle)))
    cosine, sine = cosine.T, sine.T
    ones = jnp.ones((cosine.shape[0], LANES - ROTARY), F32)
    zero8 = jnp.zeros_like(sine)
    tables = (
        jnp.concatenate([cosine, cosine, ones], axis=1).reshape(n, tokens, LANES),
        jnp.concatenate([-sine, zero8, ones * 0.0], axis=1).reshape(n, tokens, LANES),
        jnp.concatenate([zero8, sine, ones * 0.0], axis=1).reshape(n, tokens, LANES),
    )
    key_base = jnp.concatenate(
        [
            jnp.where(place >= e, (place - e) * block_len + order * own_count, FAR)
            for e in range(places)
        ]
    )
    base = jnp.concatenate([query_base, key_base])
    need = (key_base[None, None, :] <= query_base[None, :, None] + own_count - 1) & (
        key_base[None, None, :] + own_count - 1 >= begin[:, :, :1]
    )
    need = need.astype(jnp.int32)
    rank = jnp.cumsum(need, axis=2) - need
    blocks = key_base.shape[0]
    spot = jnp.arange(blocks, dtype=jnp.int32)
    chosen = (rank[..., None] == spot) & (need[..., None] > 0)
    listed = jnp.sum(chosen * spot[:, None], axis=2)
    need = jnp.concatenate([jnp.sum(need, axis=2, keepdims=True), listed], axis=2)
    need = need.astype(jnp.int32).reshape(rows, -1)
    begin = begin.reshape(rows, n, 1, own_count)

    gains = norm_gains.astype(F32)
    shifts = shift_vectors.astype(F32)
    packed = [
        pack_layer(
            project_weight[l], project_bias[l], dense_weight[l] if l else None, up_weight[l],
            up_bias[l], down_weight[l], heads,
        )
        for l in range(LAYERS)
    ]
    flat = lambda a: a.reshape(n * tokens, -1)
    by_row = lambda a: a.reshape(n, rows, own_count, -1)
    stack = lambda chunks: jnp.stack(chunks)
    shift_to = lambda v, c: lax.ppermute(v, "tensor", [(s, (s + c) % n) for s in range(n)])
    sent = block_input[:, 0].reshape(tokens, width)
    sent0 = sent
    residual = sent.astype(F32)
    cot = cotangent[:, 0].reshape(tokens, width)

    spare = jnp.zeros((-d_rows % 8, width), BF)
    chunks0 = z_gather(jnp.concatenate([sent, dense_weight[0], spare], axis=0))
    gather_all = lambda v: lax.all_gather(v, ("dp", "ctx"), axis=0, tiled=False)
    gathered = [gather_all(packed[0])]
    gather_z = lambda v: lax.all_gather(v, "tensor", axis=0, tiled=False)
    vecs = [
        jnp.concatenate([gains[l].T, shifts[l].T, jnp.zeros((2, width), F32)], axis=0)
        for l in range(LAYERS)
    ]

    def mix_groups(chunks, l):
        cut = (n + 1) // 2
        tables_of = tables
        xs, first, q, kv_a = mix_pass(
            tokens, chunks[:cut], 0, n, gathered[l], k_rows, m_own, vecs[l], tables_of, heads
        )
        groups = [kv_a]
        if cut < n:
            chunks = chunks[:cut] + list(after(tuple(chunks[cut:]), kv_a))
            xs, first, q, kv_b = mix_pass(
                tokens, chunks[cut:], cut, n, gathered[l], k_rows, m_own, vecs[l], tables_of, heads,
                (xs, first, q),
            )
            groups.append(kv_b)
        groups = [a.reshape(a.shape[0], rows, own_count, wide) for a in groups]
        kvs = [groups] + [
            [lax.ppermute(a, "ctx", [(s, s + e) for s in range(places - e)]) for a in groups]
            for e in range(1, places)
        ]
        return xs, first, by_row(q), kvs, chunks

    chunks0[0] = after(chunks0[0], packed[1], need, base, begin)
    xs0, first0, q0, kvs0, chunks0 = mix_groups(chunks0, 0)
    dense_all = jnp.stack([chunk[tokens : tokens + d_rows] for chunk in chunks0])
    dense_all = gather_all(dense_all)
    second0, active0, slope0, parts = feed_pass(xs0, gathered[0], k_rows, f_own, vecs[0])
    later = gather_all(after(packed[1], parts[0]))
    shares = z_scatter(parts)
    mixed0, ot0, lse0 = attend(need, base, begin, after(q0, parts[0]), kvs0, heads)
    sent_mixed = [after(mixed0[0], *shares)] + mixed0[1:]
    sent_mixed = [sent_mixed[0]] + [shift_to(after(mixed0[c], *shares), c) for c in range(1, n)]
    residual, sent = join(me1, sent_mixed, dense_all, shares, residual, vecs[0])

    chunks1 = z_gather(sent)
    gathered.append(after(later, sent))
    dense1 = gathered[1][:, 3 * k_rows + 8 : 3 * k_rows + 8 + d_rows].reshape(-1, width)
    xs1, first1, q1, kvs1, _ = mix_groups(chunks1, 1)
    second1, active1, slope1, parts = feed_pass(xs1, gathered[1], k_rows, f_own, vecs[1])
    cots = gather_z(after(cot.astype(BF), kvs1[0][0]))
    mixed1, ot1, lse1 = attend(need, base, begin, after(q1, parts[0]), kvs1, heads)
    do1, branches = middle(me1, mixed1, dense1, parts, cots)
    shares = z_scatter(branches)
    dq1, dkv1, *send_back = attend_back(need, base, begin, q1, do1, lse1, ot1, kvs1, heads)

    def return_pairs(sends):
        return [
            lax.ppermute(sends[e - 1], "ctx", [(s, s - e) for s in range(e, places)])
            for e in range(1, places)
        ]

    scatter_all = lambda v: lax.psum_scatter(v, ("dp", "ctx"), scatter_dimension=0, tiled=True)[0]

    own_cols = width // (n * shard_count)

    def extra_rows(sums_a):
        bias = unmix_columns(sums_a[2, : 2 * wide], heads).reshape(shard_count, 1, -1)
        return jnp.pad(bias, ((0, 0), (0, 7), (0, width - m_own)))

    def feed_out(total):
        total = total.astype(F32)
        return total[:k_rows], total[-8, :f_own], total[k_rows:-8]

    def mix_out(total):
        total = total.astype(F32)
        return unmix_columns(total[:k_rows], heads), total[-8, :m_own], total[k_rows:-8]

    got1 = return_pairs(send_back)
    cots = after(cots, dq1)
    cots = [lax.dynamic_index_in_dim(cots, (me + c) % n, 0, keepdims=False) for c in range(n)]
    scaled1, sums_b1, feed_g1 = feed_back(
        core1, cots, xs1, slope1, second1, active1, gathered[1], k_rows, vecs[1], places, False
    )
    feed1 = scatter_all(feed_g1)
    shares[0] = after(shares[0], dq1)
    block_output = residual + shifts[1, :, 2] + shifts[1, :, 3]
    for share in shares:
        block_output = block_output + share.astype(F32)
    scaled1 = after(scaled1, block_output)
    gp1, parts1, sums_a1, _ = exit_pass(
        me1, core1, dq1, dkv1, got1, tables, xs1, gathered[1], k_rows, vecs[1], scaled1, heads, places
    )
    parts1 = z_scatter(parts1)
    rows1 = extra_rows(sums_a1)
    (mix_g1,) = mix_back(core1, first1, gp1, mixed1, cots, rows1, places, False, 30)

    grad, grad_own, token_sum0, *pieces = turn(
        me1, parts1, cot, chunks1[0], dense_all, (mix_g1, feed1)
    )
    do0 = [pieces[0]] + [None] * (n - 1)
    for c in range(1, n):
        do0[n - c] = shift_to(pieces[c], c)
    mix1 = scatter_all(after(mix_g1, *do0))
    gs = z_gather(after(grad_own, *do0))
    dq0, dkv0, *send_back = attend_back(need, base, begin, q0, do0, lse0, ot0, kvs0, heads)
    got0 = return_pairs(send_back)
    scaled0, sums_b0, *feed_g0 = feed_back(
        core1, gs, xs0, slope0, second0, active0, gathered[0], k_rows, vecs[0], places, split,
        (dq0,),
    )
    gp0, (parts0,), sums_a0, mix_g0 = exit_pass(
        me1, core1, dq0, dkv0, got0, tables, xs0, gathered[0], k_rows, vecs[0], scaled0, heads,
        places, 2 if split else 1, [first0] + mixed0 + gs, (mix1,),
    )
    parts0 = [lax.psum_scatter(parts0, "tensor", scatter_dimension=0, tiled=True)[0]]
    small = [
        jnp.stack([sums_a0[0], sums_b0[0], sums_a0[1], sums_b0[1], token_sum0[0]]),
        jnp.stack([sums_a1[0], sums_b1[0], sums_a1[1], sums_b1[1], jnp.sum(cot, axis=0)]),
    ]
    sums = jnp.concatenate(small, axis=0).reshape(LAYERS * 5, n, shard_count, own_cols)
    sums = sums.transpose(1, 2, 0, 3)
    if split:
        feed_g0 = after(tuple(feed_g0), gp0)
        up_sum, rest_sum = Scatter(tuple(feed_g0[:2]), False), Scatter(tuple(feed_g0[2:]), True)
        mix_sum = Scatter(mix_g0, False)
        small_sum = Scatter(sums, False, ("tensor", "dp", "ctx"), F32)
        streams = [small_sum, mix_sum, up_sum, rest_sum]
        while mix_sum.order:
            advance(streams)
        (input_grad,) = turn(me1, parts0, grad, sent0)
        advance(streams, input_grad)
        while small_sum.order:
            advance(streams)
        mix0 = mix_out(mix_sum.value)
        feed0 = jnp.concatenate([up_sum.value, rest_sum.value], axis=0)
        total = small_sum.value
    else:
        (input_grad,) = turn(me1, parts0, grad, sent0)
        mix0 = mix_out(scatter_all(mix_g0[0]))
        feed0 = scatter_all(feed_g0[0])
        total = lax.psum_scatter(sums, "tensor", scatter_dimension=0, tiled=False)
        total = scatter_all(total)
    total = total.reshape(LAYERS, 5, own_cols)
    mix1 = mix_out(mix1)
    weight_out = []
    for feed_s, mix_s in ((feed_out(feed0), mix0), (feed_out(feed1), mix1)):
        weight_out.append((mix_s[0], mix_s[1], mix_s[2], feed_s[0], feed_s[1], feed_s[2]))

    gains_out = total[:, :2].transpose(0, 2, 1)
    shifts_out = jnp.stack([total[:, 2], total[:, 3], total[:, 4], total[:, 4]], axis=-1)
    outs = [jnp.stack([weight_out[l][j] for l in range(LAYERS)]) for j in range(6)]
    shape = (rows, 1, own_count, width)
    return (block_output.reshape(shape), input_grad.reshape(shape), *outs, gains_out, shifts_out)


def solution(mesh):
    in_specs = (
        P("dp", "ctx", "tensor", None),
        P("dp", None),
        P(None, ("dp", "ctx"), "tensor"),
        P(None, ("tensor", "dp", "ctx")),
        P(None, ("tensor", "dp", "ctx"), None),
        P(None, ("dp", "ctx"), "tensor"),
        P(None, ("tensor", "dp", "ctx")),
        P(None, ("tensor", "dp", "ctx"), None),
        P(),
        P(),
        P("dp", "ctx", "tensor", None),
    )
    out_specs = (
        P("dp", "ctx", "tensor", None),
        P("dp", "ctx", "tensor", None),
        P(None, ("dp", "ctx"), "tensor"),
        P(None, ("tensor", "dp", "ctx")),
        P(None, ("tensor", "dp", "ctx"), None),
        P(None, ("dp", "ctx"), "tensor"),
        P(None, ("tensor", "dp", "ctx")),
        P(None, ("tensor", "dp", "ctx"), None),
        P(None, ("tensor", "dp", "ctx"), None),
        P(None, ("tensor", "dp", "ctx"), None),
    )
    return jax.shard_map(shards, mesh=mesh, in_specs=in_specs, out_specs=out_specs, check_vma=False)
```

```python
from functools import partial

import jax
import jax.numpy as jnp
from jax import lax
from jax.experimental import pallas as pl
from jax.experimental.pallas import tpu as pltpu
from jax.sharding import PartitionSpec as P

HEAD_DIM = 64
ROTARY = 16
LAYERS = 2
EPSILON = 1e-05
MASKED = -1e30
LANES = 128
SCALE = HEAD_DIM ** (-0.5)
FAR = 1 << 24
BF = jnp.bfloat16
F32 = jnp.float32
NT = (((1,), (1,)), ((), ()))


def dot(a, b):
    return jnp.dot(a, b, preferred_element_type=F32)


def dot_nt(a, b):
    return lax.dot_general(a, b, NT, preferred_element_type=F32)


def cost(micros):
    return pl.CostEstimate(
        flops=int(micros * 1.1e9), transcendentals=0, bytes_accessed=int(micros * 3.6e6)
    )


def params(mib=56):
    return pltpu.CompilerParams(vmem_limit_bytes=mib << 20)


def z_gather(own):
    n = lax.axis_size("tensor")
    return [own] + [
        lax.ppermute(own, "tensor", [(s, (s - c) % n) for s in range(n)]) for c in range(1, n)
    ]


def z_scatter(parts):
    n = lax.axis_size("tensor")
    return [parts[0]] + [
        lax.ppermute(parts[c], "tensor", [(s, (s + c) % n) for s in range(n)]) for c in range(1, n)
    ]


def after(value, *needed):
    return lax.optimization_barrier((value,) + needed)[0]


def bits_of(axis):
    return lax.axis_size(axis).bit_length() - 1


def power_of_two():
    sizes = [lax.axis_size(axis) for axis in ("tensor", "dp", "ctx")]
    return sizes[1] > 1 and all(size & (size - 1) == 0 for size in sizes)


def flip(send, step):
    axis, bit = step
    return lax.ppermute(send, axis, [(s, s ^ (1 << bit)) for s in range(lax.axis_size(axis))])


class Scatter:
    def __init__(self, value, first_y, axes=("dp", "ctx"), wire=BF):
        self.labels = [(axis, b) for axis in axes for b in reversed(range(bits_of(axis)))]
        y_steps = [("dp", b) for b in range(1, bits_of("dp"))]
        x_steps = [("ctx", b) for b in range(bits_of("ctx"))]
        self.order = [("tensor", b) for b in range(bits_of("tensor"))] if "tensor" in axes else []
        self.order += [("dp", 0)] + (y_steps + x_steps if first_y else x_steps + y_steps)
        if not isinstance(value, tuple):
            value = value.reshape((2,) * len(self.labels) + value.shape[len(axes) - 1 :])
        self.value, self.wire = value, wire

    def send(self):
        self.step = self.order.pop(0)
        axis, bit = self.step
        dim = self.labels.index(self.step)
        self.labels.pop(dim)
        if isinstance(self.value, tuple):
            lead = (2,) * len(self.labels)
            out, self.keep = (v.reshape(lead + v.shape[1:]) for v in self.value)
            return out
        mine = (lax.axis_index(axis) >> bit) & 1
        self.keep = lax.dynamic_index_in_dim(self.value, mine, dim, keepdims=False)
        out = lax.dynamic_index_in_dim(self.value, 1 - mine, dim, keepdims=False)
        return out.astype(self.wire)

    def receive(self, got):
        self.value = self.keep + got.astype(F32)


def advance(streams, *needed):
    streams = [stream for stream in streams if stream.order]
    sends = lax.optimization_barrier(tuple(stream.send() for stream in streams) + needed)
    gots = [flip(send, stream.step) for send, stream in zip(sends, streams)]
    for stream, got in zip(streams, gots):
        stream.receive(got)


def rotated(tile, cosine, sine_a, sine_b):
    return tile * cosine + pltpu.roll(tile, LANES - 8, 1) * sine_a + pltpu.roll(tile, 8, 1) * sine_b


def unrotated(tile, cosine, sine_a, sine_b):
    return tile * cosine - pltpu.roll(tile, LANES - 8, 1) * sine_a - pltpu.roll(tile, 8, 1) * sine_b


def unit_of(x):
    values = x.astype(F32)
    centre = values - jnp.mean(values, axis=-1, keepdims=True)
    inverse = lax.rsqrt(jnp.mean(centre * centre, axis=-1, keepdims=True) + EPSILON)
    return centre * inverse


def gathered_row(tail_ref, row, own):
    shards = tail_ref.shape[0]
    return jnp.concatenate(
        [tail_ref[s].astype(F32)[row : row + 1, :own] for s in range(shards)], axis=1
    )


def mix_kernel(n, heads, own, *refs):
    chunk_refs = refs[:n]
    mix_ref, tail_ref, vec_ref, cos_ref, sa_ref, sb_ref = refs[n : n + 6]
    xs_ref, first_ref, q_ref, kv_ref, bias_s = refs[-5:]
    load_chunk(chunk_refs, xs_ref.at[0])
    width = xs_ref.shape[-1]

    @pl.when(pl.program_id(0) == 0)
    def _():
        raw = gathered_row(tail_ref, 1, own)
        size = 3 * HEAD_DIM
        pieces = [raw[:, h * size + HEAD_DIM : (h + 1) * size] for h in range(heads)]
        blank = jnp.zeros((1, HEAD_DIM), F32)
        for h in range(heads):
            pieces += [raw[:, h * size : h * size + HEAD_DIM], blank]
        bias_s[...] = jnp.concatenate(pieces, axis=1)

    first = (unit_of(xs_ref[0]) * vec_ref[0:1] + vec_ref[2:3]).astype(BF)
    first_ref[0] = first
    proj = dot(first, mix_ref[...].reshape(width, -1)[:, : 2 * heads * LANES]) + bias_s[...]
    cosine, sine_a, sine_b = cos_ref[0], sa_ref[0], sb_ref[0]
    for h in range(heads):
        cols = slice(h * LANES, (h + 1) * LANES)
        kv_ref[0, :, cols] = rotated(proj[:, cols], cosine, sine_a, sine_b).astype(BF)
        qcols = slice((heads + h) * LANES, (heads + h + 1) * LANES)
        q_ref[0, :, cols] = (rotated(proj[:, qcols], cosine, sine_a, sine_b) * SCALE).astype(BF)


def store_chunk(refs, value):
    for j, ref in enumerate(refs):

        @pl.when(pl.program_id(0) == j)
        def _(ref=ref):
            ref[...] = value


def load_chunk(refs, held):
    for j, ref in enumerate(refs):

        @pl.when(pl.program_id(0) == j)
        def _(ref=ref):
            held[...] = ref[...]


def feed_kernel(own, *refs):
    x_ref, up_ref, down_ref, tail_ref, vec_ref, second_ref, active_ref, slope_ref = refs[:8]
    part_refs, bias_s = refs[8:-1], refs[-1]

    @pl.when(pl.program_id(0) == 0)
    def _():
        bias_s[...] = gathered_row(tail_ref, 0, own)

    width = x_ref.shape[-1]
    second = (unit_of(x_ref[0]) * vec_ref[1:2] + vec_ref[3:4]).astype(BF)
    second_ref[0] = second
    hidden = dot(second, up_ref[...].reshape(width, -1)) + bias_s[...]
    half = 0.5 * (1.0 + lax.erf(hidden * (0.5**0.5)))
    active = (hidden * half).astype(BF)
    active_ref[0] = active
    bell = jnp.exp(hidden * hidden * -0.5) * 0.3989422804014327
    slope_ref[0] = (half + hidden * bell).astype(BF)
    store_chunk(part_refs, dot(active, down_ref[...].reshape(-1, width)).astype(BF))


def chunk_specs(n, tokens, gathered, k):
    shards, _, ff = gathered.shape
    token = lambda w: pl.BlockSpec((1, tokens, w), lambda c: (c, 0, 0))
    whole = lambda a: pl.BlockSpec(a.shape, lambda c: (0,) * a.ndim)
    weight = lambda j: pl.BlockSpec((shards, k, ff), lambda c: (0, j, 0))
    out = lambda w: jax.ShapeDtypeStruct((n, tokens, w), BF)
    return token, whole, weight, out


def mix_pass(tokens, chunks, place, n, gathered, k, own, vec, tables, heads, held=()):
    width = chunks[0].shape[1]
    count = len(chunks)
    wide = heads * LANES
    shards, _, ff = gathered.shape
    whole = lambda a: pl.BlockSpec(a.shape, lambda c: (0,) * a.ndim)
    token = lambda w: pl.BlockSpec((1, tokens, w), lambda c: (place + c, 0, 0))
    weight = pl.BlockSpec((shards, k, ff), lambda c: (0, 2, 0))
    last = gathered.shape[1] // 8 - 1
    tail = pl.BlockSpec((shards, 8, ff), lambda c: (0, last, 0))
    out = lambda m, w: jax.ShapeDtypeStruct((m, tokens, w), BF)
    first_held = count + 6
    return pl.pallas_call(
        partial(mix_kernel, count, heads, own),
        grid=(count,),
        in_specs=[pl.BlockSpec((tokens, width), lambda c: (0, 0))] * count
        + [weight, tail, whole(vec)]
        + [token(LANES)] * 3
        + [pl.BlockSpec(memory_space=pl.ANY)] * len(held),
        out_specs=[token(width), token(width), token(wide)]
        + [pl.BlockSpec((1, tokens, wide), lambda c: (c, 0, 0))],
        out_shape=[out(n, width), out(n, width), out(n, wide), out(count, wide)],
        input_output_aliases={first_held + i: i for i in range(len(held))},
        scratch_shapes=[pltpu.VMEM((1, 2 * wide), F32)],
        compiler_params=params(),
        cost_estimate=cost(12),
        name="mix_pass",
    )(*chunks, gathered, gathered, vec, *tables, *held)


def feed_pass(xs, gathered, k, own, vec):
    n, tokens, width = xs.shape
    ff = gathered.shape[2]
    token, whole, weight, out = chunk_specs(n, tokens, gathered, k)
    last = gathered.shape[1] // 8 - 1
    second, active, slope, *parts = pl.pallas_call(
        partial(feed_kernel, own),
        grid=(n,),
        in_specs=[token(width), weight(0), weight(1)]
        + [pl.BlockSpec((gathered.shape[0], 8, ff), lambda c: (0, last, 0)), whole(vec)],
        out_specs=[token(width), token(ff), token(ff)]
        + [pl.BlockSpec((tokens, width), lambda c: (0, 0))] * n,
        out_shape=[out(width), out(ff), out(ff)]
        + [jax.ShapeDtypeStruct((tokens, width), BF)] * n,
        scratch_shapes=[pltpu.VMEM((1, ff), F32)],
        compiler_params=params(),
        cost_estimate=cost(20),
        name="feed_pass",
    )(xs, gathered, gathered, gathered, vec)
    return second, active, slope, parts


def middle_kernel(n, me_ref, dense_ref, grads_ref, *refs):
    mixed_refs, part_refs = refs[:n], refs[n : 2 * n]
    do_refs, out_refs = refs[2 * n : 3 * n], refs[3 * n :]
    rows = mixed_refs[0].shape[1] // dense_ref.shape[0]
    dense = dense_ref[:, :rows].reshape(-1, dense_ref.shape[-1])
    for c in range(n):
        total = dot(mixed_refs[c][...], dense) + part_refs[c][...].astype(F32)
        out_refs[c][...] = total.astype(BF)
        grad = grads_ref[lax.rem(me_ref[0] + c, n)]
        do_refs[c][...] = dot_nt(grad, dense).astype(BF)


def middle(me1, mixed, gathered, k, d, parts, grads):
    n = len(parts)
    padded = d + -d % 8
    full = lambda a: pl.BlockSpec(a.shape, lambda i: (0,) * a.ndim)
    dense = pl.BlockSpec(
        (gathered.shape[0], padded, gathered.shape[2]), lambda i: (0, 3 * k // padded, 0)
    )
    outs = pl.pallas_call(
        partial(middle_kernel, n),
        grid=(1,),
        in_specs=[pl.BlockSpec(memory_space=pltpu.SMEM), dense, full(grads)]
        + [full(a) for a in mixed + parts],
        out_specs=[full(a) for a in mixed + parts],
        out_shape=[jax.ShapeDtypeStruct(mixed[0].shape, BF)] * n
        + [jax.ShapeDtypeStruct(parts[0].shape, BF)] * n,
        compiler_params=params(),
        cost_estimate=cost(4),
        name="middle",
    )(me1, gathered, grads, *mixed, *parts)
    return outs[:n], outs[n:]


def load_pairs(kv_refs, kv_s):
    place = 0
    for ref in kv_refs:
        for c in range(ref.shape[0]):
            kv_s[place] = ref[c, 0]
            place += 1


def each_block(plan_ref, row, c, blocks, take):
    start = c * (blocks + 1)
    count = plan_ref[row, start]

    def pair(t, _):
        take([plan_ref[row, start + 1 + 2 * t], plan_ref[row, start + 2 + 2 * t]])
        return 0

    lax.fori_loop(0, count // 2, pair, 0)

    @pl.when(count % 2 == 1)
    def _():
        take([plan_ref[row, start + count]])


def allowed_pairs(base_ref, begin_ref, kb, c, n, shape):
    key_slot = base_ref[n + kb] + lax.broadcasted_iota(jnp.int32, shape, 0)
    query_slot = base_ref[c] + lax.broadcasted_iota(jnp.int32, shape, 1)
    return (key_slot >= begin_ref[0, c]) & (key_slot <= query_slot)


def attend_kernel(heads, extras, groups, need_ref, base_ref, begin_ref, q_ref, *refs):
    kv_refs = refs[:groups]
    n, _, count, _ = q_ref.shape
    mixed_refs = refs[groups : groups + n]
    ot_ref, lse_ref, kv_s, vt_s, top_s, total_s, acc_s, mixed_s = refs[groups + n :]
    blocks = n * (1 + extras)
    row = pl.program_id(0)
    load_pairs(kv_refs, kv_s)

    def turn(kb, _):
        for h in range(heads):
            tile = kv_s[kb, :, h * LANES : (h + 1) * LANES].astype(F32)
            vt_s[kb, h] = tile.T[HEAD_DIM:].astype(BF)
        return 0

    lax.fori_loop(0, blocks, turn, 0)

    def per_query(c, _):
        top_s[...] = jnp.full(top_s.shape, MASKED, F32)
        total_s[...] = jnp.zeros(total_s.shape, F32)
        acc_s[...] = jnp.zeros(acc_s.shape, F32)

        def take(kbs):
            column = lambda h: slice(h * LANES, (h + 1) * LANES)
            held = [
                [dot_nt(kv_s[kb, :, column(h)], q_ref[c, 0, :, column(h)]) for h in range(heads)]
                for kb in kbs
            ]
            masks = [allowed_pairs(base_ref, begin_ref, kb, c, n, (count, count)) for kb in kbs]
            low, fades = [], []
            for h in range(heads):
                scores = [jnp.where(mask, own[h], MASKED) for mask, own in zip(masks, held)]
                old = top_s[h]
                new = old
                for score in scores:
                    new = jnp.maximum(new, jnp.max(score, axis=0, keepdims=True))
                fade = jnp.exp(old - new)
                total = total_s[h] * fade
                weights = []
                for score in scores:
                    weight = jnp.exp(score - new)
                    total = total + jnp.sum(weight, axis=0, keepdims=True)
                    weights.append(weight.astype(BF))
                top_s[h] = new
                total_s[h] = total
                low.append(weights)
                fades.append(fade)
            for h in range(heads):
                acc = acc_s[h] * fades[h]
                for kb, weight in zip(kbs, low[h]):
                    acc = acc + dot(vt_s[kb, h], weight)
                acc_s[h] = acc

        each_block(need_ref, row, c, blocks, take)
        outs = []
        for h in range(heads):
            total = total_s[h]
            outs.append(acc_s[h] / total)
            lse_ref[0, c, h : h + 1] = top_s[h] + jnp.log(total)
        whole = jnp.concatenate(outs, axis=0)
        ot_ref[0, c] = whole
        mixed_s[c] = whole.T.astype(BF)
        return 0

    lax.fori_loop(0, n, per_query, 0)
    for c in range(n):
        mixed_refs[c][0] = mixed_s[c]


def attention_specs(q, kvs):
    n, rows, count, wide = q.shape
    smem = pl.BlockSpec(memory_space=pltpu.SMEM)
    begin = pl.BlockSpec((1, n, 1, count), lambda r: (r, 0, 0, 0))
    tokens = lambda a: pl.BlockSpec((a.shape[0], 1, count, wide), lambda r: (0, r, 0, 0))
    flat = [a for group in kvs for a in group]
    return n, rows, count, wide, smem, begin, tokens, flat


def attend(need, base, begin, q, kvs, heads):
    extras = len(kvs) - 1
    n, rows, count, wide, smem, begin_spec, tokens, flat = attention_specs(q, kvs)
    blocks = n * (1 + extras)
    narrow = heads * HEAD_DIM
    outs = pl.pallas_call(
        partial(attend_kernel, heads, extras, len(flat)),
        grid=(rows,),
        in_specs=[smem, smem, begin_spec, tokens(q)] + [tokens(a) for a in flat],
        out_specs=[pl.BlockSpec((1, count, narrow), lambda r: (r, 0, 0))] * n
        + [
            pl.BlockSpec((1, n, narrow, count), lambda r: (r, 0, 0, 0)),
            pl.BlockSpec((1, n, heads, count), lambda r: (r, 0, 0, 0)),
        ],
        out_shape=[jax.ShapeDtypeStruct((rows, count, narrow), BF)] * n
        + [
            jax.ShapeDtypeStruct((rows, n, narrow, count), F32),
            jax.ShapeDtypeStruct((rows, n, heads, count), F32),
        ],
        scratch_shapes=[
            pltpu.VMEM((blocks, count, wide), BF),
            pltpu.VMEM((blocks, heads, HEAD_DIM, count), BF),
            pltpu.VMEM((heads, 1, count), F32),
            pltpu.VMEM((heads, 1, count), F32),
            pltpu.VMEM((heads, HEAD_DIM, count), F32),
            pltpu.VMEM((n, count, narrow), BF),
        ],
        compiler_params=params(),
        cost_estimate=cost(400),
        name="attend",
    )(need, base, begin, q, *flat)
    return [a.reshape(rows * count, narrow) for a in outs[:n]], outs[n], outs[n + 1]


def attend_back_kernel(heads, extras, groups, need_ref, base_ref, begin_ref, q_ref, *refs):
    n, _, count, _ = q_ref.shape
    do_refs, lse_ref, ot_ref = refs[:n], refs[n], refs[n + 1]
    kv_refs = refs[n + 2 : n + 2 + groups]
    dq_ref = refs[n + 2 + groups]
    dkv_refs = refs[n + 3 + groups : n + 4 + groups + extras]
    kv_s, kt_s, dkv_s, dqt_s, delta_s, do_s, narrow_s = refs[n + 4 + groups + extras :]
    blocks = n * (1 + extras)
    row = pl.program_id(0)
    load_pairs(kv_refs, kv_s)
    for c in range(n):
        narrow_s[c] = do_refs[c][0]

    def turn(kb, _):
        for h in range(heads):
            tile = kv_s[kb, :, h * LANES : (h + 1) * LANES].astype(F32)
            kt_s[kb, h] = tile.T[:HEAD_DIM].astype(BF)
        dkv_s[kb] = jnp.zeros(dkv_s.shape[1:], F32)
        return 0

    lax.fori_loop(0, blocks, turn, 0)

    def per_query(c, _):
        dqt_s[...] = jnp.zeros(dqt_s.shape, F32)
        for h in range(heads):
            cols = slice(h * LANES, (h + 1) * LANES)
            grad = narrow_s[c, :, h * HEAD_DIM : (h + 1) * HEAD_DIM].astype(F32)
            grad = jnp.concatenate([jnp.zeros((count, HEAD_DIM), F32), grad], axis=1)
            do_s[:, cols] = grad.astype(BF)
            dot_t = grad.T[HEAD_DIM:]
            out_t = ot_ref[0, c, h * HEAD_DIM : (h + 1) * HEAD_DIM]
            delta_s[h] = jnp.sum(dot_t * out_t, axis=0, keepdims=True)

        def take(kbs):
            column = lambda h: slice(h * LANES, (h + 1) * LANES)
            queries = [q_ref[c, 0, :, column(h)] for h in range(heads)]
            grads = [do_s[:, column(h)] for h in range(heads)]
            held = []
            for kb in kbs:
                pairs = [kv_s[kb, :, column(h)] for h in range(heads)]
                held.append(
                    [(dot_nt(pairs[h], queries[h]), dot_nt(pairs[h], grads[h])) for h in range(heads)]
                )
            low = []
            for kb, own in zip(kbs, held):
                allowed = allowed_pairs(base_ref, begin_ref, kb, c, n, (count, count))
                for h in range(heads):
                    scores = jnp.where(allowed, own[h][0], MASKED)
                    probs = jnp.exp(scores - lse_ref[0, c, h : h + 1])
                    steps = probs * (own[h][1] - delta_s[h])
                    low.append((steps.astype(BF), probs.astype(BF)))
            for i, kb in enumerate(kbs):
                for h in range(heads):
                    steps, probs = low[i * heads + h]
                    dqt_s[h] += dot(kt_s[kb, h], steps)
                    dkv_s[kb, :, column(h)] += dot(steps, queries[h]) + dot(probs, grads[h])

        each_block(need_ref, row, c, blocks, take)
        for h in range(heads):
            tile = jnp.concatenate([dqt_s[h], jnp.zeros((HEAD_DIM, count), F32)], axis=0)
            dq_ref[c, 0, :, h * LANES : (h + 1) * LANES] = tile.T * SCALE
        return 0

    lax.fori_loop(0, n, per_query, 0)
    for e, ref in enumerate(dkv_refs):
        for c in range(n):
            ref[c, 0] = dkv_s[e * n + c].astype(ref.dtype)


def attend_back(need, base, begin, q, do, lse, ot, kvs, heads):
    extras = len(kvs) - 1
    n, rows, count, wide, smem, begin_spec, tokens, flat = attention_specs(q, kvs)
    blocks = n * (1 + extras)
    narrow = heads * HEAD_DIM
    return pl.pallas_call(
        partial(attend_back_kernel, heads, extras, len(flat)),
        grid=(rows,),
        in_specs=[smem, smem, begin_spec, tokens(q)]
        + [pl.BlockSpec((1, count, narrow), lambda r: (r, 0, 0))] * n
        + [
            pl.BlockSpec((1, n, heads, count), lambda r: (r, 0, 0, 0)),
            pl.BlockSpec((1, n, narrow, count), lambda r: (r, 0, 0, 0)),
        ]
        + [tokens(a) for a in flat],
        out_specs=[tokens(q)] * (2 + extras),
        out_shape=[jax.ShapeDtypeStruct(q.shape, F32)] * 2
        + [jax.ShapeDtypeStruct(q.shape, BF)] * extras,
        scratch_shapes=[
            pltpu.VMEM((blocks, count, wide), BF),
            pltpu.VMEM((blocks, heads, HEAD_DIM, count), BF),
            pltpu.VMEM((blocks, count, wide), F32),
            pltpu.VMEM((heads, HEAD_DIM, count), F32),
            pltpu.VMEM((heads, 1, count), F32),
            pltpu.VMEM((count, wide), BF),
            pltpu.VMEM((n, count, narrow), BF),
        ],
        compiler_params=params(),
        cost_estimate=cost(40),
        name="attend_back",
    )(need, base, begin, q, *[a.reshape(rows, count, narrow) for a in do], lse, ot, *flat)


TN = (((0,), (0,)), ((), ()))


def dot_tn(a, b):
    return lax.dot_general(a, b, TN, preferred_element_type=F32)


def half_shard(place, inner, bit):
    return (place // inner * 2 + bit) * inner + place % inner


def store_shards(refs, core_ref, shards, inner, block):
    if len(refs) == 1:
        for s in range(shards):
            refs[0][s] = block(s)
        return
    mine = core_ref[0]
    for place in range(shards // 2):
        refs[0][place] = block(half_shard(place, inner, 1 - mine))
        refs[1][place] = block(half_shard(place, inner, mine))


def row_block(ref, s, size):
    start = s * size if isinstance(s, int) else pl.multiple_of(s * size, 8)
    return ref[pl.ds(start, size)]


def feed_back_kernel(n, gates, inner, split, core_ref, *refs):
    grad_refs = refs[:n]
    x_ref, slope_ref, second_ref, active_ref, up_ref, down_ref, vec_ref = refs[n : n + 7]
    refs = refs[n + 7 + gates :]
    scaled_ref, sums_ref, outs = refs[0], refs[1], refs[2:-4]
    up_s, down_s, grad_s, tail_s = refs[-4:]
    width = x_ref.shape[-1]
    last = pl.program_id(0) == pl.num_programs(0) - 1

    @pl.when(pl.program_id(0) == 0)
    def _():
        sums_ref[...] = jnp.zeros(sums_ref.shape, F32)
        up_s[...] = jnp.zeros(up_s.shape, F32)
        down_s[...] = jnp.zeros(down_s.shape, F32)

    load_chunk(grad_refs, grad_s)
    down = down_ref[...].reshape(-1, width)
    grad = grad_s[...]
    grad_active = dot_nt(grad, down)
    down_s[...] += dot_tn(active_ref[0], grad)
    grad_hidden = (grad_active * slope_ref[0].astype(F32)).astype(BF)
    grad_second = dot_nt(grad_hidden, up_ref[...].reshape(width, -1))
    unit = unit_of(x_ref[0])
    sums_ref[0:1] += jnp.sum(grad_second * unit, axis=0, keepdims=True)
    sums_ref[1:2] += jnp.sum(grad_second, axis=0, keepdims=True)
    sums_ref[2:3] += jnp.sum(grad_hidden.astype(F32), axis=0, keepdims=True)
    scaled_ref[0] = grad_second * vec_ref[1:2]
    up_s[...] += dot_tn(second_ref[0], grad_hidden)

    @pl.when(last)
    def _():
        shards, k = up_ref.shape[:2]
        f = down_s.shape[0] // shards
        own = up_s.shape[1] // shards
        pad = jnp.zeros((8, width - own), F32)
        for s in range(shards):
            tail = jnp.broadcast_to(sums_ref[2:3, s * own : (s + 1) * own], (8, own))
            tail_s[s] = jnp.concatenate([tail, pad], axis=1)
        up_block = lambda s: row_block(up_s, s, k).astype(BF)
        rest_block = lambda s: jnp.concatenate(
            [row_block(down_s, s, f), tail_s[s]], axis=0
        ).astype(BF)
        if split:
            store_shards(outs[:2], core_ref, shards, inner, up_block)
            store_shards(outs[2:], core_ref, shards, inner, rest_block)
        else:
            store_shards(
                outs, core_ref, shards, inner,
                lambda s: jnp.concatenate([up_block(s), rest_block(s)], axis=0),
            )


def feed_back(core1, gs, xs, slope, second, active, gathered, k, vec, inner, split, gates=()):
    n, tokens, width = xs.shape
    shards, _, ff = gathered.shape
    f = ff // shards
    token, whole, weight, _ = chunk_specs(n, tokens, gathered, k)
    fixed = pl.BlockSpec((8, width), lambda c: (0, 0))
    grads = [(shards, k + f + 8, width)]
    if split:
        grads = [(shards // 2, k, width)] * 2 + [(shards // 2, f + 8, width)] * 2
    return pl.pallas_call(
        partial(feed_back_kernel, n, len(gates), inner, split),
        grid=(n,),
        in_specs=[pl.BlockSpec(memory_space=pltpu.SMEM)]
        + [whole(gs[0])] * n
        + [token(width), token(ff), token(width), token(ff), weight(0), weight(1), fixed]
        + [pl.BlockSpec(memory_space=pl.ANY)] * len(gates),
        out_specs=[token(width), fixed] + [pl.BlockSpec(g, lambda c: (0, 0, 0)) for g in grads],
        scratch_shapes=[
            pltpu.VMEM((width, ff), F32),
            pltpu.VMEM((ff, width), F32),
            pltpu.VMEM((tokens, width), BF),
            pltpu.VMEM((shards, 8, width), F32),
        ],
        out_shape=[
            jax.ShapeDtypeStruct((n, tokens, width), F32),
            jax.ShapeDtypeStruct((8, width), F32),
        ]
        + [jax.ShapeDtypeStruct(g, BF) for g in grads],
        compiler_params=params(),
        cost_estimate=cost(12),
        name="feed_back",
    )(core1, *gs, xs, slope, second, active, gathered, gathered, vec, *gates)


def mix_back_kernel(n, inner, outs, core_ref, *refs):
    first_ref, gp_ref, bias_ref = refs[:3]
    mixed_refs, grad_refs = refs[3 : 3 + n], refs[3 + n : 3 + 2 * n]
    grads_refs = refs[-4 - outs : -4]
    mix_s, dense_s, mixed_s, grad_s = refs[-4:]
    last = pl.program_id(0) == pl.num_programs(0) - 1

    @pl.when(pl.program_id(0) == 0)
    def _():
        mix_s[...] = jnp.zeros(mix_s.shape, F32)
        dense_s[...] = jnp.zeros(dense_s.shape, F32)

    load_chunk(grad_refs, grad_s)
    load_chunk(mixed_refs, mixed_s)
    mix_s[...] += dot_tn(first_ref[0], gp_ref[0])
    dense_s[...] += dot_tn(mixed_s[...], grad_s[...])

    @pl.when(last)
    def _():
        shards = bias_ref.shape[0]
        k = mix_s.shape[0] // shards
        d = dense_s.shape[0] // shards

        def block(s):
            rows = [row_block(mix_s, s, k), row_block(dense_s, s, d), bias_ref[s]]
            return jnp.concatenate(rows, axis=0).astype(BF)

        store_shards(grads_refs, core_ref, shards, inner, block)


def mix_back(core1, first, gp, mixed, gs, bias, inner, split, micros, gates=()):
    n, tokens, width = first.shape
    shards = bias.shape[0]
    narrow = mixed[0].shape[-1]
    token = lambda w: pl.BlockSpec((1, tokens, w), lambda c: (c, 0, 0))
    whole = lambda a: pl.BlockSpec(a.shape, lambda c: (0,) * a.ndim)
    count = 2 if split else 1
    grads = (shards // count, width // shards + narrow // shards + 8, width)
    return pl.pallas_call(
        partial(mix_back_kernel, n, inner, count),
        grid=(n,),
        in_specs=[pl.BlockSpec(memory_space=pltpu.SMEM), token(width), token(gp.shape[-1]), whole(bias)]
        + [whole(mixed[0])] * n
        + [whole(gs[0])] * n
        + [pl.BlockSpec(memory_space=pl.ANY)] * len(gates),
        out_specs=[pl.BlockSpec(grads, lambda c: (0, 0, 0))] * count,
        scratch_shapes=[
            pltpu.VMEM((width, gp.shape[-1]), F32),
            pltpu.VMEM((narrow, width), F32),
            pltpu.VMEM((tokens, narrow), BF),
            pltpu.VMEM((tokens, width), BF),
        ],
        out_shape=[jax.ShapeDtypeStruct(grads, BF)] * count,
        compiler_params=params(),
        cost_estimate=cost(micros),
        name="mix_back",
    )(core1, first, gp, bias, *mixed, *gs, *gates)


def join_kernel(n, me_ref, dense_ref, residual_ref, vec_ref, *refs):
    mixed_refs, share_refs, out_ref, sent_ref = refs[:n], refs[n : 2 * n], refs[2 * n], refs[2 * n + 1]
    total = residual_ref[...] + vec_ref[4:5] + vec_ref[5:6]
    for c in range(n):
        rows = dense_ref[:, (n - c) % n]
        rows = rows.reshape(-1, rows.shape[-1])
        total = total + share_refs[c][...].astype(F32) + dot(mixed_refs[c][...], rows)
    out_ref[...] = total
    sent_ref[...] = total.astype(BF)


def join(me1, mixed, dense_all, shares, residual, vec):
    shape = residual.shape
    vmem = pl.BlockSpec(memory_space=pltpu.VMEM)
    return pl.pallas_call(
        partial(join_kernel, len(shares)),
        in_specs=[pl.BlockSpec(memory_space=pltpu.SMEM)] + [vmem] * (3 + 2 * len(shares)),
        out_specs=[vmem, vmem],
        out_shape=[jax.ShapeDtypeStruct(shape, F32), jax.ShapeDtypeStruct(shape, BF)],
        compiler_params=params(),
        cost_estimate=cost(3),
        name="join",
    )(me1, dense_all, residual, vec, *mixed, *shares)


def turn_kernel(n, gates, me_ref, *refs):
    summed = refs[0][...].astype(F32)
    for ref in refs[1:n]:
        summed = summed + ref[...].astype(F32)
    grad_ref, x_ref = refs[n : n + 2]
    refs = refs[n + 2 :]
    values = x_ref[...].astype(F32)
    centre = values - jnp.mean(values, axis=-1, keepdims=True)
    inverse = lax.rsqrt(jnp.mean(centre * centre, axis=-1, keepdims=True) + EPSILON)
    unit = centre * inverse
    mean_s = jnp.mean(summed, axis=-1, keepdims=True)
    mean_su = jnp.mean(summed * unit, axis=-1, keepdims=True)
    grad = grad_ref[...] + inverse * (summed - mean_s - unit * mean_su)
    if len(refs) == gates + 1:
        refs[-1][...] = grad
        return
    dense_ref, out_ref, sent_ref, sums_ref = refs[0], *refs[gates + 1 : gates + 4]
    piece_refs = refs[gates + 4 :]
    out_ref[...] = grad
    sent = grad.astype(BF)
    sent_ref[...] = sent
    for c, piece_ref in enumerate(piece_refs):
        rows = dense_ref[:, c]
        piece_ref[...] = dot_nt(sent, rows.reshape(-1, rows.shape[-1])).astype(BF)
    sums_ref[0:1] = jnp.sum(grad, axis=0, keepdims=True)
    sums_ref[1:2] = jnp.sum(grad_ref[...], axis=0, keepdims=True)


def turn(me1, parts, grad, x_own, dense_all=None, gates=()):
    shape = grad.shape
    outs = [jax.ShapeDtypeStruct(shape, F32)]
    vmem = pl.BlockSpec(memory_space=pltpu.VMEM)
    more = []
    if dense_all is not None:
        more = [dense_all]
        outs += [jax.ShapeDtypeStruct(shape, BF), jax.ShapeDtypeStruct((8, shape[1]), F32)]
        narrow = dense_all.shape[0] * dense_all.shape[2]
        outs += [jax.ShapeDtypeStruct((shape[0], narrow), BF)] * dense_all.shape[1]
    return pl.pallas_call(
        partial(turn_kernel, len(parts), len(gates)),
        in_specs=[pl.BlockSpec(memory_space=pltpu.SMEM)]
        + [vmem] * (len(parts) + 2 + len(more))
        + [pl.BlockSpec(memory_space=pl.ANY)] * len(gates),
        out_specs=[vmem] * len(outs),
        out_shape=outs,
        compiler_params=params(),
        cost_estimate=cost(3),
        name="turn",
    )(me1, *parts, grad, x_own, *more, *gates)


def exit_kernel(n, heads, extras, gates, inner, outs, halves, _, core_ref, dq_ref, dkv_ref, *refs):
    got_refs = refs[:extras]
    cos_ref, sa_ref, sb_ref, x_ref, mix_ref, vec_ref, scaled_ref = refs[extras : extras + 7]
    refs = refs[extras + 7 :]
    fold = halves > 0
    if fold:
        first_ref, mixed_refs, grad_refs = refs[0], refs[1 : 1 + n], refs[1 + n : 1 + 2 * n]
        refs = refs[1 + 2 * n :]
    refs = refs[gates:]
    gp_ref, sums_ref, part_refs = refs[0], refs[1], refs[2 : 2 + outs]
    grads_refs, scratch = refs[2 + outs : 2 + outs + halves], refs[2 + outs + halves :]
    width = x_ref.shape[-1]

    @pl.when(pl.program_id(0) == 0)
    def _():
        sums_ref[...] = jnp.zeros(sums_ref.shape, F32)
        if fold:
            scratch[0][...] = jnp.zeros(scratch[0].shape, F32)
            scratch[1][...] = jnp.zeros(scratch[1].shape, F32)

    if fold:
        mix_s, dense_s, mixed_s, grad_s, tail_s = scratch
        load_chunk(grad_refs, grad_s)
        load_chunk(mixed_refs, mixed_s)
        dense_s[...] += dot_tn(mixed_s[...], grad_s[...])
    cosine, sine_a, sine_b = cos_ref[0], sa_ref[0], sb_ref[0]
    for h in range(heads):
        cols = slice(h * LANES, (h + 1) * LANES)
        pair = dkv_ref[0, :, cols]
        for ref in got_refs:
            pair = pair + ref[0, :, cols].astype(F32)
        gp_ref[0, :, cols] = unrotated(pair, cosine, sine_a, sine_b).astype(BF)
        qcols = slice((heads + h) * LANES, (heads + h + 1) * LANES)
        gp_ref[0, :, qcols] = unrotated(dq_ref[0, :, cols], cosine, sine_a, sine_b).astype(BF)
    gp = gp_ref[0]
    grad_first = dot_nt(gp, mix_ref[...].reshape(width, -1))
    if fold:
        mix_s[...] += dot_tn(first_ref[0], gp)
    unit = unit_of(x_ref[0])
    sums_ref[0:1] += jnp.sum(grad_first * unit, axis=0, keepdims=True)
    sums_ref[1:2] += jnp.sum(grad_first, axis=0, keepdims=True)
    sums_ref[2:3] += jnp.sum(gp.astype(F32), axis=0, keepdims=True)
    part = (grad_first * vec_ref[0:1] + scaled_ref[0]).astype(BF)
    if outs == 1:
        part_refs[0][0] = part
    else:
        store_chunk(part_refs, part)
    if not fold:
        return

    @pl.when(pl.program_id(0) == pl.num_programs(0) - 1)
    def _():
        shards = mix_ref.shape[0]
        k = mix_s.shape[0] // shards
        d = dense_s.shape[0] // shards
        row = sums_ref[2:3]
        pieces = []
        for h in range(heads):
            query = (heads + h) * LANES
            pieces.append(row[:, query : query + HEAD_DIM])
            pieces.append(row[:, h * LANES : (h + 1) * LANES])
        raw = jnp.concatenate(pieces, axis=1)
        own = raw.shape[1] // shards
        pad = jnp.zeros((8, width - own), F32)
        for s in range(shards):
            tail = jnp.broadcast_to(raw[:, s * own : (s + 1) * own], (8, own))
            tail_s[s] = jnp.concatenate([tail, pad], axis=1)

        def block(s):
            rows = [row_block(mix_s, s, k), row_block(dense_s, s, d), tail_s[s]]
            return jnp.concatenate(rows, axis=0).astype(BF)

        store_shards(grads_refs, core_ref, shards, inner, block)


def exit_pass(
    me1, core1, dq, dkv, got, tables, xs, gathered, k, vec, scaled, heads, inner, halves=0,
    fold=(), gates=(),
):
    n, tokens, width = xs.shape
    shards, _, ff = gathered.shape
    wide = heads * LANES
    narrow = heads * HEAD_DIM
    token = lambda w: pl.BlockSpec((1, tokens, w), lambda c, s: (c, 0, 0))
    weight = lambda j: pl.BlockSpec((shards, k, ff), lambda c, s: (0, j, 0))
    whole = lambda a: pl.BlockSpec(a.shape, lambda c, s: (0,) * a.ndim)
    fixed = pl.BlockSpec((8, width), lambda c, s: (0, 0))
    flat = lambda a: a.reshape(n, tokens, wide)
    fold_specs, grad_specs, grad_shapes, scratch = [], [], [], []
    if halves:
        part_specs = [pl.BlockSpec((1, tokens, width), lambda c, s: ((s[0] + c) % n, 0, 0))]
        part_shapes = [jax.ShapeDtypeStruct((n, tokens, width), BF)]
        fold_specs = [token(width)] + [whole(a) for a in fold[1:]]
        grads = (shards // halves, width // shards + narrow // shards + 8, width)
        grad_specs = [pl.BlockSpec(grads, lambda c, s: (0, 0, 0))] * halves
        grad_shapes = [jax.ShapeDtypeStruct(grads, BF)] * halves
        scratch = [
            pltpu.VMEM((width, 2 * wide), F32),
            pltpu.VMEM((narrow, width), F32),
            pltpu.VMEM((tokens, narrow), BF),
            pltpu.VMEM((tokens, width), BF),
            pltpu.VMEM((shards, 8, width), F32),
        ]
    else:
        part_specs = [pl.BlockSpec((tokens, width), lambda c, s: (0, 0))] * n
        part_shapes = [jax.ShapeDtypeStruct((tokens, width), BF)] * n
    outs = len(part_specs)
    gp, sums, *rest = pl.pallas_call(
        partial(exit_kernel, n, heads, len(got), len(gates), inner, outs, halves),
        grid_spec=pltpu.PrefetchScalarGridSpec(
            num_scalar_prefetch=1,
            grid=(n,),
            in_specs=[pl.BlockSpec(memory_space=pltpu.SMEM)]
            + [token(wide)] * (2 + len(got))
            + [token(LANES)] * 3
            + [token(width), weight(2), fixed, token(width)]
            + fold_specs
            + [pl.BlockSpec(memory_space=pl.ANY)] * len(gates),
            out_specs=[token(2 * wide), fixed] + part_specs + grad_specs,
            scratch_shapes=scratch,
        ),
        out_shape=[
            jax.ShapeDtypeStruct((n, tokens, 2 * wide), BF),
            jax.ShapeDtypeStruct((8, width), F32),
        ]
        + part_shapes
        + grad_shapes,
        compiler_params=params(),
        cost_estimate=cost(100),
        name="exit_pass",
    )(
        me1, core1, flat(dq), flat(dkv), *[flat(a) for a in got], *tables, xs, gathered, vec,
        scaled, *fold, *gates,
    )
    return gp, rest[:outs], sums, tuple(rest[outs:])


def mix_columns(weight, heads):
    lead = weight.shape[:-1]
    split = weight.reshape(lead + (heads, 3, HEAD_DIM))
    pairs = split[..., 1:, :].reshape(lead + (heads * LANES,))
    query = jnp.concatenate([split[..., 0, :], jnp.zeros_like(split[..., 0, :])], axis=-1)
    return jnp.concatenate([pairs, query.reshape(lead + (heads * LANES,))], axis=-1)


def unmix_columns(grad, heads):
    lead = grad.shape[:-1]
    split = grad.reshape(lead + (2, heads, 2, HEAD_DIM))
    order = [split[..., 1, :, 0, :], split[..., 0, :, 0, :], split[..., 0, :, 1, :]]
    return jnp.stack(order, axis=-2).reshape(lead + (heads * 3 * HEAD_DIM,))


def pack_layer(mix_w, mix_b, dense_w, up_w, up_b, down_w, heads):
    width = up_w.shape[1]
    mix = mix_columns(mix_w, heads)
    wide = lambda v: jnp.pad(v, (0, width - v.shape[0]))[None]
    rows = [up_w, down_w, jnp.pad(mix, ((0, 0), (0, width - mix.shape[1])))]
    if dense_w is not None:
        rows += [dense_w, jnp.zeros((-dense_w.shape[0] % 8, width), up_w.dtype)]
    rows += [wide(up_b), wide(mix_b), jnp.zeros((6, width), up_w.dtype)]
    return jnp.concatenate(rows, axis=0)


def shards(
    block_input, seq_lengths, project_weight, project_bias, dense_weight, up_weight, up_bias,
    down_weight, norm_gains, shift_vectors, cotangent,
):
    rows, _, own_count, width = block_input.shape
    n = lax.axis_size("tensor")
    places = lax.axis_size("ctx")
    extras = places - 1
    place = lax.axis_index("ctx")
    me = lax.axis_index("tensor")
    me1 = me.reshape(1)
    core1 = (lax.axis_index("dp") & 1).reshape(1)
    split = power_of_two()
    block_len = own_count * n
    tokens = rows * own_count
    heads = project_weight.shape[2] // (3 * HEAD_DIM)
    wide = heads * LANES
    k_rows = up_weight.shape[1]
    d_rows = dense_weight.shape[1]
    f_own = up_bias.shape[1]
    m_own = project_bias.shape[1]
    shard_count = lax.axis_size("dp") * places

    ends = jnp.cumsum(seq_lengths, axis=1)
    order = (me + jnp.arange(n, dtype=jnp.int32)) % n
    query_base = place * block_len + order * own_count
    slots = query_base[:, None] + jnp.arange(own_count, dtype=jnp.int32)[None]
    passed = (ends[:, None, None, :] <= slots[None, :, :, None]).astype(jnp.int32)
    begin = jnp.sum(passed * seq_lengths[:, None, None, :], axis=3)
    position = (slots[None] - begin).transpose(1, 0, 2).reshape(-1)
    frequency = 1.0 / 10000.0 ** (jnp.arange(0, ROTARY, 2, dtype=F32) / ROTARY)
    angle = frequency[:, None] * position.astype(F32)[None, :]
    cosine, sine = lax.optimization_barrier((jnp.cos(angle), jnp.sin(angle)))
    cosine, sine = cosine.T, sine.T
    ones = jnp.ones((cosine.shape[0], LANES - ROTARY), F32)
    zero8 = jnp.zeros_like(sine)
    tables = (
        jnp.concatenate([cosine, cosine, ones], axis=1).reshape(n, tokens, LANES),
        jnp.concatenate([-sine, zero8, ones * 0.0], axis=1).reshape(n, tokens, LANES),
        jnp.concatenate([zero8, sine, ones * 0.0], axis=1).reshape(n, tokens, LANES),
    )
    key_base = jnp.concatenate(
        [
            jnp.where(place >= e, (place - e) * block_len + order * own_count, FAR)
            for e in range(places)
        ]
    )
    base = jnp.concatenate([query_base, key_base])
    need = (key_base[None, None, :] <= query_base[None, :, None] + own_count - 1) & (
        key_base[None, None, :] + own_count - 1 >= begin[:, :, :1]
    )
    need = need.astype(jnp.int32)
    rank = jnp.cumsum(need, axis=2) - need
    blocks = key_base.shape[0]
    spot = jnp.arange(blocks, dtype=jnp.int32)
    chosen = (rank[..., None] == spot) & (need[..., None] > 0)
    listed = jnp.sum(chosen * spot[:, None], axis=2)
    need = jnp.concatenate([jnp.sum(need, axis=2, keepdims=True), listed], axis=2)
    need = need.astype(jnp.int32).reshape(rows, -1)
    begin = begin.reshape(rows, n, 1, own_count)

    gains = norm_gains.astype(F32)
    shifts = shift_vectors.astype(F32)
    packed = [
        pack_layer(
            project_weight[l], project_bias[l], dense_weight[l] if l else None, up_weight[l],
            up_bias[l], down_weight[l], heads,
        )
        for l in range(LAYERS)
    ]
    flat = lambda a: a.reshape(n * tokens, -1)
    by_row = lambda a: a.reshape(n, rows, own_count, -1)
    stack = lambda chunks: jnp.stack(chunks)
    shift_to = lambda v, c: lax.ppermute(v, "tensor", [(s, (s + c) % n) for s in range(n)])
    sent = block_input[:, 0].reshape(tokens, width)
    sent0 = sent
    residual = sent.astype(F32)
    cot = cotangent[:, 0].reshape(tokens, width)

    spare = jnp.zeros((-d_rows % 8, width), BF)
    chunks0 = z_gather(jnp.concatenate([sent, dense_weight[0], spare], axis=0))
    gather_all = lambda v: lax.all_gather(v, ("dp", "ctx"), axis=0, tiled=False)
    gathered = [gather_all(packed[0])]
    gather_z = lambda v: lax.all_gather(v, "tensor", axis=0, tiled=False)
    vecs = [
        jnp.concatenate([gains[l].T, shifts[l].T, jnp.zeros((2, width), F32)], axis=0)
        for l in range(LAYERS)
    ]

    def mix_groups(chunks, l):
        cut = (n + 1) // 2
        tables_of = tables
        xs, first, q, kv_a = mix_pass(
            tokens, chunks[:cut], 0, n, gathered[l], k_rows, m_own, vecs[l], tables_of, heads
        )
        groups = [kv_a]
        if cut < n:
            chunks = chunks[:cut] + list(after(tuple(chunks[cut:]), kv_a))
            xs, first, q, kv_b = mix_pass(
                tokens, chunks[cut:], cut, n, gathered[l], k_rows, m_own, vecs[l], tables_of, heads,
                (xs, first, q),
            )
            groups.append(kv_b)
        groups = [a.reshape(a.shape[0], rows, own_count, wide) for a in groups]
        kvs = [groups] + [
            [lax.ppermute(a, "ctx", [(s, s + e) for s in range(places - e)]) for a in groups]
            for e in range(1, places)
        ]
        return xs, first, by_row(q), kvs, chunks

    chunks0[0] = after(chunks0[0], packed[1], need, base, begin)
    xs0, first0, q0, kvs0, chunks0 = mix_groups(chunks0, 0)
    dense_all = jnp.stack([chunk[tokens : tokens + d_rows] for chunk in chunks0])
    dense_all = gather_all(dense_all)
    second0, active0, slope0, parts = feed_pass(xs0, gathered[0], k_rows, f_own, vecs[0])
    later = gather_all(after(packed[1], parts[0]))
    shares = z_scatter(parts)
    mixed0, ot0, lse0 = attend(need, base, begin, after(q0, parts[0]), kvs0, heads)
    sent_mixed = [after(mixed0[0], *shares)] + mixed0[1:]
    sent_mixed = [sent_mixed[0]] + [shift_to(after(mixed0[c], *shares), c) for c in range(1, n)]
    residual, sent = join(me1, sent_mixed, dense_all, shares, residual, vecs[0])

    chunks1 = z_gather(sent)
    gathered.append(after(later, sent))
    xs1, first1, q1, kvs1, _ = mix_groups(chunks1, 1)
    second1, active1, slope1, parts = feed_pass(xs1, gathered[1], k_rows, f_own, vecs[1])
    cots = gather_z(after(cot.astype(BF), kvs1[0][0]))
    mixed1, ot1, lse1 = attend(need, base, begin, after(q1, parts[0]), kvs1, heads)
    do1, branches = middle(me1, mixed1, gathered[1], k_rows, d_rows, parts, cots)
    shares = z_scatter(branches)
    dq1, dkv1, *send_back = attend_back(need, base, begin, q1, do1, lse1, ot1, kvs1, heads)

    def return_pairs(sends):
        return [
            lax.ppermute(sends[e - 1], "ctx", [(s, s - e) for s in range(e, places)])
            for e in range(1, places)
        ]

    scatter_all = lambda v: lax.psum_scatter(v, ("dp", "ctx"), scatter_dimension=0, tiled=True)[0]

    own_cols = width // (n * shard_count)

    def extra_rows(sums_a):
        bias = unmix_columns(sums_a[2, : 2 * wide], heads).reshape(shard_count, 1, -1)
        return jnp.pad(bias, ((0, 0), (0, 7), (0, width - m_own)))

    def feed_out(total):
        total = total.astype(F32)
        return total[:k_rows], total[-8, :f_own], total[k_rows:-8]

    def mix_out(total):
        total = total.astype(F32)
        return unmix_columns(total[:k_rows], heads), total[-8, :m_own], total[k_rows:-8]

    got1 = return_pairs(send_back)
    cots = after(cots, dq1)
    cots = [lax.dynamic_index_in_dim(cots, (me + c) % n, 0, keepdims=False) for c in range(n)]
    scaled1, sums_b1, feed_g1 = feed_back(
        core1, cots, xs1, slope1, second1, active1, gathered[1], k_rows, vecs[1], places, False
    )
    feed1 = scatter_all(feed_g1)
    shares[0] = after(shares[0], dq1)
    block_output = shares[0].astype(F32)
    for share in shares[1:]:
        block_output = block_output + share.astype(F32)
    block_output = block_output + residual + shifts[1, :, 2] + shifts[1, :, 3]
    scaled1 = after(scaled1, block_output)
    gp1, parts1, sums_a1, _ = exit_pass(
        me1, core1, dq1, dkv1, got1, tables, xs1, gathered[1], k_rows, vecs[1], scaled1, heads, places
    )
    parts1 = z_scatter(parts1)
    rows1 = extra_rows(sums_a1)
    (mix_g1,) = mix_back(core1, first1, gp1, mixed1, cots, rows1, places, False, 30)

    grad, grad_own, token_sum0, *pieces = turn(
        me1, parts1, cot, chunks1[0], dense_all, (mix_g1, feed1)
    )
    do0 = [pieces[0]] + [None] * (n - 1)
    for c in range(1, n):
        do0[n - c] = shift_to(pieces[c], c)
    mix1 = scatter_all(after(mix_g1, *do0))
    gs = z_gather(after(grad_own, *do0))
    dq0, dkv0, *send_back = attend_back(need, base, begin, q0, do0, lse0, ot0, kvs0, heads)
    got0 = return_pairs(send_back)
    scaled0, sums_b0, *feed_g0 = feed_back(
        core1, gs, xs0, slope0, second0, active0, gathered[0], k_rows, vecs[0], places, split,
        (dq0,),
    )
    gp0, (parts0,), sums_a0, mix_g0 = exit_pass(
        me1, core1, dq0, dkv0, got0, tables, xs0, gathered[0], k_rows, vecs[0], scaled0, heads,
        places, 2 if split else 1, [first0] + mixed0 + gs, (mix1,),
    )
    parts0 = [lax.psum_scatter(parts0, "tensor", scatter_dimension=0, tiled=True)[0]]
    small = [
        jnp.stack([sums_a0[0], sums_b0[0], sums_a0[1], sums_b0[1], token_sum0[0]]),
        jnp.stack([sums_a1[0], sums_b1[0], sums_a1[1], sums_b1[1], token_sum0[1]]),
    ]
    sums = jnp.concatenate(small, axis=0).reshape(LAYERS * 5, n, shard_count, own_cols)
    sums = sums.transpose(1, 2, 0, 3)
    if split:
        feed_g0 = after(tuple(feed_g0), gp0)
        up_sum, rest_sum = Scatter(tuple(feed_g0[:2]), False), Scatter(tuple(feed_g0[2:]), True)
        mix_sum = Scatter(mix_g0, False)
        small_sum = Scatter(sums, False, ("tensor", "dp", "ctx"), F32)
        streams = [small_sum, mix_sum, up_sum, rest_sum]
        while mix_sum.order:
            advance(streams)
        (input_grad,) = turn(me1, parts0, grad, sent0)
        advance(streams, input_grad)
        while small_sum.order:
            advance(streams)
        mix0 = mix_out(mix_sum.value)
        feed0 = jnp.concatenate([up_sum.value, rest_sum.value], axis=0)
        total = small_sum.value
    else:
        (input_grad,) = turn(me1, parts0, grad, sent0)
        mix0 = mix_out(scatter_all(mix_g0[0]))
        feed0 = scatter_all(feed_g0[0])
        total = lax.psum_scatter(sums, "tensor", scatter_dimension=0, tiled=False)
        total = scatter_all(total)
    total = total.reshape(LAYERS, 5, own_cols)
    mix1 = mix_out(mix1)
    weight_out = []
    for feed_s, mix_s in ((feed_out(feed0), mix0), (feed_out(feed1), mix1)):
        weight_out.append((mix_s[0], mix_s[1], mix_s[2], feed_s[0], feed_s[1], feed_s[2]))

    gains_out = total[:, :2].transpose(0, 2, 1)
    shifts_out = jnp.stack([total[:, 2], total[:, 3], total[:, 4], total[:, 4]], axis=-1)
    outs = [jnp.stack([weight_out[l][j] for l in range(LAYERS)]) for j in range(6)]
    shape = (rows, 1, own_count, width)
    return (block_output.reshape(shape), input_grad.reshape(shape), *outs, gains_out, shifts_out)


def solution(mesh):
    in_specs = (
        P("dp", "ctx", "tensor", None),
        P("dp", None),
        P(None, ("dp", "ctx"), "tensor"),
        P(None, ("tensor", "dp", "ctx")),
        P(None, ("tensor", "dp", "ctx"), None),
        P(None, ("dp", "ctx"), "tensor"),
        P(None, ("tensor", "dp", "ctx")),
        P(None, ("tensor", "dp", "ctx"), None),
        P(),
        P(),
        P("dp", "ctx", "tensor", None),
    )
    out_specs = (
        P("dp", "ctx", "tensor", None),
        P("dp", "ctx", "tensor", None),
        P(None, ("dp", "ctx"), "tensor"),
        P(None, ("tensor", "dp", "ctx")),
        P(None, ("tensor", "dp", "ctx"), None),
        P(None, ("dp", "ctx"), "tensor"),
        P(None, ("tensor", "dp", "ctx")),
        P(None, ("tensor", "dp", "ctx"), None),
        P(None, ("tensor", "dp", "ctx"), None),
        P(None, ("tensor", "dp", "ctx"), None),
    )
    return jax.shard_map(shards, mesh=mesh, in_specs=in_specs, out_specs=out_specs, check_vma=False)
```

```python
from functools import partial

import jax
import jax.numpy as jnp
from jax import lax
from jax.experimental import pallas as pl
from jax.experimental.pallas import tpu as pltpu
from jax.sharding import PartitionSpec as P

HEAD_DIM = 64
ROTARY = 16
LAYERS = 2
EPSILON = 1e-05
MASKED = -1e30
LANES = 128
SCALE = HEAD_DIM ** (-0.5)
FAR = 1 << 24
BF = jnp.bfloat16
F32 = jnp.float32
NT = (((1,), (1,)), ((), ()))


def dot(a, b):
    return jnp.dot(a, b, preferred_element_type=F32)


def dot_nt(a, b):
    return lax.dot_general(a, b, NT, preferred_element_type=F32)


def cost(micros):
    return pl.CostEstimate(
        flops=int(micros * 1.1e9), transcendentals=0, bytes_accessed=int(micros * 3.6e6)
    )


def params(mib=56):
    return pltpu.CompilerParams(vmem_limit_bytes=mib << 20)


def z_gather(own):
    n = lax.axis_size("tensor")
    return [own] + [
        lax.ppermute(own, "tensor", [(s, (s - c) % n) for s in range(n)]) for c in range(1, n)
    ]


def z_scatter(parts):
    n = lax.axis_size("tensor")
    return [parts[0]] + [
        lax.ppermute(parts[c], "tensor", [(s, (s + c) % n) for s in range(n)]) for c in range(1, n)
    ]


def after(value, *needed):
    return lax.optimization_barrier((value,) + needed)[0]


def bits_of(axis):
    return lax.axis_size(axis).bit_length() - 1


def power_of_two():
    sizes = [lax.axis_size(axis) for axis in ("tensor", "dp", "ctx")]
    return sizes[1] > 1 and all(size & (size - 1) == 0 for size in sizes)


def flip(send, step):
    axis, bit = step
    return lax.ppermute(send, axis, [(s, s ^ (1 << bit)) for s in range(lax.axis_size(axis))])


class Scatter:
    def __init__(self, value, first_y, axes=("dp", "ctx"), wire=BF):
        self.labels = [(axis, b) for axis in axes for b in reversed(range(bits_of(axis)))]
        y_steps = [("dp", b) for b in range(1, bits_of("dp"))]
        x_steps = [("ctx", b) for b in range(bits_of("ctx"))]
        self.order = [("tensor", b) for b in range(bits_of("tensor"))] if "tensor" in axes else []
        self.order += [("dp", 0)] + (y_steps + x_steps if first_y else x_steps + y_steps)
        if not isinstance(value, tuple):
            value = value.reshape((2,) * len(self.labels) + value.shape[len(axes) - 1 :])
        self.value, self.wire = value, wire

    def send(self):
        self.step = self.order.pop(0)
        axis, bit = self.step
        dim = self.labels.index(self.step)
        self.labels.pop(dim)
        if isinstance(self.value, tuple):
            lead = (2,) * len(self.labels)
            out, self.keep = (v.reshape(lead + v.shape[1:]) for v in self.value)
            return out
        mine = (lax.axis_index(axis) >> bit) & 1
        self.keep = lax.dynamic_index_in_dim(self.value, mine, dim, keepdims=False)
        out = lax.dynamic_index_in_dim(self.value, 1 - mine, dim, keepdims=False)
        return out.astype(self.wire)

    def receive(self, got):
        self.value = self.keep + got.astype(F32)


def advance(streams, *needed):
    streams = [stream for stream in streams if stream.order]
    sends = lax.optimization_barrier(tuple(stream.send() for stream in streams) + needed)
    gots = [flip(send, stream.step) for send, stream in zip(sends, streams)]
    for stream, got in zip(streams, gots):
        stream.receive(got)


def rotated(tile, cosine, sine_a, sine_b):
    return tile * cosine + pltpu.roll(tile, LANES - 8, 1) * sine_a + pltpu.roll(tile, 8, 1) * sine_b


def unrotated(tile, cosine, sine_a, sine_b):
    return tile * cosine - pltpu.roll(tile, LANES - 8, 1) * sine_a - pltpu.roll(tile, 8, 1) * sine_b


def unit_of(x):
    values = x.astype(F32)
    centre = values - jnp.mean(values, axis=-1, keepdims=True)
    inverse = lax.rsqrt(jnp.mean(centre * centre, axis=-1, keepdims=True) + EPSILON)
    return centre * inverse


def gathered_row(tail_ref, row, own):
    shards = tail_ref.shape[0]
    return jnp.concatenate(
        [tail_ref[s].astype(F32)[row : row + 1, :own] for s in range(shards)], axis=1
    )


def mix_kernel(n, heads, own, *refs):
    chunk_refs = refs[:n]
    mix_ref, tail_ref, vec_ref, cos_ref, sa_ref, sb_ref = refs[n : n + 6]
    xs_ref, first_ref, q_ref, kv_ref, bias_s = refs[-5:]
    load_chunk(chunk_refs, xs_ref.at[0])
    width = xs_ref.shape[-1]

    @pl.when(pl.program_id(0) == 0)
    def _():
        raw = gathered_row(tail_ref, 1, own)
        size = 3 * HEAD_DIM
        pieces = [raw[:, h * size + HEAD_DIM : (h + 1) * size] for h in range(heads)]
        blank = jnp.zeros((1, HEAD_DIM), F32)
        for h in range(heads):
            pieces += [raw[:, h * size : h * size + HEAD_DIM], blank]
        bias_s[...] = jnp.concatenate(pieces, axis=1)

    first = (unit_of(xs_ref[0]) * vec_ref[0:1] + vec_ref[2:3]).astype(BF)
    first_ref[0] = first
    proj = dot(first, mix_ref[...].reshape(width, -1)[:, : 2 * heads * LANES]) + bias_s[...]
    cosine, sine_a, sine_b = cos_ref[0], sa_ref[0], sb_ref[0]
    for h in range(heads):
        cols = slice(h * LANES, (h + 1) * LANES)
        kv_ref[0, :, cols] = rotated(proj[:, cols], cosine, sine_a, sine_b).astype(BF)
        qcols = slice((heads + h) * LANES, (heads + h + 1) * LANES)
        q_ref[0, :, cols] = (rotated(proj[:, qcols], cosine, sine_a, sine_b) * SCALE).astype(BF)


def store_chunk(refs, value):
    for j, ref in enumerate(refs):

        @pl.when(pl.program_id(0) == j)
        def _(ref=ref):
            ref[...] = value


def load_chunk(refs, held):
    for j, ref in enumerate(refs):

        @pl.when(pl.program_id(0) == j)
        def _(ref=ref):
            held[...] = ref[...]


def feed_kernel(own, *refs):
    x_ref, up_ref, down_ref, tail_ref, vec_ref, second_ref, active_ref, slope_ref = refs[:8]
    part_refs, bias_s = refs[8:-1], refs[-1]

    @pl.when(pl.program_id(0) == 0)
    def _():
        bias_s[...] = gathered_row(tail_ref, 0, own)

    width = x_ref.shape[-1]
    second = (unit_of(x_ref[0]) * vec_ref[1:2] + vec_ref[3:4]).astype(BF)
    second_ref[0] = second
    hidden = dot(second, up_ref[...].reshape(width, -1)) + bias_s[...]
    half = 0.5 * (1.0 + lax.erf(hidden * (0.5**0.5)))
    active = (hidden * half).astype(BF)
    active_ref[0] = active
    bell = jnp.exp(hidden * hidden * -0.5) * 0.3989422804014327
    slope_ref[0] = (half + hidden * bell).astype(BF)
    store_chunk(part_refs, dot(active, down_ref[...].reshape(-1, width)).astype(BF))


def chunk_specs(n, tokens, gathered, k):
    shards, _, ff = gathered.shape
    token = lambda w: pl.BlockSpec((1, tokens, w), lambda c: (c, 0, 0))
    whole = lambda a: pl.BlockSpec(a.shape, lambda c: (0,) * a.ndim)
    weight = lambda j: pl.BlockSpec((shards, k, ff), lambda c: (0, j, 0))
    out = lambda w: jax.ShapeDtypeStruct((n, tokens, w), BF)
    return token, whole, weight, out


def mix_pass(tokens, chunks, place, n, gathered, k, own, vec, tables, heads, held=()):
    width = chunks[0].shape[1]
    count = len(chunks)
    wide = heads * LANES
    shards, _, ff = gathered.shape
    whole = lambda a: pl.BlockSpec(a.shape, lambda c: (0,) * a.ndim)
    token = lambda w: pl.BlockSpec((1, tokens, w), lambda c: (place + c, 0, 0))
    weight = pl.BlockSpec((shards, k, ff), lambda c: (0, 2, 0))
    last = gathered.shape[1] // 8 - 1
    tail = pl.BlockSpec((shards, 8, ff), lambda c: (0, last, 0))
    out = lambda m, w: jax.ShapeDtypeStruct((m, tokens, w), BF)
    first_held = count + 6
    return pl.pallas_call(
        partial(mix_kernel, count, heads, own),
        grid=(count,),
        in_specs=[pl.BlockSpec((tokens, width), lambda c: (0, 0))] * count
        + [weight, tail, whole(vec)]
        + [token(LANES)] * 3
        + [pl.BlockSpec(memory_space=pl.ANY)] * len(held),
        out_specs=[token(width), token(width), token(wide)]
        + [pl.BlockSpec((1, tokens, wide), lambda c: (c, 0, 0))],
        out_shape=[out(n, width), out(n, width), out(n, wide), out(count, wide)],
        input_output_aliases={first_held + i: i for i in range(len(held))},
        scratch_shapes=[pltpu.VMEM((1, 2 * wide), F32)],
        compiler_params=params(),
        cost_estimate=cost(12),
        name="mix_pass",
    )(*chunks, gathered, gathered, vec, *tables, *held)


def feed_pass(xs, gathered, k, own, vec):
    n, tokens, width = xs.shape
    ff = gathered.shape[2]
    token, whole, weight, out = chunk_specs(n, tokens, gathered, k)
    last = gathered.shape[1] // 8 - 1
    second, active, slope, *parts = pl.pallas_call(
        partial(feed_kernel, own),
        grid=(n,),
        in_specs=[token(width), weight(0), weight(1)]
        + [pl.BlockSpec((gathered.shape[0], 8, ff), lambda c: (0, last, 0)), whole(vec)],
        out_specs=[token(width), token(ff), token(ff)]
        + [pl.BlockSpec((tokens, width), lambda c: (0, 0))] * n,
        out_shape=[out(width), out(ff), out(ff)]
        + [jax.ShapeDtypeStruct((tokens, width), BF)] * n,
        scratch_shapes=[pltpu.VMEM((1, ff), F32)],
        compiler_params=params(),
        cost_estimate=cost(20),
        name="feed_pass",
    )(xs, gathered, gathered, gathered, vec)
    return second, active, slope, parts


def middle_kernel(n, me_ref, dense_ref, grads_ref, *refs):
    mixed_refs, part_refs = refs[:n], refs[n : 2 * n]
    do_refs, out_refs = refs[2 * n : 3 * n], refs[3 * n :]
    rows = mixed_refs[0].shape[1] // dense_ref.shape[0]
    dense = dense_ref[:, :rows].reshape(-1, dense_ref.shape[-1])
    for c in range(n):
        total = dot(mixed_refs[c][...], dense) + part_refs[c][...].astype(F32)
        out_refs[c][...] = total.astype(BF)
        grad = grads_ref[lax.rem(me_ref[0] + c, n)]
        do_refs[c][...] = dot_nt(grad, dense).astype(BF)


def middle(me1, mixed, gathered, k, d, parts, grads):
    n = len(parts)
    padded = d + -d % 8
    full = lambda a: pl.BlockSpec(a.shape, lambda i: (0,) * a.ndim)
    dense = pl.BlockSpec(
        (gathered.shape[0], padded, gathered.shape[2]), lambda i: (0, 3 * k // padded, 0)
    )
    outs = pl.pallas_call(
        partial(middle_kernel, n),
        grid=(1,),
        in_specs=[pl.BlockSpec(memory_space=pltpu.SMEM), dense, full(grads)]
        + [full(a) for a in mixed + parts],
        out_specs=[full(a) for a in mixed + parts],
        out_shape=[jax.ShapeDtypeStruct(mixed[0].shape, BF)] * n
        + [jax.ShapeDtypeStruct(parts[0].shape, BF)] * n,
        compiler_params=params(),
        cost_estimate=cost(4),
        name="middle",
    )(me1, gathered, grads, *mixed, *parts)
    return outs[:n], outs[n:]


def load_pairs(kv_refs, kv_s):
    place = 0
    for ref in kv_refs:
        for c in range(ref.shape[0]):
            kv_s[place] = ref[c, 0]
            place += 1


def each_block(plan_ref, row, c, blocks, take):
    start = c * (blocks + 1)
    count = plan_ref[row, start]

    def pair(t, _):
        take([plan_ref[row, start + 1 + 2 * t], plan_ref[row, start + 2 + 2 * t]])
        return 0

    lax.fori_loop(0, count // 2, pair, 0)

    @pl.when(count % 2 == 1)
    def _():
        take([plan_ref[row, start + count]])


def allowed_pairs(base_ref, begin_ref, kb, c, n, shape):
    key_slot = base_ref[n + kb] + lax.broadcasted_iota(jnp.int32, shape, 0)
    query_slot = base_ref[c] + lax.broadcasted_iota(jnp.int32, shape, 1)
    return (key_slot >= begin_ref[0, c]) & (key_slot <= query_slot)


def attend_kernel(heads, extras, groups, need_ref, base_ref, begin_ref, q_ref, *refs):
    kv_refs = refs[:groups]
    n, _, count, _ = q_ref.shape
    mixed_refs = refs[groups : groups + n]
    ot_ref, lse_ref, kv_s, vt_s, top_s, total_s, acc_s, mixed_s = refs[groups + n :]
    blocks = n * (1 + extras)
    row = pl.program_id(0)
    load_pairs(kv_refs, kv_s)

    def turn(kb, _):
        for h in range(heads):
            tile = kv_s[kb, :, h * LANES : (h + 1) * LANES].astype(F32)
            vt_s[kb, h] = tile.T[HEAD_DIM:].astype(BF)
        return 0

    lax.fori_loop(0, blocks, turn, 0)

    def per_query(c, _):
        top_s[...] = jnp.full(top_s.shape, MASKED, F32)
        total_s[...] = jnp.zeros(total_s.shape, F32)
        acc_s[...] = jnp.zeros(acc_s.shape, F32)

        def take(kbs):
            column = lambda h: slice(h * LANES, (h + 1) * LANES)
            held = [
                [dot_nt(kv_s[kb, :, column(h)], q_ref[c, 0, :, column(h)]) for h in range(heads)]
                for kb in kbs
            ]
            masks = [allowed_pairs(base_ref, begin_ref, kb, c, n, (count, count)) for kb in kbs]
            low, fades = [], []
            for h in range(heads):
                scores = [jnp.where(mask, own[h], MASKED) for mask, own in zip(masks, held)]
                old = top_s[h]
                new = old
                for score in scores:
                    new = jnp.maximum(new, jnp.max(score, axis=0, keepdims=True))
                fade = jnp.exp(old - new)
                total = total_s[h] * fade
                weights = []
                for score in scores:
                    weight = jnp.exp(score - new)
                    total = total + jnp.sum(weight, axis=0, keepdims=True)
                    weights.append(weight.astype(BF))
                top_s[h] = new
                total_s[h] = total
                low.append(weights)
                fades.append(fade)
            for h in range(heads):
                acc = acc_s[h] * fades[h]
                for kb, weight in zip(kbs, low[h]):
                    acc = acc + dot(vt_s[kb, h], weight)
                acc_s[h] = acc

        each_block(need_ref, row, c, blocks, take)
        outs = []
        for h in range(heads):
            total = total_s[h]
            outs.append(acc_s[h] / total)
            lse_ref[0, c, h : h + 1] = top_s[h] + jnp.log(total)
        whole = jnp.concatenate(outs, axis=0)
        ot_ref[0, c] = whole
        mixed_s[c] = whole.T.astype(BF)
        return 0

    lax.fori_loop(0, n, per_query, 0)
    for c in range(n):
        mixed_refs[c][0] = mixed_s[c]


def attention_specs(q, kvs):
    n, rows, count, wide = q.shape
    smem = pl.BlockSpec(memory_space=pltpu.SMEM)
    begin = pl.BlockSpec((1, n, 1, count), lambda r: (r, 0, 0, 0))
    tokens = lambda a: pl.BlockSpec((a.shape[0], 1, count, wide), lambda r: (0, r, 0, 0))
    flat = [a for group in kvs for a in group]
    return n, rows, count, wide, smem, begin, tokens, flat


def attend(need, base, begin, q, kvs, heads):
    extras = len(kvs) - 1
    n, rows, count, wide, smem, begin_spec, tokens, flat = attention_specs(q, kvs)
    blocks = n * (1 + extras)
    narrow = heads * HEAD_DIM
    outs = pl.pallas_call(
        partial(attend_kernel, heads, extras, len(flat)),
        grid=(rows,),
        in_specs=[smem, smem, begin_spec, tokens(q)] + [tokens(a) for a in flat],
        out_specs=[pl.BlockSpec((1, count, narrow), lambda r: (r, 0, 0))] * n
        + [
            pl.BlockSpec((1, n, narrow, count), lambda r: (r, 0, 0, 0)),
            pl.BlockSpec((1, n, heads, count), lambda r: (r, 0, 0, 0)),
        ],
        out_shape=[jax.ShapeDtypeStruct((rows, count, narrow), BF)] * n
        + [
            jax.ShapeDtypeStruct((rows, n, narrow, count), F32),
            jax.ShapeDtypeStruct((rows, n, heads, count), F32),
        ],
        scratch_shapes=[
            pltpu.VMEM((blocks, count, wide), BF),
            pltpu.VMEM((blocks, heads, HEAD_DIM, count), BF),
            pltpu.VMEM((heads, 1, count), F32),
            pltpu.VMEM((heads, 1, count), F32),
            pltpu.VMEM((heads, HEAD_DIM, count), F32),
            pltpu.VMEM((n, count, narrow), BF),
        ],
        compiler_params=params(),
        cost_estimate=cost(400),
        name="attend",
    )(need, base, begin, q, *flat)
    return [a.reshape(rows * count, narrow) for a in outs[:n]], outs[n], outs[n + 1]


def attend_back_kernel(heads, extras, groups, need_ref, base_ref, begin_ref, q_ref, *refs):
    n, _, count, _ = q_ref.shape
    do_refs, lse_ref, ot_ref = refs[:n], refs[n], refs[n + 1]
    kv_refs = refs[n + 2 : n + 2 + groups]
    dq_ref = refs[n + 2 + groups]
    dkv_refs = refs[n + 3 + groups : n + 4 + groups + extras]
    kv_s, kt_s, dkv_s, dqt_s, delta_s, do_s, narrow_s = refs[n + 4 + groups + extras :]
    blocks = n * (1 + extras)
    row = pl.program_id(0)
    load_pairs(kv_refs, kv_s)
    for c in range(n):
        narrow_s[c] = do_refs[c][0]

    def turn(kb, _):
        for h in range(heads):
            tile = kv_s[kb, :, h * LANES : (h + 1) * LANES].astype(F32)
            kt_s[kb, h] = tile.T[:HEAD_DIM].astype(BF)
        dkv_s[kb] = jnp.zeros(dkv_s.shape[1:], F32)
        return 0

    lax.fori_loop(0, blocks, turn, 0)

    def per_query(c, _):
        dqt_s[...] = jnp.zeros(dqt_s.shape, F32)
        for h in range(heads):
            cols = slice(h * LANES, (h + 1) * LANES)
            grad = narrow_s[c, :, h * HEAD_DIM : (h + 1) * HEAD_DIM].astype(F32)
            grad = jnp.concatenate([jnp.zeros((count, HEAD_DIM), F32), grad], axis=1)
            do_s[:, cols] = grad.astype(BF)
            dot_t = grad.T[HEAD_DIM:]
            out_t = ot_ref[0, c, h * HEAD_DIM : (h + 1) * HEAD_DIM]
            delta_s[h] = jnp.sum(dot_t * out_t, axis=0, keepdims=True)

        def take(kbs):
            column = lambda h: slice(h * LANES, (h + 1) * LANES)
            queries = [q_ref[c, 0, :, column(h)] for h in range(heads)]
            grads = [do_s[:, column(h)] for h in range(heads)]
            held = []
            for kb in kbs:
                pairs = [kv_s[kb, :, column(h)] for h in range(heads)]
                held.append(
                    [(dot_nt(pairs[h], queries[h]), dot_nt(pairs[h], grads[h])) for h in range(heads)]
                )
            low = []
            for kb, own in zip(kbs, held):
                allowed = allowed_pairs(base_ref, begin_ref, kb, c, n, (count, count))
                for h in range(heads):
                    scores = jnp.where(allowed, own[h][0], MASKED)
                    probs = jnp.exp(scores - lse_ref[0, c, h : h + 1])
                    steps = probs * (own[h][1] - delta_s[h])
                    low.append((steps.astype(BF), probs.astype(BF)))
            for i, kb in enumerate(kbs):
                for h in range(heads):
                    steps, probs = low[i * heads + h]
                    dqt_s[h] += dot(kt_s[kb, h], steps)
                    dkv_s[kb, :, column(h)] += dot(steps, queries[h]) + dot(probs, grads[h])

        each_block(need_ref, row, c, blocks, take)
        for h in range(heads):
            tile = jnp.concatenate([dqt_s[h], jnp.zeros((HEAD_DIM, count), F32)], axis=0)
            dq_ref[c, 0, :, h * LANES : (h + 1) * LANES] = tile.T * SCALE
        return 0

    lax.fori_loop(0, n, per_query, 0)
    for e, ref in enumerate(dkv_refs):
        for c in range(n):
            ref[c, 0] = dkv_s[e * n + c].astype(ref.dtype)


def attend_back(need, base, begin, q, do, lse, ot, kvs, heads):
    extras = len(kvs) - 1
    n, rows, count, wide, smem, begin_spec, tokens, flat = attention_specs(q, kvs)
    blocks = n * (1 + extras)
    narrow = heads * HEAD_DIM
    return pl.pallas_call(
        partial(attend_back_kernel, heads, extras, len(flat)),
        grid=(rows,),
        in_specs=[smem, smem, begin_spec, tokens(q)]
        + [pl.BlockSpec((1, count, narrow), lambda r: (r, 0, 0))] * n
        + [
            pl.BlockSpec((1, n, heads, count), lambda r: (r, 0, 0, 0)),
            pl.BlockSpec((1, n, narrow, count), lambda r: (r, 0, 0, 0)),
        ]
        + [tokens(a) for a in flat],
        out_specs=[tokens(q)] * (2 + extras),
        out_shape=[jax.ShapeDtypeStruct(q.shape, F32)] * 2
        + [jax.ShapeDtypeStruct(q.shape, BF)] * extras,
        scratch_shapes=[
            pltpu.VMEM((blocks, count, wide), BF),
            pltpu.VMEM((blocks, heads, HEAD_DIM, count), BF),
            pltpu.VMEM((blocks, count, wide), F32),
            pltpu.VMEM((heads, HEAD_DIM, count), F32),
            pltpu.VMEM((heads, 1, count), F32),
            pltpu.VMEM((count, wide), BF),
            pltpu.VMEM((n, count, narrow), BF),
        ],
        compiler_params=params(),
        cost_estimate=cost(40),
        name="attend_back",
    )(need, base, begin, q, *[a.reshape(rows, count, narrow) for a in do], lse, ot, *flat)


TN = (((0,), (0,)), ((), ()))


def dot_tn(a, b):
    return lax.dot_general(a, b, TN, preferred_element_type=F32)


def half_shard(place, inner, bit):
    return (place // inner * 2 + bit) * inner + place % inner


def store_shards(refs, core_ref, shards, inner, block):
    if len(refs) == 1:
        for s in range(shards):
            refs[0][s] = block(s)
        return
    mine = core_ref[0]
    for place in range(shards // 2):
        refs[0][place] = block(half_shard(place, inner, 1 - mine))
        refs[1][place] = block(half_shard(place, inner, mine))


def row_block(ref, s, size):
    start = s * size if isinstance(s, int) else pl.multiple_of(s * size, 8)
    return ref[pl.ds(start, size)]


def feed_back_kernel(n, gates, inner, split, core_ref, *refs):
    grad_refs = refs[:n]
    x_ref, slope_ref, second_ref, active_ref, up_ref, down_ref, vec_ref = refs[n : n + 7]
    refs = refs[n + 7 + gates :]
    scaled_ref, sums_ref, outs = refs[0], refs[1], refs[2:-4]
    up_s, down_s, grad_s, tail_s = refs[-4:]
    width = x_ref.shape[-1]
    last = pl.program_id(0) == pl.num_programs(0) - 1

    @pl.when(pl.program_id(0) == 0)
    def _():
        sums_ref[...] = jnp.zeros(sums_ref.shape, F32)
        up_s[...] = jnp.zeros(up_s.shape, F32)
        down_s[...] = jnp.zeros(down_s.shape, F32)

    load_chunk(grad_refs, grad_s)
    down = down_ref[...].reshape(-1, width)
    grad = grad_s[...]
    grad_active = dot_nt(grad, down)
    down_s[...] += dot_tn(active_ref[0], grad)
    grad_hidden = (grad_active * slope_ref[0].astype(F32)).astype(BF)
    grad_second = dot_nt(grad_hidden, up_ref[...].reshape(width, -1))
    unit = unit_of(x_ref[0])
    sums_ref[0:1] += jnp.sum(grad_second * unit, axis=0, keepdims=True)
    sums_ref[1:2] += jnp.sum(grad_second, axis=0, keepdims=True)
    sums_ref[2:3] += jnp.sum(grad_hidden.astype(F32), axis=0, keepdims=True)
    scaled_ref[0] = grad_second * vec_ref[1:2]
    up_s[...] += dot_tn(second_ref[0], grad_hidden)

    @pl.when(last)
    def _():
        shards, k = up_ref.shape[:2]
        f = down_s.shape[0] // shards
        own = up_s.shape[1] // shards
        pad = jnp.zeros((8, width - own), F32)
        for s in range(shards):
            tail = jnp.broadcast_to(sums_ref[2:3, s * own : (s + 1) * own], (8, own))
            tail_s[s] = jnp.concatenate([tail, pad], axis=1)
        up_block = lambda s: row_block(up_s, s, k).astype(BF)
        rest_block = lambda s: jnp.concatenate(
            [row_block(down_s, s, f), tail_s[s]], axis=0
        ).astype(BF)
        if split:
            store_shards(outs[:2], core_ref, shards, inner, up_block)
            store_shards(outs[2:], core_ref, shards, inner, rest_block)
        else:
            store_shards(
                outs, core_ref, shards, inner,
                lambda s: jnp.concatenate([up_block(s), rest_block(s)], axis=0),
            )


def feed_back(core1, gs, xs, slope, second, active, gathered, k, vec, inner, split, gates=()):
    n, tokens, width = xs.shape
    shards, _, ff = gathered.shape
    f = ff // shards
    token, whole, weight, _ = chunk_specs(n, tokens, gathered, k)
    fixed = pl.BlockSpec((8, width), lambda c: (0, 0))
    grads = [(shards, k + f + 8, width)]
    if split:
        grads = [(shards // 2, k, width)] * 2 + [(shards // 2, f + 8, width)] * 2
    return pl.pallas_call(
        partial(feed_back_kernel, n, len(gates), inner, split),
        grid=(n,),
        in_specs=[pl.BlockSpec(memory_space=pltpu.SMEM)]
        + [whole(gs[0])] * n
        + [token(width), token(ff), token(width), token(ff), weight(0), weight(1), fixed]
        + [pl.BlockSpec(memory_space=pl.ANY)] * len(gates),
        out_specs=[token(width), fixed] + [pl.BlockSpec(g, lambda c: (0, 0, 0)) for g in grads],
        scratch_shapes=[
            pltpu.VMEM((width, ff), F32),
            pltpu.VMEM((ff, width), F32),
            pltpu.VMEM((tokens, width), BF),
            pltpu.VMEM((shards, 8, width), F32),
        ],
        out_shape=[
            jax.ShapeDtypeStruct((n, tokens, width), F32),
            jax.ShapeDtypeStruct((8, width), F32),
        ]
        + [jax.ShapeDtypeStruct(g, BF) for g in grads],
        compiler_params=params(),
        cost_estimate=cost(12),
        name="feed_back",
    )(core1, *gs, xs, slope, second, active, gathered, gathered, vec, *gates)


def mix_back_kernel(n, inner, outs, core_ref, *refs):
    first_ref, gp_ref, bias_ref = refs[:3]
    mixed_refs, grad_refs = refs[3 : 3 + n], refs[3 + n : 3 + 2 * n]
    grads_refs = refs[-4 - outs : -4]
    mix_s, dense_s, mixed_s, grad_s = refs[-4:]
    last = pl.program_id(0) == pl.num_programs(0) - 1

    @pl.when(pl.program_id(0) == 0)
    def _():
        mix_s[...] = jnp.zeros(mix_s.shape, F32)
        dense_s[...] = jnp.zeros(dense_s.shape, F32)

    load_chunk(grad_refs, grad_s)
    load_chunk(mixed_refs, mixed_s)
    mix_s[...] += dot_tn(first_ref[0], gp_ref[0])
    dense_s[...] += dot_tn(mixed_s[...], grad_s[...])

    @pl.when(last)
    def _():
        shards = bias_ref.shape[0]
        k = mix_s.shape[0] // shards
        d = dense_s.shape[0] // shards

        def block(s):
            rows = [row_block(mix_s, s, k), row_block(dense_s, s, d), bias_ref[s]]
            return jnp.concatenate(rows, axis=0).astype(BF)

        store_shards(grads_refs, core_ref, shards, inner, block)


def mix_back(core1, first, gp, mixed, gs, bias, inner, split, micros, gates=()):
    n, tokens, width = first.shape
    shards = bias.shape[0]
    narrow = mixed[0].shape[-1]
    token = lambda w: pl.BlockSpec((1, tokens, w), lambda c: (c, 0, 0))
    whole = lambda a: pl.BlockSpec(a.shape, lambda c: (0,) * a.ndim)
    count = 2 if split else 1
    grads = (shards // count, width // shards + narrow // shards + 8, width)
    return pl.pallas_call(
        partial(mix_back_kernel, n, inner, count),
        grid=(n,),
        in_specs=[pl.BlockSpec(memory_space=pltpu.SMEM), token(width), token(gp.shape[-1]), whole(bias)]
        + [whole(mixed[0])] * n
        + [whole(gs[0])] * n
        + [pl.BlockSpec(memory_space=pl.ANY)] * len(gates),
        out_specs=[pl.BlockSpec(grads, lambda c: (0, 0, 0))] * count,
        scratch_shapes=[
            pltpu.VMEM((width, gp.shape[-1]), F32),
            pltpu.VMEM((narrow, width), F32),
            pltpu.VMEM((tokens, narrow), BF),
            pltpu.VMEM((tokens, width), BF),
        ],
        out_shape=[jax.ShapeDtypeStruct(grads, BF)] * count,
        compiler_params=params(),
        cost_estimate=cost(micros),
        name="mix_back",
    )(core1, first, gp, bias, *mixed, *gs, *gates)


def join_kernel(n, me_ref, dense_ref, residual_ref, vec_ref, *refs):
    mixed_refs, share_refs, out_ref, sent_ref = refs[:n], refs[n : 2 * n], refs[2 * n], refs[2 * n + 1]
    total = residual_ref[...] + vec_ref[4:5] + vec_ref[5:6]
    for c in range(n):
        rows = dense_ref[:, (n - c) % n]
        rows = rows.reshape(-1, rows.shape[-1])
        total = total + share_refs[c][...].astype(F32) + dot(mixed_refs[c][...], rows)
    out_ref[...] = total
    sent_ref[...] = total.astype(BF)


def join(me1, mixed, dense_all, shares, residual, vec):
    shape = residual.shape
    vmem = pl.BlockSpec(memory_space=pltpu.VMEM)
    return pl.pallas_call(
        partial(join_kernel, len(shares)),
        in_specs=[pl.BlockSpec(memory_space=pltpu.SMEM)] + [vmem] * (3 + 2 * len(shares)),
        out_specs=[vmem, vmem],
        out_shape=[jax.ShapeDtypeStruct(shape, F32), jax.ShapeDtypeStruct(shape, BF)],
        compiler_params=params(),
        cost_estimate=cost(3),
        name="join",
    )(me1, dense_all, residual, vec, *mixed, *shares)


def turn_kernel(n, gates, me_ref, *refs):
    summed = refs[0][...].astype(F32)
    for ref in refs[1:n]:
        summed = summed + ref[...].astype(F32)
    grad_ref, x_ref = refs[n : n + 2]
    refs = refs[n + 2 :]
    values = x_ref[...].astype(F32)
    centre = values - jnp.mean(values, axis=-1, keepdims=True)
    inverse = lax.rsqrt(jnp.mean(centre * centre, axis=-1, keepdims=True) + EPSILON)
    unit = centre * inverse
    mean_s = jnp.mean(summed, axis=-1, keepdims=True)
    mean_su = jnp.mean(summed * unit, axis=-1, keepdims=True)
    grad = grad_ref[...] + inverse * (summed - mean_s - unit * mean_su)
    if len(refs) == gates + 1:
        refs[-1][...] = grad
        return
    dense_ref, out_ref, sent_ref, sums_ref = refs[0], *refs[gates + 1 : gates + 4]
    piece_refs = refs[gates + 4 :]
    out_ref[...] = grad
    sent = grad.astype(BF)
    sent_ref[...] = sent
    for c, piece_ref in enumerate(piece_refs):
        rows = dense_ref[:, c]
        piece_ref[...] = dot_nt(sent, rows.reshape(-1, rows.shape[-1])).astype(BF)
    sums_ref[0:1] = jnp.sum(grad, axis=0, keepdims=True)
    sums_ref[1:2] = jnp.sum(grad_ref[...], axis=0, keepdims=True)


def turn(me1, parts, grad, x_own, dense_all=None, gates=()):
    shape = grad.shape
    outs = [jax.ShapeDtypeStruct(shape, F32)]
    vmem = pl.BlockSpec(memory_space=pltpu.VMEM)
    more = []
    if dense_all is not None:
        more = [dense_all]
        outs += [jax.ShapeDtypeStruct(shape, BF), jax.ShapeDtypeStruct((8, shape[1]), F32)]
        narrow = dense_all.shape[0] * dense_all.shape[2]
        outs += [jax.ShapeDtypeStruct((shape[0], narrow), BF)] * dense_all.shape[1]
    return pl.pallas_call(
        partial(turn_kernel, len(parts), len(gates)),
        in_specs=[pl.BlockSpec(memory_space=pltpu.SMEM)]
        + [vmem] * (len(parts) + 2 + len(more))
        + [pl.BlockSpec(memory_space=pl.ANY)] * len(gates),
        out_specs=[vmem] * len(outs),
        out_shape=outs,
        compiler_params=params(),
        cost_estimate=cost(3),
        name="turn",
    )(me1, *parts, grad, x_own, *more, *gates)


def exit_kernel(n, heads, extras, gates, inner, outs, halves, _, core_ref, dq_ref, dkv_ref, *refs):
    got_refs = refs[:extras]
    cos_ref, sa_ref, sb_ref, x_ref, mix_ref, vec_ref, scaled_ref = refs[extras : extras + 7]
    refs = refs[extras + 7 :]
    fold = halves > 0
    if fold:
        first_ref, mixed_refs, grad_refs = refs[0], refs[1 : 1 + n], refs[1 + n : 1 + 2 * n]
        refs = refs[1 + 2 * n :]
    refs = refs[gates:]
    gp_ref, sums_ref, part_refs = refs[0], refs[1], refs[2 : 2 + outs]
    grads_refs, scratch = refs[2 + outs : 2 + outs + halves], refs[2 + outs + halves :]
    width = x_ref.shape[-1]

    @pl.when(pl.program_id(0) == 0)
    def _():
        sums_ref[...] = jnp.zeros(sums_ref.shape, F32)
        if fold:
            scratch[0][...] = jnp.zeros(scratch[0].shape, F32)
            scratch[1][...] = jnp.zeros(scratch[1].shape, F32)

    if fold:
        mix_s, dense_s, mixed_s, grad_s, tail_s = scratch
        load_chunk(grad_refs, grad_s)
        load_chunk(mixed_refs, mixed_s)
        dense_s[...] += dot_tn(mixed_s[...], grad_s[...])
    cosine, sine_a, sine_b = cos_ref[0], sa_ref[0], sb_ref[0]
    for h in range(heads):
        cols = slice(h * LANES, (h + 1) * LANES)
        pair = dkv_ref[0, :, cols]
        for ref in got_refs:
            pair = pair + ref[0, :, cols].astype(F32)
        gp_ref[0, :, cols] = unrotated(pair, cosine, sine_a, sine_b).astype(BF)
        qcols = slice((heads + h) * LANES, (heads + h + 1) * LANES)
        gp_ref[0, :, qcols] = unrotated(dq_ref[0, :, cols], cosine, sine_a, sine_b).astype(BF)
    gp = gp_ref[0]
    grad_first = dot_nt(gp, mix_ref[...].reshape(width, -1))
    if fold:
        mix_s[...] += dot_tn(first_ref[0], gp)
    unit = unit_of(x_ref[0])
    sums_ref[0:1] += jnp.sum(grad_first * unit, axis=0, keepdims=True)
    sums_ref[1:2] += jnp.sum(grad_first, axis=0, keepdims=True)
    sums_ref[2:3] += jnp.sum(gp.astype(F32), axis=0, keepdims=True)
    part = (grad_first * vec_ref[0:1] + scaled_ref[0]).astype(BF)
    if outs == 1:
        part_refs[0][0] = part
    else:
        store_chunk(part_refs, part)
    if not fold:
        return

    @pl.when(pl.program_id(0) == pl.num_programs(0) - 1)
    def _():
        shards = mix_ref.shape[0]
        k = mix_s.shape[0] // shards
        d = dense_s.shape[0] // shards
        row = sums_ref[2:3]
        pieces = []
        for h in range(heads):
            query = (heads + h) * LANES
            pieces.append(row[:, query : query + HEAD_DIM])
            pieces.append(row[:, h * LANES : (h + 1) * LANES])
        raw = jnp.concatenate(pieces, axis=1)
        own = raw.shape[1] // shards
        pad = jnp.zeros((8, width - own), F32)
        for s in range(shards):
            tail = jnp.broadcast_to(raw[:, s * own : (s + 1) * own], (8, own))
            tail_s[s] = jnp.concatenate([tail, pad], axis=1)

        def block(s):
            rows = [row_block(mix_s, s, k), row_block(dense_s, s, d), tail_s[s]]
            return jnp.concatenate(rows, axis=0).astype(BF)

        store_shards(grads_refs, core_ref, shards, inner, block)


def exit_pass(
    me1, core1, dq, dkv, got, tables, xs, gathered, k, vec, scaled, heads, inner, halves=0,
    fold=(), gates=(),
):
    n, tokens, width = xs.shape
    shards, _, ff = gathered.shape
    wide = heads * LANES
    narrow = heads * HEAD_DIM
    token = lambda w: pl.BlockSpec((1, tokens, w), lambda c, s: (c, 0, 0))
    weight = lambda j: pl.BlockSpec((shards, k, ff), lambda c, s: (0, j, 0))
    whole = lambda a: pl.BlockSpec(a.shape, lambda c, s: (0,) * a.ndim)
    fixed = pl.BlockSpec((8, width), lambda c, s: (0, 0))
    flat = lambda a: a.reshape(n, tokens, wide)
    fold_specs, grad_specs, grad_shapes, scratch = [], [], [], []
    if halves:
        part_specs = [pl.BlockSpec((1, tokens, width), lambda c, s: ((s[0] + c) % n, 0, 0))]
        part_shapes = [jax.ShapeDtypeStruct((n, tokens, width), BF)]
        fold_specs = [token(width)] + [whole(a) for a in fold[1:]]
        grads = (shards // halves, width // shards + narrow // shards + 8, width)
        grad_specs = [pl.BlockSpec(grads, lambda c, s: (0, 0, 0))] * halves
        grad_shapes = [jax.ShapeDtypeStruct(grads, BF)] * halves
        scratch = [
            pltpu.VMEM((width, 2 * wide), F32),
            pltpu.VMEM((narrow, width), F32),
            pltpu.VMEM((tokens, narrow), BF),
            pltpu.VMEM((tokens, width), BF),
            pltpu.VMEM((shards, 8, width), F32),
        ]
    else:
        part_specs = [pl.BlockSpec((tokens, width), lambda c, s: (0, 0))] * n
        part_shapes = [jax.ShapeDtypeStruct((tokens, width), BF)] * n
    outs = len(part_specs)
    gp, sums, *rest = pl.pallas_call(
        partial(exit_kernel, n, heads, len(got), len(gates), inner, outs, halves),
        grid_spec=pltpu.PrefetchScalarGridSpec(
            num_scalar_prefetch=1,
            grid=(n,),
            in_specs=[pl.BlockSpec(memory_space=pltpu.SMEM)]
            + [token(wide)] * (2 + len(got))
            + [token(LANES)] * 3
            + [token(width), weight(2), fixed, token(width)]
            + fold_specs
            + [pl.BlockSpec(memory_space=pl.ANY)] * len(gates),
            out_specs=[token(2 * wide), fixed] + part_specs + grad_specs,
            scratch_shapes=scratch,
        ),
        out_shape=[
            jax.ShapeDtypeStruct((n, tokens, 2 * wide), BF),
            jax.ShapeDtypeStruct((8, width), F32),
        ]
        + part_shapes
        + grad_shapes,
        compiler_params=params(),
        cost_estimate=cost(100),
        name="exit_pass",
    )(
        me1, core1, flat(dq), flat(dkv), *[flat(a) for a in got], *tables, xs, gathered, vec,
        scaled, *fold, *gates,
    )
    return gp, rest[:outs], sums, tuple(rest[outs:])


def mix_columns(weight, heads):
    lead = weight.shape[:-1]
    split = weight.reshape(lead + (heads, 3, HEAD_DIM))
    pairs = split[..., 1:, :].reshape(lead + (heads * LANES,))
    query = jnp.concatenate([split[..., 0, :], jnp.zeros_like(split[..., 0, :])], axis=-1)
    return jnp.concatenate([pairs, query.reshape(lead + (heads * LANES,))], axis=-1)


def unmix_columns(grad, heads):
    lead = grad.shape[:-1]
    split = grad.reshape(lead + (2, heads, 2, HEAD_DIM))
    order = [split[..., 1, :, 0, :], split[..., 0, :, 0, :], split[..., 0, :, 1, :]]
    return jnp.stack(order, axis=-2).reshape(lead + (heads * 3 * HEAD_DIM,))


def pack_layer(mix_w, mix_b, dense_w, up_w, up_b, down_w, heads):
    width = up_w.shape[1]
    mix = mix_columns(mix_w, heads)
    wide = lambda v: jnp.pad(v, (0, width - v.shape[0]))[None]
    rows = [up_w, down_w, jnp.pad(mix, ((0, 0), (0, width - mix.shape[1])))]
    if dense_w is not None:
        rows += [dense_w, jnp.zeros((-dense_w.shape[0] % 8, width), up_w.dtype)]
    rows += [wide(up_b), wide(mix_b), jnp.zeros((6, width), up_w.dtype)]
    return jnp.concatenate(rows, axis=0)


def shards(
    block_input, seq_lengths, project_weight, project_bias, dense_weight, up_weight, up_bias,
    down_weight, norm_gains, shift_vectors, cotangent,
):
    rows, _, own_count, width = block_input.shape
    n = lax.axis_size("tensor")
    places = lax.axis_size("ctx")
    extras = places - 1
    place = lax.axis_index("ctx")
    me = lax.axis_index("tensor")
    me1 = me.reshape(1)
    core1 = (lax.axis_index("dp") & 1).reshape(1)
    split = power_of_two()
    block_len = own_count * n
    tokens = rows * own_count
    heads = project_weight.shape[2] // (3 * HEAD_DIM)
    wide = heads * LANES
    k_rows = up_weight.shape[1]
    d_rows = dense_weight.shape[1]
    f_own = up_bias.shape[1]
    m_own = project_bias.shape[1]
    shard_count = lax.axis_size("dp") * places

    ends = jnp.cumsum(seq_lengths, axis=1)
    order = (me + jnp.arange(n, dtype=jnp.int32)) % n
    query_base = place * block_len + order * own_count
    slots = query_base[:, None] + jnp.arange(own_count, dtype=jnp.int32)[None]
    passed = (ends[:, None, None, :] <= slots[None, :, :, None]).astype(jnp.int32)
    begin = jnp.sum(passed * seq_lengths[:, None, None, :], axis=3)
    position = (slots[None] - begin).transpose(1, 0, 2).reshape(-1)
    frequency = 1.0 / 10000.0 ** (jnp.arange(0, ROTARY, 2, dtype=F32) / ROTARY)
    angle = frequency[:, None] * position.astype(F32)[None, :]
    cosine, sine = lax.optimization_barrier((jnp.cos(angle), jnp.sin(angle)))
    cosine, sine = cosine.T, sine.T
    ones = jnp.ones((cosine.shape[0], LANES - ROTARY), F32)
    zero8 = jnp.zeros_like(sine)
    tables = (
        jnp.concatenate([cosine, cosine, ones], axis=1).reshape(n, tokens, LANES),
        jnp.concatenate([-sine, zero8, ones * 0.0], axis=1).reshape(n, tokens, LANES),
        jnp.concatenate([zero8, sine, ones * 0.0], axis=1).reshape(n, tokens, LANES),
    )
    key_base = jnp.concatenate(
        [
            jnp.where(place >= e, (place - e) * block_len + order * own_count, FAR)
            for e in range(places)
        ]
    )
    base = jnp.concatenate([query_base, key_base])
    need = (key_base[None, None, :] <= query_base[None, :, None] + own_count - 1) & (
        key_base[None, None, :] + own_count - 1 >= begin[:, :, :1]
    )
    need = need.astype(jnp.int32)
    rank = jnp.cumsum(need, axis=2) - need
    blocks = key_base.shape[0]
    spot = jnp.arange(blocks, dtype=jnp.int32)
    chosen = (rank[..., None] == spot) & (need[..., None] > 0)
    listed = jnp.sum(chosen * spot[:, None], axis=2)
    need = jnp.concatenate([jnp.sum(need, axis=2, keepdims=True), listed], axis=2)
    need = need.astype(jnp.int32).reshape(rows, -1)
    begin = begin.reshape(rows, n, 1, own_count)

    gains = norm_gains.astype(F32)
    shifts = shift_vectors.astype(F32)
    packed = [
        pack_layer(
            project_weight[l], project_bias[l], dense_weight[l] if l else None, up_weight[l],
            up_bias[l], down_weight[l], heads,
        )
        for l in range(LAYERS)
    ]
    flat = lambda a: a.reshape(n * tokens, -1)
    by_row = lambda a: a.reshape(n, rows, own_count, -1)
    stack = lambda chunks: jnp.stack(chunks)
    shift_to = lambda v, c: lax.ppermute(v, "tensor", [(s, (s + c) % n) for s in range(n)])
    sent = block_input[:, 0].reshape(tokens, width)
    sent0 = sent
    residual = sent.astype(F32)
    cot = cotangent[:, 0].reshape(tokens, width)

    spare = jnp.zeros((-d_rows % 8, width), BF)
    chunks0 = z_gather(jnp.concatenate([sent, dense_weight[0], spare], axis=0))
    gather_all = lambda v: lax.all_gather(v, ("dp", "ctx"), axis=0, tiled=False)
    gathered = [gather_all(packed[0])]
    gather_z = lambda v: lax.all_gather(v, "tensor", axis=0, tiled=False)
    vecs = [
        jnp.concatenate([gains[l].T, shifts[l].T, jnp.zeros((2, width), F32)], axis=0)
        for l in range(LAYERS)
    ]

    def mix_groups(chunks, l):
        cut = (n + 1) // 2
        tables_of = tables
        xs, first, q, kv_a = mix_pass(
            tokens, chunks[:cut], 0, n, gathered[l], k_rows, m_own, vecs[l], tables_of, heads
        )
        groups = [kv_a]
        if cut < n:
            chunks = chunks[:cut] + list(after(tuple(chunks[cut:]), kv_a))
            xs, first, q, kv_b = mix_pass(
                tokens, chunks[cut:], cut, n, gathered[l], k_rows, m_own, vecs[l], tables_of, heads,
                (xs, first, q),
            )
            groups.append(kv_b)
        groups = [a.reshape(a.shape[0], rows, own_count, wide) for a in groups]
        kvs = [groups] + [
            [lax.ppermute(a, "ctx", [(s, s + e) for s in range(places - e)]) for a in groups]
            for e in range(1, places)
        ]
        return xs, first, by_row(q), kvs, chunks

    chunks0[0] = after(chunks0[0], packed[1], need, base, begin)
    xs0, first0, q0, kvs0, chunks0 = mix_groups(chunks0, 0)
    dense_all = jnp.stack([chunk[tokens : tokens + d_rows] for chunk in chunks0])
    dense_all = gather_all(dense_all)
    second0, active0, slope0, parts = feed_pass(xs0, gathered[0], k_rows, f_own, vecs[0])
    later = gather_all(after(packed[1], parts[0]))
    shares = z_scatter(parts)
    mixed0, ot0, lse0 = attend(need, base, begin, after(q0, parts[0]), kvs0, heads)
    sent_mixed = [after(mixed0[0], *shares)] + mixed0[1:]
    sent_mixed = [sent_mixed[0]] + [shift_to(after(mixed0[c], *shares), c) for c in range(1, n)]
    residual, sent = join(me1, sent_mixed, dense_all, shares, residual, vecs[0])

    chunks1 = z_gather(sent)
    gathered.append(after(later, sent))
    xs1, first1, q1, kvs1, _ = mix_groups(chunks1, 1)
    second1, active1, slope1, parts = feed_pass(xs1, gathered[1], k_rows, f_own, vecs[1])
    cots = gather_z(after(cot.astype(BF), kvs1[0][0]))
    mixed1, ot1, lse1 = attend(need, base, begin, after(q1, parts[0]), kvs1, heads)
    do1, branches = middle(me1, mixed1, gathered[1], k_rows, d_rows, parts, cots)
    shares = z_scatter(branches)
    dq1, dkv1, *send_back = attend_back(need, base, begin, q1, do1, lse1, ot1, kvs1, heads)

    def return_pairs(sends):
        return [
            lax.ppermute(sends[e - 1], "ctx", [(s, s - e) for s in range(e, places)])
            for e in range(1, places)
        ]

    scatter_all = lambda v: lax.psum_scatter(v, ("dp", "ctx"), scatter_dimension=0, tiled=True)[0]

    own_cols = width // (n * shard_count)

    def extra_rows(sums_a):
        bias = unmix_columns(sums_a[2, : 2 * wide], heads).reshape(shard_count, 1, -1)
        return jnp.pad(bias, ((0, 0), (0, 7), (0, width - m_own)))

    def feed_out(total):
        total = total.astype(F32)
        return total[:k_rows], total[-8, :f_own], total[k_rows:-8]

    def mix_out(total):
        total = total.astype(F32)
        return unmix_columns(total[:k_rows], heads), total[-8, :m_own], total[k_rows:-8]

    got1 = return_pairs(send_back)
    cots = after(cots, dq1)
    cots = [lax.dynamic_index_in_dim(cots, (me + c) % n, 0, keepdims=False) for c in range(n)]
    scaled1, sums_b1, feed_g1 = feed_back(
        core1, cots, xs1, slope1, second1, active1, gathered[1], k_rows, vecs[1], places, False
    )
    feed1 = scatter_all(feed_g1)
    shares[0] = after(shares[0], dq1)
    block_output = shares[0].astype(F32)
    for share in shares[1:]:
        block_output = block_output + share.astype(F32)
    block_output = block_output + residual + shifts[1, :, 2] + shifts[1, :, 3]
    scaled1 = after(scaled1, block_output)
    gp1, parts1, sums_a1, _ = exit_pass(
        me1, core1, dq1, dkv1, got1, tables, xs1, gathered[1], k_rows, vecs[1], scaled1, heads, places
    )
    parts1 = z_scatter(parts1)
    rows1 = extra_rows(sums_a1)
    (mix_g1,) = mix_back(core1, first1, gp1, mixed1, cots, rows1, places, False, 30)

    grad, grad_own, token_sum0, *pieces = turn(
        me1, parts1, cot, chunks1[0], dense_all, (mix_g1, feed1)
    )
    do0 = [pieces[0]] + [None] * (n - 1)
    for c in range(1, n):
        do0[n - c] = shift_to(pieces[c], c)
    mix1 = scatter_all(after(mix_g1, *do0))
    gs = z_gather(after(grad_own, *do0))
    dq0, dkv0, *send_back = attend_back(need, base, begin, q0, do0, lse0, ot0, kvs0, heads)
    got0 = return_pairs(send_back)
    scaled0, sums_b0, *feed_g0 = feed_back(
        core1, gs, xs0, slope0, second0, active0, gathered[0], k_rows, vecs[0], places, split,
        (dq0,),
    )
    gp0, (parts0,), sums_a0, mix_g0 = exit_pass(
        me1, core1, dq0, dkv0, got0, tables, xs0, gathered[0], k_rows, vecs[0], scaled0, heads,
        places, 2 if split else 1, [first0] + mixed0 + gs, (mix1,),
    )
    parts0 = [lax.psum_scatter(parts0, "tensor", scatter_dimension=0, tiled=True)[0]]
    small = [
        jnp.stack([sums_a0[0], sums_b0[0], sums_a0[1], sums_b0[1], token_sum0[0]]),
        jnp.stack([sums_a1[0], sums_b1[0], sums_a1[1], sums_b1[1], token_sum0[1]]),
    ]
    sums = jnp.concatenate(small, axis=0).reshape(LAYERS * 5, n, shard_count, own_cols)
    sums = sums.transpose(1, 2, 0, 3)
    if split:
        feed_g0 = after(tuple(feed_g0), gp0)
        up_sum, rest_sum = Scatter(tuple(feed_g0[:2]), False), Scatter(tuple(feed_g0[2:]), True)
        mix_sum = Scatter(mix_g0, False)
        picks = [lax.dynamic_index_in_dim(sums, (me + c) % n, 0, keepdims=False) for c in range(n)]
        total = picks[0]
        for c in range(1, n):
            total = total + shift_to(picks[c], c)
        advance([mix_sum, up_sum, rest_sum])
        small_sum = Scatter(total, False, wire=F32)
        streams = [small_sum, mix_sum, up_sum, rest_sum]
        while mix_sum.order:
            advance(streams)
        (input_grad,) = turn(me1, parts0, grad, sent0)
        advance(streams, input_grad)
        while small_sum.order:
            advance(streams)
        mix0 = mix_out(mix_sum.value)
        feed0 = jnp.concatenate([up_sum.value, rest_sum.value], axis=0)
        total = small_sum.value
    else:
        (input_grad,) = turn(me1, parts0, grad, sent0)
        mix0 = mix_out(scatter_all(mix_g0[0]))
        feed0 = scatter_all(feed_g0[0])
        total = lax.psum_scatter(sums, "tensor", scatter_dimension=0, tiled=False)
        total = scatter_all(total)
    total = total.reshape(LAYERS, 5, own_cols)
    mix1 = mix_out(mix1)
    weight_out = []
    for feed_s, mix_s in ((feed_out(feed0), mix0), (feed_out(feed1), mix1)):
        weight_out.append((mix_s[0], mix_s[1], mix_s[2], feed_s[0], feed_s[1], feed_s[2]))

    gains_out = total[:, :2].transpose(0, 2, 1)
    shifts_out = jnp.stack([total[:, 2], total[:, 3], total[:, 4], total[:, 4]], axis=-1)
    outs = [jnp.stack([weight_out[l][j] for l in range(LAYERS)]) for j in range(6)]
    shape = (rows, 1, own_count, width)
    return (block_output.reshape(shape), input_grad.reshape(shape), *outs, gains_out, shifts_out)


def solution(mesh):
    in_specs = (
        P("dp", "ctx", "tensor", None),
        P("dp", None),
        P(None, ("dp", "ctx"), "tensor"),
        P(None, ("tensor", "dp", "ctx")),
        P(None, ("tensor", "dp", "ctx"), None),
        P(None, ("dp", "ctx"), "tensor"),
        P(None, ("tensor", "dp", "ctx")),
        P(None, ("tensor", "dp", "ctx"), None),
        P(),
        P(),
        P("dp", "ctx", "tensor", None),
    )
    out_specs = (
        P("dp", "ctx", "tensor", None),
        P("dp", "ctx", "tensor", None),
        P(None, ("dp", "ctx"), "tensor"),
        P(None, ("tensor", "dp", "ctx")),
        P(None, ("tensor", "dp", "ctx"), None),
        P(None, ("dp", "ctx"), "tensor"),
        P(None, ("tensor", "dp", "ctx")),
        P(None, ("tensor", "dp", "ctx"), None),
        P(None, ("tensor", "dp", "ctx"), None),
        P(None, ("tensor", "dp", "ctx"), None),
    )
    return jax.shard_map(shards, mesh=mesh, in_specs=in_specs, out_specs=out_specs, check_vma=False)
```

```python
from functools import partial

import jax
import jax.numpy as jnp
from jax import lax
from jax.experimental import pallas as pl
from jax.experimental.pallas import tpu as pltpu
from jax.sharding import PartitionSpec as P

HEAD_DIM = 64
ROTARY = 16
LAYERS = 2
EPSILON = 1e-05
MASKED = -1e30
LANES = 128
SCALE = HEAD_DIM ** (-0.5)
FAR = 1 << 24
BF = jnp.bfloat16
F32 = jnp.float32
NT = (((1,), (1,)), ((), ()))


def dot(a, b):
    return jnp.dot(a, b, preferred_element_type=F32)


def dot_nt(a, b):
    return lax.dot_general(a, b, NT, preferred_element_type=F32)


def cost(micros):
    return pl.CostEstimate(
        flops=int(micros * 1.1e9), transcendentals=0, bytes_accessed=int(micros * 3.6e6)
    )


def params(mib=56):
    return pltpu.CompilerParams(vmem_limit_bytes=mib << 20)


def z_gather(own):
    n = lax.axis_size("tensor")
    return [own] + [
        lax.ppermute(own, "tensor", [(s, (s - c) % n) for s in range(n)]) for c in range(1, n)
    ]


def z_scatter(parts):
    n = lax.axis_size("tensor")
    return [parts[0]] + [
        lax.ppermute(parts[c], "tensor", [(s, (s + c) % n) for s in range(n)]) for c in range(1, n)
    ]


def after(value, *needed):
    return lax.optimization_barrier((value,) + needed)[0]


def bits_of(axis):
    return lax.axis_size(axis).bit_length() - 1


def power_of_two():
    sizes = [lax.axis_size(axis) for axis in ("tensor", "dp", "ctx")]
    return sizes[1] > 1 and all(size & (size - 1) == 0 for size in sizes)


def flip(send, step):
    axis, bit = step
    return lax.ppermute(send, axis, [(s, s ^ (1 << bit)) for s in range(lax.axis_size(axis))])


class Scatter:
    def __init__(self, value, first_y, axes=("dp", "ctx"), wire=BF):
        self.labels = [(axis, b) for axis in axes for b in reversed(range(bits_of(axis)))]
        y_steps = [("dp", b) for b in range(1, bits_of("dp"))]
        x_steps = [("ctx", b) for b in range(bits_of("ctx"))]
        self.order = [("tensor", b) for b in range(bits_of("tensor"))] if "tensor" in axes else []
        self.order += [("dp", 0)] + (y_steps + x_steps if first_y else x_steps + y_steps)
        if not isinstance(value, tuple):
            value = value.reshape((2,) * len(self.labels) + value.shape[len(axes) - 1 :])
        self.value, self.wire = value, wire

    def send(self):
        self.step = self.order.pop(0)
        axis, bit = self.step
        dim = self.labels.index(self.step)
        self.labels.pop(dim)
        if isinstance(self.value, tuple):
            lead = (2,) * len(self.labels)
            out, self.keep = (v.reshape(lead + v.shape[1:]) for v in self.value)
            return out
        mine = (lax.axis_index(axis) >> bit) & 1
        self.keep = lax.dynamic_index_in_dim(self.value, mine, dim, keepdims=False)
        out = lax.dynamic_index_in_dim(self.value, 1 - mine, dim, keepdims=False)
        return out.astype(self.wire)

    def receive(self, got):
        self.value = self.keep + got.astype(F32)


def advance(streams, *needed):
    streams = [stream for stream in streams if stream.order]
    sends = lax.optimization_barrier(tuple(stream.send() for stream in streams) + needed)
    gots = [flip(send, stream.step) for send, stream in zip(sends, streams)]
    for stream, got in zip(streams, gots):
        stream.receive(got)


def rotated(tile, cosine, sine_a, sine_b):
    return tile * cosine + pltpu.roll(tile, LANES - 8, 1) * sine_a + pltpu.roll(tile, 8, 1) * sine_b


def unrotated(tile, cosine, sine_a, sine_b):
    return tile * cosine - pltpu.roll(tile, LANES - 8, 1) * sine_a - pltpu.roll(tile, 8, 1) * sine_b


def unit_of(x):
    values = x.astype(F32)
    centre = values - jnp.mean(values, axis=-1, keepdims=True)
    inverse = lax.rsqrt(jnp.mean(centre * centre, axis=-1, keepdims=True) + EPSILON)
    return centre * inverse


def gathered_row(tail_ref, row, own):
    shards = tail_ref.shape[0]
    return jnp.concatenate(
        [tail_ref[s].astype(F32)[row : row + 1, :own] for s in range(shards)], axis=1
    )


def mix_kernel(n, heads, own, *refs):
    chunk_refs = refs[:n]
    mix_ref, tail_ref, vec_ref, cos_ref, sa_ref, sb_ref = refs[n : n + 6]
    xs_ref, first_ref, q_ref, kv_ref, bias_s = refs[-5:]
    load_chunk(chunk_refs, xs_ref.at[0])
    width = xs_ref.shape[-1]

    @pl.when(pl.program_id(0) == 0)
    def _():
        raw = gathered_row(tail_ref, 1, own)
        size = 3 * HEAD_DIM
        pieces = [raw[:, h * size + HEAD_DIM : (h + 1) * size] for h in range(heads)]
        blank = jnp.zeros((1, HEAD_DIM), F32)
        for h in range(heads):
            pieces += [raw[:, h * size : h * size + HEAD_DIM], blank]
        bias_s[...] = jnp.concatenate(pieces, axis=1)

    first = (unit_of(xs_ref[0]) * vec_ref[0:1] + vec_ref[2:3]).astype(BF)
    first_ref[0] = first
    proj = dot(first, mix_ref[...].reshape(width, -1)[:, : 2 * heads * LANES]) + bias_s[...]
    cosine, sine_a, sine_b = cos_ref[0], sa_ref[0], sb_ref[0]
    for h in range(heads):
        cols = slice(h * LANES, (h + 1) * LANES)
        kv_ref[0, :, cols] = rotated(proj[:, cols], cosine, sine_a, sine_b).astype(BF)
        qcols = slice((heads + h) * LANES, (heads + h + 1) * LANES)
        q_ref[0, :, cols] = (rotated(proj[:, qcols], cosine, sine_a, sine_b) * SCALE).astype(BF)


def store_chunk(refs, value):
    for j, ref in enumerate(refs):

        @pl.when(pl.program_id(0) == j)
        def _(ref=ref):
            ref[...] = value


def load_chunk(refs, held):
    for j, ref in enumerate(refs):

        @pl.when(pl.program_id(0) == j)
        def _(ref=ref):
            held[...] = ref[...]


def feed_kernel(own, *refs):
    x_ref, up_ref, down_ref, tail_ref, vec_ref, second_ref, active_ref, slope_ref = refs[:8]
    part_refs, bias_s = refs[8:-1], refs[-1]

    @pl.when(pl.program_id(0) == 0)
    def _():
        bias_s[...] = gathered_row(tail_ref, 0, own)

    width = x_ref.shape[-1]
    second = (unit_of(x_ref[0]) * vec_ref[1:2] + vec_ref[3:4]).astype(BF)
    second_ref[0] = second
    hidden = dot(second, up_ref[...].reshape(width, -1)) + bias_s[...]
    half = 0.5 * (1.0 + lax.erf(hidden * (0.5**0.5)))
    active = (hidden * half).astype(BF)
    active_ref[0] = active
    bell = jnp.exp(hidden * hidden * -0.5) * 0.3989422804014327
    slope_ref[0] = (half + hidden * bell).astype(BF)
    store_chunk(part_refs, dot(active, down_ref[...].reshape(-1, width)).astype(BF))


def chunk_specs(n, tokens, gathered, k):
    shards, _, ff = gathered.shape
    token = lambda w: pl.BlockSpec((1, tokens, w), lambda c: (c, 0, 0))
    whole = lambda a: pl.BlockSpec(a.shape, lambda c: (0,) * a.ndim)
    weight = lambda j: pl.BlockSpec((shards, k, ff), lambda c: (0, j, 0))
    out = lambda w: jax.ShapeDtypeStruct((n, tokens, w), BF)
    return token, whole, weight, out


def mix_pass(tokens, chunks, place, n, gathered, k, own, vec, tables, heads, held=()):
    width = chunks[0].shape[1]
    count = len(chunks)
    wide = heads * LANES
    shards, _, ff = gathered.shape
    whole = lambda a: pl.BlockSpec(a.shape, lambda c: (0,) * a.ndim)
    token = lambda w: pl.BlockSpec((1, tokens, w), lambda c: (place + c, 0, 0))
    weight = pl.BlockSpec((shards, k, ff), lambda c: (0, 2, 0))
    last = gathered.shape[1] // 8 - 1
    tail = pl.BlockSpec((shards, 8, ff), lambda c: (0, last, 0))
    out = lambda m, w: jax.ShapeDtypeStruct((m, tokens, w), BF)
    first_held = count + 6
    return pl.pallas_call(
        partial(mix_kernel, count, heads, own),
        grid=(count,),
        in_specs=[pl.BlockSpec((tokens, width), lambda c: (0, 0))] * count
        + [weight, tail, whole(vec)]
        + [token(LANES)] * 3
        + [pl.BlockSpec(memory_space=pl.ANY)] * len(held),
        out_specs=[token(width), token(width), token(wide)]
        + [pl.BlockSpec((1, tokens, wide), lambda c: (c, 0, 0))],
        out_shape=[out(n, width), out(n, width), out(n, wide), out(count, wide)],
        input_output_aliases={first_held + i: i for i in range(len(held))},
        scratch_shapes=[pltpu.VMEM((1, 2 * wide), F32)],
        compiler_params=params(),
        cost_estimate=cost(12),
        name="mix_pass",
    )(*chunks, gathered, gathered, vec, *tables, *held)


def feed_pass(xs, gathered, k, own, vec):
    n, tokens, width = xs.shape
    ff = gathered.shape[2]
    token, whole, weight, out = chunk_specs(n, tokens, gathered, k)
    last = gathered.shape[1] // 8 - 1
    second, active, slope, *parts = pl.pallas_call(
        partial(feed_kernel, own),
        grid=(n,),
        in_specs=[token(width), weight(0), weight(1)]
        + [pl.BlockSpec((gathered.shape[0], 8, ff), lambda c: (0, last, 0)), whole(vec)],
        out_specs=[token(width), token(ff), token(ff)]
        + [pl.BlockSpec((tokens, width), lambda c: (0, 0))] * n,
        out_shape=[out(width), out(ff), out(ff)]
        + [jax.ShapeDtypeStruct((tokens, width), BF)] * n,
        scratch_shapes=[pltpu.VMEM((1, ff), F32)],
        compiler_params=params(),
        cost_estimate=cost(20),
        name="feed_pass",
    )(xs, gathered, gathered, gathered, vec)
    return second, active, slope, parts


def middle_kernel(n, me_ref, dense_ref, grads_ref, *refs):
    mixed_refs, part_refs = refs[:n], refs[n : 2 * n]
    do_refs, out_refs = refs[2 * n : 3 * n], refs[3 * n :]
    rows = mixed_refs[0].shape[1] // dense_ref.shape[0]
    dense = dense_ref[:, :rows].reshape(-1, dense_ref.shape[-1])
    for c in range(n):
        total = dot(mixed_refs[c][...], dense) + part_refs[c][...].astype(F32)
        out_refs[c][...] = total.astype(BF)
        grad = grads_ref[lax.rem(me_ref[0] + c, n)]
        do_refs[c][...] = dot_nt(grad, dense).astype(BF)


def middle(me1, mixed, gathered, k, d, parts, grads):
    n = len(parts)
    padded = d + -d % 8
    full = lambda a: pl.BlockSpec(a.shape, lambda i: (0,) * a.ndim)
    dense = pl.BlockSpec(
        (gathered.shape[0], padded, gathered.shape[2]), lambda i: (0, 3 * k // padded, 0)
    )
    outs = pl.pallas_call(
        partial(middle_kernel, n),
        grid=(1,),
        in_specs=[pl.BlockSpec(memory_space=pltpu.SMEM), dense, full(grads)]
        + [full(a) for a in mixed + parts],
        out_specs=[full(a) for a in mixed + parts],
        out_shape=[jax.ShapeDtypeStruct(mixed[0].shape, BF)] * n
        + [jax.ShapeDtypeStruct(parts[0].shape, BF)] * n,
        compiler_params=params(),
        cost_estimate=cost(4),
        name="middle",
    )(me1, gathered, grads, *mixed, *parts)
    return outs[:n], outs[n:]


def load_pairs(kv_refs, kv_s):
    place = 0
    for ref in kv_refs:
        for c in range(ref.shape[0]):
            kv_s[place] = ref[c, 0]
            place += 1


def each_block(plan_ref, row, c, blocks, take):
    start = c * (blocks + 1)
    count = plan_ref[row, start]

    def pair(t, _):
        take([plan_ref[row, start + 1 + 2 * t], plan_ref[row, start + 2 + 2 * t]])
        return 0

    lax.fori_loop(0, count // 2, pair, 0)

    @pl.when(count % 2 == 1)
    def _():
        take([plan_ref[row, start + count]])


def allowed_pairs(base_ref, begin_ref, kb, c, n, shape):
    key_slot = base_ref[n + kb] + lax.broadcasted_iota(jnp.int32, shape, 0)
    query_slot = base_ref[c] + lax.broadcasted_iota(jnp.int32, shape, 1)
    return (key_slot >= begin_ref[0, c]) & (key_slot <= query_slot)


def attend_kernel(heads, extras, groups, need_ref, base_ref, begin_ref, q_ref, *refs):
    kv_refs = refs[:groups]
    n, _, count, _ = q_ref.shape
    mixed_refs = refs[groups : groups + n]
    ot_ref, lse_ref, kv_s, vt_s, top_s, total_s, acc_s, mixed_s = refs[groups + n :]
    blocks = n * (1 + extras)
    row = pl.program_id(0)
    load_pairs(kv_refs, kv_s)

    def turn(kb, _):
        for h in range(heads):
            tile = kv_s[kb, :, h * LANES : (h + 1) * LANES].astype(F32)
            vt_s[kb, h] = tile.T[HEAD_DIM:].astype(BF)
        return 0

    lax.fori_loop(0, blocks, turn, 0)

    def per_query(c, _):
        top_s[...] = jnp.full(top_s.shape, MASKED, F32)
        total_s[...] = jnp.zeros(total_s.shape, F32)
        acc_s[...] = jnp.zeros(acc_s.shape, F32)

        def take(kbs):
            column = lambda h: slice(h * LANES, (h + 1) * LANES)
            held = [
                [dot_nt(kv_s[kb, :, column(h)], q_ref[c, 0, :, column(h)]) for h in range(heads)]
                for kb in kbs
            ]
            masks = [allowed_pairs(base_ref, begin_ref, kb, c, n, (count, count)) for kb in kbs]
            low, fades = [], []
            for h in range(heads):
                scores = [jnp.where(mask, own[h], MASKED) for mask, own in zip(masks, held)]
                old = top_s[h]
                new = old
                for score in scores:
                    new = jnp.maximum(new, jnp.max(score, axis=0, keepdims=True))
                fade = jnp.exp(old - new)
                total = total_s[h] * fade
                weights = []
                for score in scores:
                    weight = jnp.exp(score - new)
                    total = total + jnp.sum(weight, axis=0, keepdims=True)
                    weights.append(weight.astype(BF))
                top_s[h] = new
                total_s[h] = total
                low.append(weights)
                fades.append(fade)
            for h in range(heads):
                acc = acc_s[h] * fades[h]
                for kb, weight in zip(kbs, low[h]):
                    acc = acc + dot(vt_s[kb, h], weight)
                acc_s[h] = acc

        each_block(need_ref, row, c, blocks, take)
        outs = []
        for h in range(heads):
            total = total_s[h]
            outs.append(acc_s[h] / total)
            lse_ref[0, c, h : h + 1] = top_s[h] + jnp.log(total)
        whole = jnp.concatenate(outs, axis=0)
        ot_ref[0, c] = whole
        mixed_s[c] = whole.T.astype(BF)
        return 0

    lax.fori_loop(0, n, per_query, 0)
    for c in range(n):
        mixed_refs[c][0] = mixed_s[c]


def attention_specs(q, kvs):
    n, rows, count, wide = q.shape
    smem = pl.BlockSpec(memory_space=pltpu.SMEM)
    begin = pl.BlockSpec((1, n, 1, count), lambda r: (r, 0, 0, 0))
    tokens = lambda a: pl.BlockSpec((a.shape[0], 1, count, wide), lambda r: (0, r, 0, 0))
    flat = [a for group in kvs for a in group]
    return n, rows, count, wide, smem, begin, tokens, flat


def attend(need, base, begin, q, kvs, heads):
    extras = len(kvs) - 1
    n, rows, count, wide, smem, begin_spec, tokens, flat = attention_specs(q, kvs)
    blocks = n * (1 + extras)
    narrow = heads * HEAD_DIM
    outs = pl.pallas_call(
        partial(attend_kernel, heads, extras, len(flat)),
        grid=(rows,),
        in_specs=[smem, smem, begin_spec, tokens(q)] + [tokens(a) for a in flat],
        out_specs=[pl.BlockSpec((1, count, narrow), lambda r: (r, 0, 0))] * n
        + [
            pl.BlockSpec((1, n, narrow, count), lambda r: (r, 0, 0, 0)),
            pl.BlockSpec((1, n, heads, count), lambda r: (r, 0, 0, 0)),
        ],
        out_shape=[jax.ShapeDtypeStruct((rows, count, narrow), BF)] * n
        + [
            jax.ShapeDtypeStruct((rows, n, narrow, count), F32),
            jax.ShapeDtypeStruct((rows, n, heads, count), F32),
        ],
        scratch_shapes=[
            pltpu.VMEM((blocks, count, wide), BF),
            pltpu.VMEM((blocks, heads, HEAD_DIM, count), BF),
            pltpu.VMEM((heads, 1, count), F32),
            pltpu.VMEM((heads, 1, count), F32),
            pltpu.VMEM((heads, HEAD_DIM, count), F32),
            pltpu.VMEM((n, count, narrow), BF),
        ],
        compiler_params=params(),
        cost_estimate=cost(400),
        name="attend",
    )(need, base, begin, q, *flat)
    return [a.reshape(rows * count, narrow) for a in outs[:n]], outs[n], outs[n + 1]


def attend_back_kernel(heads, extras, groups, need_ref, base_ref, begin_ref, q_ref, *refs):
    n, _, count, _ = q_ref.shape
    do_refs, lse_ref, ot_ref = refs[:n], refs[n], refs[n + 1]
    kv_refs = refs[n + 2 : n + 2 + groups]
    dq_ref = refs[n + 2 + groups]
    dkv_refs = refs[n + 3 + groups : n + 4 + groups + extras]
    kv_s, kt_s, dkv_s, dqt_s, delta_s, do_s, narrow_s = refs[n + 4 + groups + extras :]
    blocks = n * (1 + extras)
    row = pl.program_id(0)
    load_pairs(kv_refs, kv_s)
    for c in range(n):
        narrow_s[c] = do_refs[c][0]

    def turn(kb, _):
        for h in range(heads):
            tile = kv_s[kb, :, h * LANES : (h + 1) * LANES].astype(F32)
            kt_s[kb, h] = tile.T[:HEAD_DIM].astype(BF)
        dkv_s[kb] = jnp.zeros(dkv_s.shape[1:], F32)
        return 0

    lax.fori_loop(0, blocks, turn, 0)

    def per_query(c, _):
        dqt_s[...] = jnp.zeros(dqt_s.shape, F32)
        for h in range(heads):
            cols = slice(h * LANES, (h + 1) * LANES)
            grad = narrow_s[c, :, h * HEAD_DIM : (h + 1) * HEAD_DIM].astype(F32)
            grad = jnp.concatenate([jnp.zeros((count, HEAD_DIM), F32), grad], axis=1)
            do_s[:, cols] = grad.astype(BF)
            dot_t = grad.T[HEAD_DIM:]
            out_t = ot_ref[0, c, h * HEAD_DIM : (h + 1) * HEAD_DIM]
            delta_s[h] = jnp.sum(dot_t * out_t, axis=0, keepdims=True)

        def take(kbs):
            column = lambda h: slice(h * LANES, (h + 1) * LANES)
            queries = [q_ref[c, 0, :, column(h)] for h in range(heads)]
            grads = [do_s[:, column(h)] for h in range(heads)]
            held = []
            for kb in kbs:
                pairs = [kv_s[kb, :, column(h)] for h in range(heads)]
                held.append(
                    [(dot_nt(pairs[h], queries[h]), dot_nt(pairs[h], grads[h])) for h in range(heads)]
                )
            low = []
            for kb, own in zip(kbs, held):
                allowed = allowed_pairs(base_ref, begin_ref, kb, c, n, (count, count))
                for h in range(heads):
                    scores = jnp.where(allowed, own[h][0], MASKED)
                    probs = jnp.exp(scores - lse_ref[0, c, h : h + 1])
                    steps = probs * (own[h][1] - delta_s[h])
                    low.append((steps.astype(BF), probs.astype(BF)))
            for i, kb in enumerate(kbs):
                for h in range(heads):
                    steps, probs = low[i * heads + h]
                    dqt_s[h] += dot(kt_s[kb, h], steps)
                    dkv_s[kb, :, column(h)] += dot(steps, queries[h]) + dot(probs, grads[h])

        each_block(need_ref, row, c, blocks, take)
        for h in range(heads):
            tile = jnp.concatenate([dqt_s[h], jnp.zeros((HEAD_DIM, count), F32)], axis=0)
            dq_ref[c, 0, :, h * LANES : (h + 1) * LANES] = tile.T * SCALE
        return 0

    lax.fori_loop(0, n, per_query, 0)
    for e, ref in enumerate(dkv_refs):
        for c in range(n):
            ref[c, 0] = dkv_s[e * n + c].astype(ref.dtype)


def attend_back(need, base, begin, q, do, lse, ot, kvs, heads):
    extras = len(kvs) - 1
    n, rows, count, wide, smem, begin_spec, tokens, flat = attention_specs(q, kvs)
    blocks = n * (1 + extras)
    narrow = heads * HEAD_DIM
    return pl.pallas_call(
        partial(attend_back_kernel, heads, extras, len(flat)),
        grid=(rows,),
        in_specs=[smem, smem, begin_spec, tokens(q)]
        + [pl.BlockSpec((1, count, narrow), lambda r: (r, 0, 0))] * n
        + [
            pl.BlockSpec((1, n, heads, count), lambda r: (r, 0, 0, 0)),
            pl.BlockSpec((1, n, narrow, count), lambda r: (r, 0, 0, 0)),
        ]
        + [tokens(a) for a in flat],
        out_specs=[tokens(q)] * (2 + extras),
        out_shape=[jax.ShapeDtypeStruct(q.shape, F32)] * 2
        + [jax.ShapeDtypeStruct(q.shape, BF)] * extras,
        scratch_shapes=[
            pltpu.VMEM((blocks, count, wide), BF),
            pltpu.VMEM((blocks, heads, HEAD_DIM, count), BF),
            pltpu.VMEM((blocks, count, wide), F32),
            pltpu.VMEM((heads, HEAD_DIM, count), F32),
            pltpu.VMEM((heads, 1, count), F32),
            pltpu.VMEM((count, wide), BF),
            pltpu.VMEM((n, count, narrow), BF),
        ],
        compiler_params=params(),
        cost_estimate=cost(40),
        name="attend_back",
    )(need, base, begin, q, *[a.reshape(rows, count, narrow) for a in do], lse, ot, *flat)


TN = (((0,), (0,)), ((), ()))


def dot_tn(a, b):
    return lax.dot_general(a, b, TN, preferred_element_type=F32)


def half_shard(place, inner, bit):
    return (place // inner * 2 + bit) * inner + place % inner


def store_shards(refs, core_ref, shards, inner, block):
    if len(refs) == 1:
        for s in range(shards):
            refs[0][s] = block(s)
        return
    mine = core_ref[0]
    for place in range(shards // 2):
        refs[0][place] = block(half_shard(place, inner, 1 - mine))
        refs[1][place] = block(half_shard(place, inner, mine))


def row_block(ref, s, size):
    start = s * size if isinstance(s, int) else pl.multiple_of(s * size, 8)
    return ref[pl.ds(start, size)]


def feed_back_kernel(n, gates, inner, split, core_ref, *refs):
    grad_refs = refs[:n]
    x_ref, slope_ref, second_ref, active_ref, up_ref, down_ref, vec_ref = refs[n : n + 7]
    refs = refs[n + 7 + gates :]
    scaled_ref, sums_ref, outs = refs[0], refs[1], refs[2:-4]
    up_s, down_s, grad_s, tail_s = refs[-4:]
    width = x_ref.shape[-1]
    last = pl.program_id(0) == pl.num_programs(0) - 1

    @pl.when(pl.program_id(0) == 0)
    def _():
        sums_ref[...] = jnp.zeros(sums_ref.shape, F32)
        up_s[...] = jnp.zeros(up_s.shape, F32)
        down_s[...] = jnp.zeros(down_s.shape, F32)

    load_chunk(grad_refs, grad_s)
    down = down_ref[...].reshape(-1, width)
    grad = grad_s[...]
    grad_active = dot_nt(grad, down)
    down_s[...] += dot_tn(active_ref[0], grad)
    grad_hidden = (grad_active * slope_ref[0].astype(F32)).astype(BF)
    grad_second = dot_nt(grad_hidden, up_ref[...].reshape(width, -1))
    unit = unit_of(x_ref[0])
    sums_ref[0:1] += jnp.sum(grad_second * unit, axis=0, keepdims=True)
    sums_ref[1:2] += jnp.sum(grad_second, axis=0, keepdims=True)
    sums_ref[2:3] += jnp.sum(grad_hidden.astype(F32), axis=0, keepdims=True)
    scaled_ref[0] = grad_second * vec_ref[1:2]
    up_s[...] += dot_tn(second_ref[0], grad_hidden)

    @pl.when(last)
    def _():
        shards, k = up_ref.shape[:2]
        f = down_s.shape[0] // shards
        own = up_s.shape[1] // shards
        pad = jnp.zeros((8, width - own), F32)
        for s in range(shards):
            tail = jnp.broadcast_to(sums_ref[2:3, s * own : (s + 1) * own], (8, own))
            tail_s[s] = jnp.concatenate([tail, pad], axis=1)
        up_block = lambda s: row_block(up_s, s, k).astype(BF)
        rest_block = lambda s: jnp.concatenate(
            [row_block(down_s, s, f), tail_s[s]], axis=0
        ).astype(BF)
        if split:
            store_shards(outs[:2], core_ref, shards, inner, up_block)
            store_shards(outs[2:], core_ref, shards, inner, rest_block)
        else:
            store_shards(
                outs, core_ref, shards, inner,
                lambda s: jnp.concatenate([up_block(s), rest_block(s)], axis=0),
            )


def feed_back(core1, gs, xs, slope, second, active, gathered, k, vec, inner, split, gates=()):
    n, tokens, width = xs.shape
    shards, _, ff = gathered.shape
    f = ff // shards
    token, whole, weight, _ = chunk_specs(n, tokens, gathered, k)
    fixed = pl.BlockSpec((8, width), lambda c: (0, 0))
    grads = [(shards, k + f + 8, width)]
    if split:
        grads = [(shards // 2, k, width)] * 2 + [(shards // 2, f + 8, width)] * 2
    return pl.pallas_call(
        partial(feed_back_kernel, n, len(gates), inner, split),
        grid=(n,),
        in_specs=[pl.BlockSpec(memory_space=pltpu.SMEM)]
        + [whole(gs[0])] * n
        + [token(width), token(ff), token(width), token(ff), weight(0), weight(1), fixed]
        + [pl.BlockSpec(memory_space=pl.ANY)] * len(gates),
        out_specs=[token(width), fixed] + [pl.BlockSpec(g, lambda c: (0, 0, 0)) for g in grads],
        scratch_shapes=[
            pltpu.VMEM((width, ff), F32),
            pltpu.VMEM((ff, width), F32),
            pltpu.VMEM((tokens, width), BF),
            pltpu.VMEM((shards, 8, width), F32),
        ],
        out_shape=[
            jax.ShapeDtypeStruct((n, tokens, width), F32),
            jax.ShapeDtypeStruct((8, width), F32),
        ]
        + [jax.ShapeDtypeStruct(g, BF) for g in grads],
        compiler_params=params(),
        cost_estimate=cost(12),
        name="feed_back",
    )(core1, *gs, xs, slope, second, active, gathered, gathered, vec, *gates)


def mix_back_kernel(n, inner, outs, core_ref, *refs):
    first_ref, gp_ref, bias_ref = refs[:3]
    mixed_refs, grad_refs = refs[3 : 3 + n], refs[3 + n : 3 + 2 * n]
    grads_refs = refs[-4 - outs : -4]
    mix_s, dense_s, mixed_s, grad_s = refs[-4:]
    last = pl.program_id(0) == pl.num_programs(0) - 1

    @pl.when(pl.program_id(0) == 0)
    def _():
        mix_s[...] = jnp.zeros(mix_s.shape, F32)
        dense_s[...] = jnp.zeros(dense_s.shape, F32)

    load_chunk(grad_refs, grad_s)
    load_chunk(mixed_refs, mixed_s)
    mix_s[...] += dot_tn(first_ref[0], gp_ref[0])
    dense_s[...] += dot_tn(mixed_s[...], grad_s[...])

    @pl.when(last)
    def _():
        shards = bias_ref.shape[0]
        k = mix_s.shape[0] // shards
        d = dense_s.shape[0] // shards

        def block(s):
            rows = [row_block(mix_s, s, k), row_block(dense_s, s, d), bias_ref[s]]
            return jnp.concatenate(rows, axis=0).astype(BF)

        store_shards(grads_refs, core_ref, shards, inner, block)


def mix_back(core1, first, gp, mixed, gs, bias, inner, split, micros, gates=()):
    n, tokens, width = first.shape
    shards = bias.shape[0]
    narrow = mixed[0].shape[-1]
    token = lambda w: pl.BlockSpec((1, tokens, w), lambda c: (c, 0, 0))
    whole = lambda a: pl.BlockSpec(a.shape, lambda c: (0,) * a.ndim)
    count = 2 if split else 1
    grads = (shards // count, width // shards + narrow // shards + 8, width)
    return pl.pallas_call(
        partial(mix_back_kernel, n, inner, count),
        grid=(n,),
        in_specs=[pl.BlockSpec(memory_space=pltpu.SMEM), token(width), token(gp.shape[-1]), whole(bias)]
        + [whole(mixed[0])] * n
        + [whole(gs[0])] * n
        + [pl.BlockSpec(memory_space=pl.ANY)] * len(gates),
        out_specs=[pl.BlockSpec(grads, lambda c: (0, 0, 0))] * count,
        scratch_shapes=[
            pltpu.VMEM((width, gp.shape[-1]), F32),
            pltpu.VMEM((narrow, width), F32),
            pltpu.VMEM((tokens, narrow), BF),
            pltpu.VMEM((tokens, width), BF),
        ],
        out_shape=[jax.ShapeDtypeStruct(grads, BF)] * count,
        compiler_params=params(),
        cost_estimate=cost(micros),
        name="mix_back",
    )(core1, first, gp, bias, *mixed, *gs, *gates)


def join_kernel(n, me_ref, dense_ref, residual_ref, vec_ref, *refs):
    mixed_refs, share_refs, out_ref, sent_ref = refs[:n], refs[n : 2 * n], refs[2 * n], refs[2 * n + 1]
    total = residual_ref[...] + vec_ref[4:5] + vec_ref[5:6]
    for c in range(n):
        rows = dense_ref[:, (n - c) % n]
        rows = rows.reshape(-1, rows.shape[-1])
        total = total + share_refs[c][...].astype(F32) + dot(mixed_refs[c][...], rows)
    out_ref[...] = total
    sent_ref[...] = total.astype(BF)


def join(me1, mixed, dense_all, shares, residual, vec):
    shape = residual.shape
    vmem = pl.BlockSpec(memory_space=pltpu.VMEM)
    return pl.pallas_call(
        partial(join_kernel, len(shares)),
        in_specs=[pl.BlockSpec(memory_space=pltpu.SMEM)] + [vmem] * (3 + 2 * len(shares)),
        out_specs=[vmem, vmem],
        out_shape=[jax.ShapeDtypeStruct(shape, F32), jax.ShapeDtypeStruct(shape, BF)],
        compiler_params=params(),
        cost_estimate=cost(3),
        name="join",
    )(me1, dense_all, residual, vec, *mixed, *shares)


def turn_kernel(n, gates, me_ref, *refs):
    summed = refs[0][...].astype(F32)
    for ref in refs[1:n]:
        summed = summed + ref[...].astype(F32)
    grad_ref, x_ref = refs[n : n + 2]
    refs = refs[n + 2 :]
    values = x_ref[...].astype(F32)
    centre = values - jnp.mean(values, axis=-1, keepdims=True)
    inverse = lax.rsqrt(jnp.mean(centre * centre, axis=-1, keepdims=True) + EPSILON)
    unit = centre * inverse
    mean_s = jnp.mean(summed, axis=-1, keepdims=True)
    mean_su = jnp.mean(summed * unit, axis=-1, keepdims=True)
    grad = grad_ref[...] + inverse * (summed - mean_s - unit * mean_su)
    if len(refs) == gates + 1:
        refs[-1][...] = grad
        return
    dense_ref, out_ref, sent_ref, sums_ref = refs[0], *refs[gates + 1 : gates + 4]
    piece_refs = refs[gates + 4 :]
    out_ref[...] = grad
    sent = grad.astype(BF)
    sent_ref[...] = sent
    for c, piece_ref in enumerate(piece_refs):
        rows = dense_ref[:, c]
        piece_ref[...] = dot_nt(sent, rows.reshape(-1, rows.shape[-1])).astype(BF)
    sums_ref[0:1] = jnp.sum(grad, axis=0, keepdims=True)
    sums_ref[1:2] = jnp.sum(grad_ref[...], axis=0, keepdims=True)


def turn(me1, parts, grad, x_own, dense_all=None, gates=()):
    shape = grad.shape
    outs = [jax.ShapeDtypeStruct(shape, F32)]
    vmem = pl.BlockSpec(memory_space=pltpu.VMEM)
    more = []
    if dense_all is not None:
        more = [dense_all]
        outs += [jax.ShapeDtypeStruct(shape, BF), jax.ShapeDtypeStruct((8, shape[1]), F32)]
        narrow = dense_all.shape[0] * dense_all.shape[2]
        outs += [jax.ShapeDtypeStruct((shape[0], narrow), BF)] * dense_all.shape[1]
    return pl.pallas_call(
        partial(turn_kernel, len(parts), len(gates)),
        in_specs=[pl.BlockSpec(memory_space=pltpu.SMEM)]
        + [vmem] * (len(parts) + 2 + len(more))
        + [pl.BlockSpec(memory_space=pl.ANY)] * len(gates),
        out_specs=[vmem] * len(outs),
        out_shape=outs,
        compiler_params=params(),
        cost_estimate=cost(3),
        name="turn",
    )(me1, *parts, grad, x_own, *more, *gates)


def exit_kernel(n, heads, extras, gates, inner, outs, halves, _, core_ref, dq_ref, dkv_ref, *refs):
    got_refs = refs[:extras]
    cos_ref, sa_ref, sb_ref, x_ref, mix_ref, vec_ref, scaled_ref = refs[extras : extras + 7]
    refs = refs[extras + 7 :]
    fold = halves > 0
    if fold:
        first_ref, mixed_refs, grad_refs = refs[0], refs[1 : 1 + n], refs[1 + n : 1 + 2 * n]
        refs = refs[1 + 2 * n :]
    refs = refs[gates:]
    gp_ref, sums_ref, part_refs = refs[0], refs[1], refs[2 : 2 + outs]
    grads_refs, scratch = refs[2 + outs : 2 + outs + halves], refs[2 + outs + halves :]
    width = x_ref.shape[-1]

    @pl.when(pl.program_id(0) == 0)
    def _():
        sums_ref[...] = jnp.zeros(sums_ref.shape, F32)
        if fold:
            scratch[0][...] = jnp.zeros(scratch[0].shape, F32)
            scratch[1][...] = jnp.zeros(scratch[1].shape, F32)

    if fold:
        mix_s, dense_s, mixed_s, grad_s, tail_s = scratch
        load_chunk(grad_refs, grad_s)
        load_chunk(mixed_refs, mixed_s)
        dense_s[...] += dot_tn(mixed_s[...], grad_s[...])
    cosine, sine_a, sine_b = cos_ref[0], sa_ref[0], sb_ref[0]
    for h in range(heads):
        cols = slice(h * LANES, (h + 1) * LANES)
        pair = dkv_ref[0, :, cols]
        for ref in got_refs:
            pair = pair + ref[0, :, cols].astype(F32)
        gp_ref[0, :, cols] = unrotated(pair, cosine, sine_a, sine_b).astype(BF)
        qcols = slice((heads + h) * LANES, (heads + h + 1) * LANES)
        gp_ref[0, :, qcols] = unrotated(dq_ref[0, :, cols], cosine, sine_a, sine_b).astype(BF)
    gp = gp_ref[0]
    grad_first = dot_nt(gp, mix_ref[...].reshape(width, -1))
    if fold:
        mix_s[...] += dot_tn(first_ref[0], gp)
    unit = unit_of(x_ref[0])
    sums_ref[0:1] += jnp.sum(grad_first * unit, axis=0, keepdims=True)
    sums_ref[1:2] += jnp.sum(grad_first, axis=0, keepdims=True)
    sums_ref[2:3] += jnp.sum(gp.astype(F32), axis=0, keepdims=True)
    part = (grad_first * vec_ref[0:1] + scaled_ref[0]).astype(BF)
    if outs == 1:
        part_refs[0][0] = part
    else:
        store_chunk(part_refs, part)
    if not fold:
        return

    @pl.when(pl.program_id(0) == pl.num_programs(0) - 1)
    def _():
        shards = mix_ref.shape[0]
        k = mix_s.shape[0] // shards
        d = dense_s.shape[0] // shards
        row = sums_ref[2:3]
        pieces = []
        for h in range(heads):
            query = (heads + h) * LANES
            pieces.append(row[:, query : query + HEAD_DIM])
            pieces.append(row[:, h * LANES : (h + 1) * LANES])
        raw = jnp.concatenate(pieces, axis=1)
        own = raw.shape[1] // shards
        pad = jnp.zeros((8, width - own), F32)
        for s in range(shards):
            tail = jnp.broadcast_to(raw[:, s * own : (s + 1) * own], (8, own))
            tail_s[s] = jnp.concatenate([tail, pad], axis=1)

        def block(s):
            rows = [row_block(mix_s, s, k), row_block(dense_s, s, d), tail_s[s]]
            return jnp.concatenate(rows, axis=0).astype(BF)

        store_shards(grads_refs, core_ref, shards, inner, block)


def exit_pass(
    me1, core1, dq, dkv, got, tables, xs, gathered, k, vec, scaled, heads, inner, halves=0,
    fold=(), gates=(),
):
    n, tokens, width = xs.shape
    shards, _, ff = gathered.shape
    wide = heads * LANES
    narrow = heads * HEAD_DIM
    token = lambda w: pl.BlockSpec((1, tokens, w), lambda c, s: (c, 0, 0))
    weight = lambda j: pl.BlockSpec((shards, k, ff), lambda c, s: (0, j, 0))
    whole = lambda a: pl.BlockSpec(a.shape, lambda c, s: (0,) * a.ndim)
    fixed = pl.BlockSpec((8, width), lambda c, s: (0, 0))
    flat = lambda a: a.reshape(n, tokens, wide)
    fold_specs, grad_specs, grad_shapes, scratch = [], [], [], []
    if halves:
        part_specs = [pl.BlockSpec((1, tokens, width), lambda c, s: ((s[0] + c) % n, 0, 0))]
        part_shapes = [jax.ShapeDtypeStruct((n, tokens, width), BF)]
        fold_specs = [token(width)] + [whole(a) for a in fold[1:]]
        grads = (shards // halves, width // shards + narrow // shards + 8, width)
        grad_specs = [pl.BlockSpec(grads, lambda c, s: (0, 0, 0))] * halves
        grad_shapes = [jax.ShapeDtypeStruct(grads, BF)] * halves
        scratch = [
            pltpu.VMEM((width, 2 * wide), F32),
            pltpu.VMEM((narrow, width), F32),
            pltpu.VMEM((tokens, narrow), BF),
            pltpu.VMEM((tokens, width), BF),
            pltpu.VMEM((shards, 8, width), F32),
        ]
    else:
        part_specs = [pl.BlockSpec((tokens, width), lambda c, s: (0, 0))] * n
        part_shapes = [jax.ShapeDtypeStruct((tokens, width), BF)] * n
    outs = len(part_specs)
    gp, sums, *rest = pl.pallas_call(
        partial(exit_kernel, n, heads, len(got), len(gates), inner, outs, halves),
        grid_spec=pltpu.PrefetchScalarGridSpec(
            num_scalar_prefetch=1,
            grid=(n,),
            in_specs=[pl.BlockSpec(memory_space=pltpu.SMEM)]
            + [token(wide)] * (2 + len(got))
            + [token(LANES)] * 3
            + [token(width), weight(2), fixed, token(width)]
            + fold_specs
            + [pl.BlockSpec(memory_space=pl.ANY)] * len(gates),
            out_specs=[token(2 * wide), fixed] + part_specs + grad_specs,
            scratch_shapes=scratch,
        ),
        out_shape=[
            jax.ShapeDtypeStruct((n, tokens, 2 * wide), BF),
            jax.ShapeDtypeStruct((8, width), F32),
        ]
        + part_shapes
        + grad_shapes,
        compiler_params=params(),
        cost_estimate=cost(100),
        name="exit_pass",
    )(
        me1, core1, flat(dq), flat(dkv), *[flat(a) for a in got], *tables, xs, gathered, vec,
        scaled, *fold, *gates,
    )
    return gp, rest[:outs], sums, tuple(rest[outs:])


def mix_columns(weight, heads):
    lead = weight.shape[:-1]
    split = weight.reshape(lead + (heads, 3, HEAD_DIM))
    pairs = split[..., 1:, :].reshape(lead + (heads * LANES,))
    query = jnp.concatenate([split[..., 0, :], jnp.zeros_like(split[..., 0, :])], axis=-1)
    return jnp.concatenate([pairs, query.reshape(lead + (heads * LANES,))], axis=-1)


def unmix_columns(grad, heads):
    lead = grad.shape[:-1]
    split = grad.reshape(lead + (2, heads, 2, HEAD_DIM))
    order = [split[..., 1, :, 0, :], split[..., 0, :, 0, :], split[..., 0, :, 1, :]]
    return jnp.stack(order, axis=-2).reshape(lead + (heads * 3 * HEAD_DIM,))


def pack_layer(mix_w, mix_b, dense_w, up_w, up_b, down_w, heads):
    width = up_w.shape[1]
    mix = mix_columns(mix_w, heads)
    wide = lambda v: jnp.pad(v, (0, width - v.shape[0]))[None]
    rows = [up_w, down_w, jnp.pad(mix, ((0, 0), (0, width - mix.shape[1])))]
    if dense_w is not None:
        rows += [dense_w, jnp.zeros((-dense_w.shape[0] % 8, width), up_w.dtype)]
    rows += [wide(up_b), wide(mix_b), jnp.zeros((6, width), up_w.dtype)]
    return jnp.concatenate(rows, axis=0)


def shards(
    block_input, seq_lengths, project_weight, project_bias, dense_weight, up_weight, up_bias,
    down_weight, norm_gains, shift_vectors, cotangent,
):
    rows, _, own_count, width = block_input.shape
    n = lax.axis_size("tensor")
    places = lax.axis_size("ctx")
    extras = places - 1
    place = lax.axis_index("ctx")
    me = lax.axis_index("tensor")
    me1 = me.reshape(1)
    core1 = (lax.axis_index("dp") & 1).reshape(1)
    split = power_of_two()
    block_len = own_count * n
    tokens = rows * own_count
    heads = project_weight.shape[2] // (3 * HEAD_DIM)
    wide = heads * LANES
    k_rows = up_weight.shape[1]
    d_rows = dense_weight.shape[1]
    f_own = up_bias.shape[1]
    m_own = project_bias.shape[1]
    shard_count = lax.axis_size("dp") * places

    ends = jnp.cumsum(seq_lengths, axis=1)
    order = (me + jnp.arange(n, dtype=jnp.int32)) % n
    query_base = place * block_len + order * own_count
    slots = query_base[:, None] + jnp.arange(own_count, dtype=jnp.int32)[None]
    passed = (ends[:, None, None, :] <= slots[None, :, :, None]).astype(jnp.int32)
    begin = jnp.sum(passed * seq_lengths[:, None, None, :], axis=3)
    position = (slots[None] - begin).transpose(1, 0, 2).reshape(-1)
    frequency = 1.0 / 10000.0 ** (jnp.arange(0, ROTARY, 2, dtype=F32) / ROTARY)
    angle = frequency[:, None] * position.astype(F32)[None, :]
    cosine, sine = lax.optimization_barrier((jnp.cos(angle), jnp.sin(angle)))
    cosine, sine = cosine.T, sine.T
    ones = jnp.ones((cosine.shape[0], LANES - ROTARY), F32)
    zero8 = jnp.zeros_like(sine)
    tables = (
        jnp.concatenate([cosine, cosine, ones], axis=1).reshape(n, tokens, LANES),
        jnp.concatenate([-sine, zero8, ones * 0.0], axis=1).reshape(n, tokens, LANES),
        jnp.concatenate([zero8, sine, ones * 0.0], axis=1).reshape(n, tokens, LANES),
    )
    key_base = jnp.concatenate(
        [
            jnp.where(place >= e, (place - e) * block_len + order * own_count, FAR)
            for e in range(places)
        ]
    )
    base = jnp.concatenate([query_base, key_base])
    need = (key_base[None, None, :] <= query_base[None, :, None] + own_count - 1) & (
        key_base[None, None, :] + own_count - 1 >= begin[:, :, :1]
    )
    need = need.astype(jnp.int32)
    rank = jnp.cumsum(need, axis=2) - need
    blocks = key_base.shape[0]
    spot = jnp.arange(blocks, dtype=jnp.int32)
    chosen = (rank[..., None] == spot) & (need[..., None] > 0)
    listed = jnp.sum(chosen * spot[:, None], axis=2)
    need = jnp.concatenate([jnp.sum(need, axis=2, keepdims=True), listed], axis=2)
    need = need.astype(jnp.int32).reshape(rows, -1)
    begin = begin.reshape(rows, n, 1, own_count)

    gains = norm_gains.astype(F32)
    shifts = shift_vectors.astype(F32)
    packed = [
        pack_layer(
            project_weight[l], project_bias[l], dense_weight[l] if l else None, up_weight[l],
            up_bias[l], down_weight[l], heads,
        )
        for l in range(LAYERS)
    ]
    flat = lambda a: a.reshape(n * tokens, -1)
    by_row = lambda a: a.reshape(n, rows, own_count, -1)
    stack = lambda chunks: jnp.stack(chunks)
    shift_to = lambda v, c: lax.ppermute(v, "tensor", [(s, (s + c) % n) for s in range(n)])
    sent = block_input[:, 0].reshape(tokens, width)
    sent0 = sent
    residual = sent.astype(F32)
    cot = cotangent[:, 0].reshape(tokens, width)

    spare = jnp.zeros((-d_rows % 8, width), BF)
    chunks0 = z_gather(jnp.concatenate([sent, dense_weight[0], spare], axis=0))
    gather_all = lambda v: lax.all_gather(v, ("dp", "ctx"), axis=0, tiled=False)
    gathered = [gather_all(packed[0])]
    gather_z = lambda v: lax.all_gather(v, "tensor", axis=0, tiled=False)
    vecs = [
        jnp.concatenate([gains[l].T, shifts[l].T, jnp.zeros((2, width), F32)], axis=0)
        for l in range(LAYERS)
    ]

    def mix_groups(chunks, l):
        cut = (n + 1) // 2
        tables_of = tables
        xs, first, q, kv_a = mix_pass(
            tokens, chunks[:cut], 0, n, gathered[l], k_rows, m_own, vecs[l], tables_of, heads
        )
        groups = [kv_a]
        if cut < n:
            chunks = chunks[:cut] + list(after(tuple(chunks[cut:]), kv_a))
            xs, first, q, kv_b = mix_pass(
                tokens, chunks[cut:], cut, n, gathered[l], k_rows, m_own, vecs[l], tables_of, heads,
                (xs, first, q),
            )
            groups.append(kv_b)
        groups = [a.reshape(a.shape[0], rows, own_count, wide) for a in groups]
        kvs = [groups] + [
            [lax.ppermute(a, "ctx", [(s, s + e) for s in range(places - e)]) for a in groups]
            for e in range(1, places)
        ]
        return xs, first, by_row(q), kvs, chunks

    chunks0[0] = after(chunks0[0], packed[1], need, base, begin)
    xs0, first0, q0, kvs0, chunks0 = mix_groups(chunks0, 0)
    dense_all = jnp.stack([chunk[tokens : tokens + d_rows] for chunk in chunks0])
    dense_all = gather_all(dense_all)
    second0, active0, slope0, parts = feed_pass(xs0, gathered[0], k_rows, f_own, vecs[0])
    later = gather_all(after(packed[1], parts[0]))
    shares = z_scatter(parts)
    mixed0, ot0, lse0 = attend(need, base, begin, after(q0, parts[0]), kvs0, heads)
    sent_mixed = [after(mixed0[0], *shares)] + mixed0[1:]
    sent_mixed = [sent_mixed[0]] + [shift_to(after(mixed0[c], *shares), c) for c in range(1, n)]
    residual, sent = join(me1, sent_mixed, dense_all, shares, residual, vecs[0])

    chunks1 = z_gather(sent)
    gathered.append(after(later, sent))
    xs1, first1, q1, kvs1, _ = mix_groups(chunks1, 1)
    second1, active1, slope1, parts = feed_pass(xs1, gathered[1], k_rows, f_own, vecs[1])
    cots = gather_z(after(cot.astype(BF), kvs1[0][0]))
    mixed1, ot1, lse1 = attend(need, base, begin, after(q1, parts[0]), kvs1, heads)
    do1, branches = middle(me1, mixed1, gathered[1], k_rows, d_rows, parts, cots)
    shares = z_scatter(branches)
    dq1, dkv1, *send_back = attend_back(need, base, begin, q1, do1, lse1, ot1, kvs1, heads)

    def return_pairs(sends):
        return [
            lax.ppermute(sends[e - 1], "ctx", [(s, s - e) for s in range(e, places)])
            for e in range(1, places)
        ]

    scatter_all = lambda v: lax.psum_scatter(v, ("dp", "ctx"), scatter_dimension=0, tiled=True)[0]

    own_cols = width // (n * shard_count)

    def extra_rows(sums_a):
        bias = unmix_columns(sums_a[2, : 2 * wide], heads).reshape(shard_count, 1, -1)
        return jnp.pad(bias, ((0, 0), (0, 7), (0, width - m_own)))

    def feed_out(total):
        total = total.astype(F32)
        return total[:k_rows], total[-8, :f_own], total[k_rows:-8]

    def mix_out(total):
        total = total.astype(F32)
        return unmix_columns(total[:k_rows], heads), total[-8, :m_own], total[k_rows:-8]

    got1 = return_pairs(send_back)
    cots = after(cots, dq1)
    cots = [lax.dynamic_index_in_dim(cots, (me + c) % n, 0, keepdims=False) for c in range(n)]
    scaled1, sums_b1, feed_g1 = feed_back(
        core1, cots, xs1, slope1, second1, active1, gathered[1], k_rows, vecs[1], places, False
    )
    feed1 = scatter_all(feed_g1)
    shares[0] = after(shares[0], dq1)
    block_output = shares[0].astype(F32)
    for share in shares[1:]:
        block_output = block_output + share.astype(F32)
    block_output = block_output + residual + shifts[1, :, 2] + shifts[1, :, 3]
    scaled1 = after(scaled1, block_output)
    gp1, parts1, sums_a1, _ = exit_pass(
        me1, core1, dq1, dkv1, got1, tables, xs1, gathered[1], k_rows, vecs[1], scaled1, heads, places
    )
    parts1 = z_scatter(parts1)
    rows1 = extra_rows(sums_a1)
    (mix_g1,) = mix_back(core1, first1, gp1, mixed1, cots, rows1, places, False, 30)

    grad, grad_own, token_sum0, *pieces = turn(
        me1, parts1, cot, chunks1[0], dense_all, (mix_g1, feed1)
    )
    do0 = [pieces[0]] + [None] * (n - 1)
    for c in range(1, n):
        do0[n - c] = shift_to(pieces[c], c)
    mix1 = scatter_all(after(mix_g1, *do0))
    gs = z_gather(after(grad_own, do0[n - 1]))
    dq0, dkv0, *send_back = attend_back(need, base, begin, q0, do0, lse0, ot0, kvs0, heads)
    got0 = return_pairs(send_back)
    scaled0, sums_b0, *feed_g0 = feed_back(
        core1, gs, xs0, slope0, second0, active0, gathered[0], k_rows, vecs[0], places, split,
        (dq0,),
    )
    gp0, (parts0,), sums_a0, mix_g0 = exit_pass(
        me1, core1, dq0, dkv0, got0, tables, xs0, gathered[0], k_rows, vecs[0], scaled0, heads,
        places, 2 if split else 1, [first0] + mixed0 + gs, (mix1,),
    )
    parts0 = [lax.psum_scatter(parts0, "tensor", scatter_dimension=0, tiled=True)[0]]
    small = [
        jnp.stack([sums_a0[0], sums_b0[0], sums_a0[1], sums_b0[1], token_sum0[0]]),
        jnp.stack([sums_a1[0], sums_b1[0], sums_a1[1], sums_b1[1], token_sum0[1]]),
    ]
    sums = jnp.concatenate(small, axis=0).reshape(LAYERS * 5, n, shard_count, own_cols)
    sums = sums.transpose(1, 2, 0, 3)
    if split:
        feed_g0 = after(tuple(feed_g0), gp0)
        up_sum, rest_sum = Scatter(tuple(feed_g0[:2]), False), Scatter(tuple(feed_g0[2:]), True)
        mix_sum = Scatter(mix_g0, False)
        picks = [lax.dynamic_index_in_dim(sums, (me + c) % n, 0, keepdims=False) for c in range(n)]
        total = picks[0]
        for c in range(1, n):
            total = total + shift_to(picks[c], c)
        advance([mix_sum, up_sum, rest_sum])
        small_sum = Scatter(total, False, wire=F32)
        streams = [small_sum, mix_sum, up_sum, rest_sum]
        while mix_sum.order:
            advance(streams)
        (input_grad,) = turn(me1, parts0, grad, sent0)
        advance(streams, input_grad)
        while small_sum.order:
            advance(streams)
        mix0 = mix_out(mix_sum.value)
        feed0 = jnp.concatenate([up_sum.value, rest_sum.value], axis=0)
        total = small_sum.value
    else:
        (input_grad,) = turn(me1, parts0, grad, sent0)
        mix0 = mix_out(scatter_all(mix_g0[0]))
        feed0 = scatter_all(feed_g0[0])
        total = lax.psum_scatter(sums, "tensor", scatter_dimension=0, tiled=False)
        total = scatter_all(total)
    total = total.reshape(LAYERS, 5, own_cols)
    mix1 = mix_out(mix1)
    weight_out = []
    for feed_s, mix_s in ((feed_out(feed0), mix0), (feed_out(feed1), mix1)):
        weight_out.append((mix_s[0], mix_s[1], mix_s[2], feed_s[0], feed_s[1], feed_s[2]))

    gains_out = total[:, :2].transpose(0, 2, 1)
    shifts_out = jnp.stack([total[:, 2], total[:, 3], total[:, 4], total[:, 4]], axis=-1)
    outs = [jnp.stack([weight_out[l][j] for l in range(LAYERS)]) for j in range(6)]
    shape = (rows, 1, own_count, width)
    return (block_output.reshape(shape), input_grad.reshape(shape), *outs, gains_out, shifts_out)


def solution(mesh):
    in_specs = (
        P("dp", "ctx", "tensor", None),
        P("dp", None),
        P(None, ("dp", "ctx"), "tensor"),
        P(None, ("tensor", "dp", "ctx")),
        P(None, ("tensor", "dp", "ctx"), None),
        P(None, ("dp", "ctx"), "tensor"),
        P(None, ("tensor", "dp", "ctx")),
        P(None, ("tensor", "dp", "ctx"), None),
        P(),
        P(),
        P("dp", "ctx", "tensor", None),
    )
    out_specs = (
        P("dp", "ctx", "tensor", None),
        P("dp", "ctx", "tensor", None),
        P(None, ("dp", "ctx"), "tensor"),
        P(None, ("tensor", "dp", "ctx")),
        P(None, ("tensor", "dp", "ctx"), None),
        P(None, ("dp", "ctx"), "tensor"),
        P(None, ("tensor", "dp", "ctx")),
        P(None, ("tensor", "dp", "ctx"), None),
        P(None, ("tensor", "dp", "ctx"), None),
        P(None, ("tensor", "dp", "ctx"), None),
    )
    return jax.shard_map(shards, mesh=mesh, in_specs=in_specs, out_specs=out_specs, check_vma=False)
```
